32 devices in a mesh: dp: 8 (over y, x, core), tensor: 4 (over z).
Axes of the slice: x: 2, y: 2, z: 4, core: 2. Of those that a mesh axis runs over, the one named last changes fastest.
Arguments:
- tokens: bfloat16 [16384, 1536], P('dp'), may hold values from -6 to 6
- cotangent: bfloat16 [16384, 1536], P('dp'), may hold values from -6 to 6
- destination: int32 [16384], P('dp'), may hold values from 0 to 16383, as said below
- lengths: int32 [8, 4], P('dp'), may hold values from 1 to 1024, 2048 in all within a row
- norm_gain: float32 [1536], replicated, may hold values from 0.1 to 1.9
- inner_weight: float32 [1536, 2, 3072], P('dp', None, 'tensor'), may hold values from -0.15625 to 0.15625
- shared_weight: float32 [1536, 256], P('dp'), may hold values from -0.15625 to 0.15625
- step_weight: float32 [1536, 48], P('dp', 'tensor'), may hold values from -0.15625 to 0.15625
- filter_weight: float32 [4, 3072], P(None, 'tensor'), may hold values from -3 to 3
- filter_bias: float32 [3072], P('tensor'), may hold values from -3 to 3
- shared_filter: float32 [4, 256], replicated, may hold values from -3 to 3
- shared_filter_bias: float32 [256], replicated, may hold values from -3 to 3
- step_bias: float32 [48], P('tensor'), may hold values from -6 to -2
- decay_log: float32 [48], P('tensor'), may hold values from 0 to 2.77
- skip_gain: float32 [48], P('tensor'), may hold values from 0.5 to 1.5
- gate_gain: float32 [3072], P('tensor'), may hold values from 0.1 to 1.9
- out_weight: float32 [1536, 3072], P('dp', 'tensor'), may hold values from -0.109375 to 0.109375
Outputs:
- layer_out: bfloat16 [16384, 1536], P('dp')
- input_grad: bfloat16 [16384, 1536], P('dp')
- norm_gain_grad: float32 [1536], replicated
- inner_weight_grad: float32 [1536, 2, 3072], P('dp', None, 'tensor')
- shared_weight_grad: float32 [1536, 256], P('dp')
- step_weight_grad: float32 [1536, 48], P('dp', 'tensor')
- filter_weight_grad: float32 [4, 3072], P(None, 'tensor')
- filter_bias_grad: float32 [3072], P('tensor')
- shared_filter_grad: float32 [4, 256], replicated
- shared_filter_bias_grad: float32 [256], replicated
- step_bias_grad: float32 [48], P('tensor')
- decay_log_grad: float32 [48], P('tensor')
- skip_gain_grad: float32 [48], P('tensor')
- gate_gain_grad: float32 [3072], P('tensor')
- out_weight_grad: float32 [1536, 3072], P('dp', 'tensor')
The draws below stay inside these ranges and needn't reach their ends.
Inputs may be any that keep to these rules, and one draw needn't show every extreme that they name: destination is a permutation. The tokens at given positions s * 2048 to (s + 1) * 2048 - 1 that go to work block w take exactly the work positions w * 2048 + s * 256 to w * 2048 + (s + 1) * 256 - 1. `lengths`: each row sums to 2048, and its longest sequence has exactly 1024 tokens.
All inputs are finite; a program needn't handle non-finite values.
Results may differ from the reference program's by a relative error of at most 0.012.
Values may be sent and summed in bfloat16 or wider, within the bound.
No kernel may reach another device: no remote copies, remote signals or barrier semaphores. Data moves between devices by JAX's collectives and lax.ppermute only.
A program may use at most 256 MiB of HBM per device.

```python
import math
import jax
import jax.numpy as jnp
import numpy as np
from jax import lax

D = 1536
INNER = 3072
HEADS = 48
STATE = 128
CONV = 4
SPAN = 256
TOK_DEV = 2048
MAX_LEN = 1024
SEQ_DEV = 4
BLOCKS = 8
TOKENS = 16384


def draw_destination(key, part):
    row_count = TOK_DEV
    sources = TOKENS // TOK_DEV
    group_rows = TOK_DEV // sources

    def one_source(source):
        order = jax.random.permutation(jax.random.fold_in(key, source), row_count)
        return order // group_rows * row_count + source * group_rows + order % group_rows
    return jax.vmap(one_source)(jnp.arange(sources, dtype=jnp.int32)).reshape(-1).astype(jnp.int32)


def shard_levels(stream_key, dims, pieces, low, largest):
    gain = 1.0
    for axis_at, parts in pieces:
        heights = jax.random.uniform(jax.random.fold_in(jax.random.fold_in(stream_key, 6), axis_at), (parts,), jnp.float32, low / len(pieces), largest / len(pieces))
        gain = gain * jnp.repeat(jnp.exp(heights), dims[axis_at] // parts).reshape((-1,) + (1,) * (len(dims) - 1 - axis_at))
    return gain


def length_profile(count, total, limit, lean):
    loads = [(1 << 20) // math.isqrt(rank ** lean) + 1 for rank in range(2, count + 1)]
    spare, counts = total - limit - (count - 1), [1] * (count - 1)
    while spare > 0:
        candidates = [i for i in range(count - 1) if counts[i] < limit]
        mass, remaining = sum([loads[i] for i in candidates]), spare
        for i in candidates:
            extra = min(limit - counts[i], max(1, remaining * loads[i] // mass), spare)
            counts[i] = counts[i] + extra
            spare = spare - extra
    return np.array([limit] + counts)


def uneven(own_key, count, total, reach, lean):
    if count == 2:
        one = jax.random.randint(own_key, (), max(1, total - reach), min(reach, total - 1) + 1)
        return jnp.stack([one, total - one])
    sizes = jnp.asarray(length_profile(count, total, reach, lean), jnp.int32)
    couples = (count - 1) // 2
    giver, receiver = sizes[1:1 + 2 * couples:2], sizes[2:2 + 2 * couples:2]
    margin = jnp.minimum(giver - 1, reach - receiver)
    moved = jax.random.randint(jax.random.fold_in(own_key, 1), (couples,), 0, 1 << 20) % (margin + 1)
    sizes = sizes.at[1:1 + 2 * couples:2].set(giver - moved).at[2:2 + 2 * couples:2].set(receiver + moved)
    return sizes[jax.random.permutation(jax.random.fold_in(own_key, 2), count)]


def bell_draw(key, shape, scale, bound, split=(), kind=jnp.bfloat16):
    level = shard_levels(key, shape, split, -0.22, 0.18) if split else 1.0
    values = jax.random.normal(key, shape, jnp.float32) * scale * level
    return jnp.minimum(jnp.maximum(values, -bound), bound).astype(kind)


def setup_inputs(seed: int = 0) -> dict:
    splits = jax.random.split(jax.random.key(seed), 18)
    tokens = bell_draw(splits[0], (TOKENS, D), 1.0, 6.0, ((0, 8),))
    cotangent = bell_draw(splits[1], (TOKENS, D), 1.0, 6.0, ((0, 8),))
    destination = draw_destination(jax.random.fold_in(splits[17], 71), 0)
    lengths = jax.vmap(lambda own: uneven(own, SEQ_DEV, TOK_DEV, MAX_LEN, 2))(jax.random.split(splits[3], BLOCKS)).reshape((BLOCKS, SEQ_DEV)).astype(jnp.int32)
    norm_gain = jnp.clip(1.0 + 0.18 * jax.random.normal(splits[4], (D,), jnp.float32), 0.1, 1.9)
    inner_weight = bell_draw(splits[5], (D, 2, INNER), D ** -0.5, 0.15625, ((0, 8), (2, 4)), jnp.float32)
    shared_weight = bell_draw(splits[6], (D, 2 * STATE), D ** -0.5, 0.15625, ((0, 8),), jnp.float32)
    step_weight = bell_draw(splits[7], (D, HEADS), D ** -0.5, 0.15625, ((0, 8), (1, 4)), jnp.float32)
    filter_weight = bell_draw(splits[8], (CONV, INNER), CONV ** -0.5, 3.0, ((1, 4),), jnp.float32)
    filter_bias = bell_draw(splits[9], (INNER,), 0.5, 3.0, ((0, 4),), jnp.float32)
    shared_filter = bell_draw(splits[10], (CONV, 2 * STATE), CONV ** -0.5, 3.0, (), jnp.float32)
    shared_filter_bias = bell_draw(splits[11], (2 * STATE,), 0.5, 3.0, (), jnp.float32)
    step_bias = jnp.clip(-6.0 + 4.0 * jax.random.uniform(splits[12], (HEADS,), jnp.float32) ** shard_levels(splits[12], (HEADS,), ((0, 4),), -0.2, 0.2), -6.0, -2.0)
    decay_log = jnp.clip(2.77 * jax.random.uniform(splits[13], (HEADS,), jnp.float32) ** shard_levels(splits[13], (HEADS,), ((0, 4),), -0.2, 0.2), 0.0, 2.77)
    skip_gain = jnp.clip(0.5 + 1.0 * jax.random.uniform(splits[14], (HEADS,), jnp.float32) ** shard_levels(splits[14], (HEADS,), ((0, 4),), -0.2, 0.2), 0.5, 1.5)
    gate_gain = jnp.clip(1.0 + 0.18 * jax.random.normal(splits[15], (INNER,), jnp.float32), 0.1, 1.9)
    out_weight = bell_draw(splits[16], (D, INNER), INNER ** -0.5, 0.109375, ((0, 8), (1, 4)), jnp.float32)
    return {"tokens": tokens, "cotangent": cotangent, "destination": destination, "lengths": lengths, "norm_gain": norm_gain, "inner_weight": inner_weight, "shared_weight": shared_weight, "step_weight": step_weight, "filter_weight": filter_weight, "filter_bias": filter_bias, "shared_filter": shared_filter, "shared_filter_bias": shared_filter_bias, "step_bias": step_bias, "decay_log": decay_log, "skip_gain": skip_gain, "gate_gain": gate_gain, "out_weight": out_weight}


EPSILON = 1e-05
PRECISE = lax.Precision.HIGHEST

@jax.custom_vjp
def low(v):
    return lax.optimization_barrier(v.astype(jnp.bfloat16)).astype(jnp.float32)

@jax.custom_vjp
def low_back(v):
    return v

def low_keep(v):
    return (low(v), None)

def low_pass(kept, grad):
    return (grad,)

def back_keep(v):
    return (v, None)

def back_low(kept, grad):
    return (low(grad),)
low.defvjp(low_keep, low_pass)
low_back.defvjp(back_keep, back_low)

def segments_of(lengths, row_count):
    seq_ends = jnp.cumsum(lengths.astype(jnp.int32)).astype(jnp.int32)
    seq_starts = (seq_ends - lengths.astype(jnp.int32)).astype(jnp.int32)
    places = jnp.arange(row_count, dtype=jnp.int32)
    segment = lax.optimization_barrier(jnp.sum((places[:, None] >= seq_ends[None, :]).astype(jnp.int32), axis=1)).astype(jnp.int32)
    belongs = segment[:, None] == jnp.arange(lengths.shape[0], dtype=jnp.int32)[None, :]
    position = (places - lax.optimization_barrier(jnp.sum(jnp.where(belongs, seq_starts[None, :], 0), axis=1))).astype(jnp.int32)
    return (segment, position)

def causal_filter(signal, kernel, offset_bias, position):
    result = offset_bias + kernel[0] * signal
    for offset in range(1, kernel.shape[0]):
        shifted = jnp.pad(signal, ((offset, 0), (0, 0)))[:signal.shape[0]]
        allowed = (position >= offset).astype(signal.dtype)
        result = result + kernel[offset] * shifted * allowed[:, None]
    return result

def mixer(inputs, shared, step_raw, filter_weight, filter_bias, shared_filter, shared_filter_bias, step_bias, decay_log, skip_gain, segment, position):
    row_count = inputs.shape[0]
    heads_here = step_bias.shape[0]
    state_size = shared.shape[1] // 2
    values = jax.nn.silu(causal_filter(inputs, filter_weight, filter_bias, position)).reshape(row_count, heads_here, -1)
    factors = jax.nn.silu(causal_filter(shared, shared_filter, shared_filter_bias, position))
    writes = factors[:, :state_size]
    read_vectors = factors[:, state_size:]
    step_size = jax.nn.softplus(step_raw + step_bias)
    log_decay = -step_size * jnp.exp(decay_log)
    blocks = row_count // SPAN
    causal = jnp.arange(SPAN)[:, None] >= jnp.arange(SPAN)[None, :]

    def blocked(whole_array):
        return whole_array.reshape((blocks, SPAN) + whole_array.shape[1:])

    def span_step(state_carry, block_item):
        memory, last_segment = state_carry
        value_blk, write_blk, read_blk, size_blk, decay_blk, segment_blk = block_item
        cumulative = jnp.cumsum(decay_blk, axis=0).T
        inside = causal & (segment_blk[:, None] == segment_blk[None, :])
        spread = cumulative[:, :, None] - cumulative[:, None, :]
        decays = jnp.exp(jnp.where(inside[None], spread, -jnp.inf))
        scores = jnp.dot(read_blk, write_blk.T, precision=PRECISE)
        mixing = scores[None] * decays * size_blk.T[:, None, :]
        local_out = jnp.einsum('hts,shp->thp', mixing, value_blk, precision=PRECISE)
        carried = (segment_blk == last_segment).astype(value_blk.dtype)
        entering = jnp.exp(cumulative).T * carried[:, None]
        remote_out = jnp.einsum('tn,hnp->thp', read_blk, memory, precision=PRECISE) * entering[:, :, None]
        block_out = local_out + remote_out + skip_gain[None, :, None] * value_blk
        end_segment = segment_blk[-1].astype(jnp.int32)
        closing = (segment_blk == end_segment).astype(value_blk.dtype)
        weights = jnp.exp(cumulative[:, -1:] - cumulative) * size_blk.T * closing[None, :]
        added_state = jnp.einsum('sn,hs,shp->hnp', write_blk, weights, value_blk, precision=PRECISE)
        keeping = jnp.exp(cumulative[:, -1]) * (last_segment == end_segment).astype(value_blk.dtype)
        memory = memory * keeping[:, None, None] + added_state
        return ((memory, end_segment), block_out)
    initial = (jnp.zeros((heads_here, state_size, values.shape[2]), values.dtype), jnp.int32(-1))
    unused, outputs = lax.scan(jax.checkpoint(span_step), initial, (blocked(values), blocked(writes), blocked(read_vectors), blocked(step_size), blocked(log_decay), blocked(segment)))
    return outputs.reshape(row_count, -1)

def layer(hidden_in, params, lengths):
    norm_gain, inner_weight, shared_weight, step_weight, filter_weight, filter_bias, shared_filter, shared_filter_bias, step_bias, decay_log, skip_gain, gate_gain, out_weight = params
    row_count = hidden_in.shape[0]
    segment, position = segments_of(lengths, row_count)
    scale = lax.rsqrt(lax.optimization_barrier(jnp.mean(hidden_in * hidden_in, axis=1, keepdims=True)) + EPSILON)
    normed = low(hidden_in * scale * norm_gain)
    both = low_back(jnp.dot(normed, low(inner_weight).reshape(inner_weight.shape[0], -1), precision=PRECISE))
    half_width = both.shape[1] // 2
    gate_in = both[:, :half_width]
    inputs = both[:, half_width:]
    shared = low_back(jnp.dot(normed, low(shared_weight), precision=PRECISE))
    step_raw = low_back(jnp.dot(normed, low(step_weight), precision=PRECISE))
    mixed_in = mixer(inputs, shared, step_raw, filter_weight, filter_bias, shared_filter, shared_filter_bias, step_bias, decay_log, skip_gain, segment, position)
    gated = mixed_in * jax.nn.silu(gate_in)
    gate_scale = lax.rsqrt(lax.optimization_barrier(jnp.mean(gated * gated, axis=1, keepdims=True)) + EPSILON)
    gate_normed = low(gated * gate_scale * gate_gain)
    branch = jnp.einsum('ti,di->td', gate_normed, low(out_weight), precision=PRECISE)
    return hidden_in + branch

def reference(tokens, cotangent, destination, lengths, norm_gain, inner_weight, shared_weight, step_weight, filter_weight, filter_bias, shared_filter, shared_filter_bias, step_bias, decay_log, skip_gain, gate_gain, out_weight):
    token_count = tokens.shape[0]
    model_width = tokens.shape[1]
    block_rows = token_count // lengths.shape[0]
    source_of = jnp.zeros((token_count,), jnp.int32).at[destination.astype(jnp.int32)].set(jnp.arange(token_count, dtype=jnp.int32))
    work_in = tokens[source_of].astype(jnp.float32).reshape(-1, block_rows, model_width)
    work_cot = cotangent[source_of].astype(jnp.float32).reshape(-1, block_rows, model_width)
    params = tuple((weight_array.astype(jnp.float32) for weight_array in (norm_gain, inner_weight, shared_weight, step_weight, filter_weight, filter_bias, shared_filter, shared_filter_bias, step_bias, decay_log, skip_gain, gate_gain, out_weight)))

    def per_block(totals, block_item):
        block_in, block_cot, block_lengths = block_item

        def forward_fn(hidden_in, weights):
            return layer(hidden_in, weights, block_lengths)
        block_out, pullback = jax.vjp(forward_fn, block_in, params)
        block_grad, weight_grads = pullback(block_cot)
        totals = jax.tree.map(lambda left, right: left + right, totals, weight_grads)
        return (totals, (block_out, block_grad))
    initial = jax.tree.map(jnp.zeros_like, params)
    grads, (block_outs, block_grads) = lax.scan(per_block, initial, (work_in, work_cot, lengths.astype(jnp.int32)))
    layer_out = block_outs.reshape(token_count, model_width).astype(jnp.bfloat16)[destination]
    input_grad = block_grads.reshape(token_count, model_width).astype(jnp.bfloat16)[destination]
    return (layer_out, input_grad, grads[0], grads[1], grads[2], grads[3], grads[4], grads[5], grads[6], grads[7], grads[8], grads[9], grads[10], grads[11], grads[12])
```

```python
import jax
import jax.numpy as jnp
from jax import lax
from jax.experimental import pallas as pl
from jax.experimental.pallas import tpu as pltpu
from jax.sharding import PartitionSpec as P

SPAN = 128
HALO = 8
LANES = 128
F32 = jnp.float32
BF16 = jnp.bfloat16
EPSILON = 1e-05


def mm(a, b):
    return jnp.dot(a, b, preferred_element_type=F32)


def mm_t(a, b):
    return lax.dot_general(a, b, (((1,), (1,)), ((), ())), preferred_element_type=F32)


def halves(v):
    high = v.astype(BF16)
    return high, (v - high.astype(F32)).astype(BF16)


def widen(v, spread):
    high, rest = halves(v)
    return mm(high, spread) + mm(rest, spread)


def head_sum(v, spread):
    high, rest = halves(v)
    return mm_t(high, spread) + mm_t(rest, spread)


def start_of(place, lens_ref):
    end, start = jnp.int32(0), jnp.zeros_like(place)
    for i in range(lens_ref.shape[0]):
        start = jnp.where(place >= end, end, start)
        end = end + lens_ref[i]
    return start


def taps(current, before, reach):
    whole = jnp.concatenate([before, current], axis=0)
    rows = current.shape[0]
    return [whole[HALO - k : HALO - k + rows] for k in range(reach)]


def filtered(shifted, allowed, kernel, bias):
    result = bias + kernel[0:1] * shifted[0]
    for k in range(1, len(shifted)):
        result = result + kernel[k : k + 1] * shifted[k] * allowed[k]
    return result


def permitted(place, start, reach, width):
    flags = [None]
    for k in range(1, reach):
        flags.append(jnp.where(place - k >= start, 1.0, 0.0)[:, :1])
    return flags


def softplus(v):
    return jnp.maximum(v, 0.0) + jnp.log1p(jnp.exp(-jnp.abs(v)))


def chunk_setup(base, lens_ref, span):
    place = base + lax.broadcasted_iota(jnp.int32, (span, LANES), 0)
    start = start_of(place, lens_ref)
    last_start = start_of(jnp.full((1, LANES), base + span - 1, jnp.int32), lens_ref)
    return place, start, last_start


def stacked(pair, low_lanes):
    zero = jnp.zeros_like(pair)
    return jnp.concatenate([jnp.where(low_lanes, pair, zero), jnp.where(low_lanes, zero, pair)], axis=0)


def forward_kernel(
    lens_ref, proj_ref, shared_ref, fw_ref, fb_ref, sf_ref, sb_ref, head_ref, skip_ref, spread_ref,
    out_ref, kept_ref, memory, before, shared_before,
):
    step = pl.program_id(0)
    span = proj_ref.shape[0]
    width = out_ref.shape[1]
    reach = fw_ref.shape[0]
    pairs = width // LANES
    base = step * span

    @pl.when(step == 0)
    def _():
        memory[...] = jnp.zeros_like(memory)
        before[...] = jnp.zeros_like(before)
        shared_before[...] = jnp.zeros_like(shared_before)

    place, start, last_start = chunk_setup(base, lens_ref, span)
    allowed = permitted(place, start, reach, width)
    inputs = proj_ref[:, :width]
    shared = shared_ref[...]
    conv = filtered(taps(inputs, before[...], reach), allowed, fw_ref, fb_ref[...])
    values = conv * jax.nn.sigmoid(conv)
    conv = filtered(taps(shared, shared_before[...], reach), allowed, sf_ref, sb_ref[...])
    factors = conv * jax.nn.sigmoid(conv)
    before[...] = inputs[span - HALO :]
    shared_before[...] = shared[span - HALO :]
    writes = factors[:, :LANES].astype(BF16)
    reads = factors[:, LANES:].astype(BF16)
    size = softplus(proj_ref[:, width:] + head_ref[0:1])
    decay = -size * head_ref[1:2]
    row = lax.broadcasted_iota(jnp.int32, (span, span), 0)
    col = lax.broadcasted_iota(jnp.int32, (span, span), 1)
    lower = jnp.where(row >= col, 1.0, 0.0)
    total = jnp.dot(lower, decay, precision=lax.Precision.HIGHEST, preferred_element_type=F32)
    total_t = total.T
    inside = (col <= row) & (col + base >= start)
    scores = jnp.where(inside, mm_t(reads, writes), 0.0)
    spread = spread_ref[...]
    scaled = values * widen(size, spread)
    scaled_low = scaled.astype(BF16)
    entering = jnp.exp(total) * jnp.where(start < base, 1.0, 0.0)
    state = memory[...]
    state_low = state.astype(BF16)
    kept_ref[0] = state_low
    remote = mm(reads, state_low) * widen(entering, spread) + skip_ref[...] * values
    low_lanes = lax.broadcasted_iota(jnp.int32, (span, LANES), 1) < LANES // 2
    for pair in range(pairs):
        lanes = slice(pair * LANES, (pair + 1) * LANES)
        mixing = []
        for head in (2 * pair, 2 * pair + 1):
            fade = jnp.exp(jnp.minimum(total[:, head : head + 1] - total_t[head : head + 1, :], 0.0))
            mixing.append((scores * fade).astype(BF16))
        local = mm(jnp.concatenate(mixing, axis=1), stacked(scaled_low[:, lanes], low_lanes))
        out_ref[:, lanes] = (local + remote[:, lanes]).astype(out_ref.dtype)
    end = total[span - 1 : span]
    closing = jnp.exp(end - total) * jnp.where(place >= last_start, 1.0, 0.0)
    added = mm(writes.T, (scaled * widen(closing, spread)).astype(BF16))
    keeping = jnp.exp(end) * jnp.where(last_start < base, 1.0, 0.0)
    memory[...] = state * widen(jnp.broadcast_to(keeping, (8, LANES)), spread)[0:1] + added


def backward_kernel(
    lens_ref, proj_ref, proj_before_ref, shared_ref, shared_before_ref, grad_ref, out_ref, kept_ref,
    fw_ref, fb_ref, sf_ref, sb_ref, head_ref, skip_ref, spread_ref,
    inputs_grad_ref, shared_grad_ref, raw_grad_ref, fsum_ref, ssum_ref, hsum_ref,
    memory_grad, after, shared_after,
):
    step = pl.program_id(0)
    steps = pl.num_programs(0)
    span = proj_ref.shape[0]
    width = out_ref.shape[1]
    reach = fw_ref.shape[0]
    pairs = width // LANES
    chunk = steps - 1 - step
    base = chunk * span

    @pl.when(step == 0)
    def _():
        memory_grad[...] = jnp.zeros_like(memory_grad)
        after[...] = jnp.zeros_like(after)
        shared_after[...] = jnp.zeros_like(shared_after)
        fsum_ref[...] = jnp.zeros_like(fsum_ref)
        ssum_ref[...] = jnp.zeros_like(ssum_ref)
        hsum_ref[...] = jnp.zeros_like(hsum_ref)

    place, start, last_start = chunk_setup(base, lens_ref, span)
    allowed = permitted(place, start, reach, width)
    first = jnp.where(chunk > 0, 1.0, 0.0)
    inputs = proj_ref[:, :width]
    shifted = taps(inputs, proj_before_ref[:, :width] * first, reach)
    conv = filtered(shifted, allowed, fw_ref, fb_ref[...])
    gate = jax.nn.sigmoid(conv)
    values = conv * gate
    slope = gate * (1.0 + conv * (1.0 - gate))
    shared_shifted = taps(shared_ref[...], shared_before_ref[...] * first, reach)
    conv = filtered(shared_shifted, allowed, sf_ref, sb_ref[...])
    gate = jax.nn.sigmoid(conv)
    factors = conv * gate
    shared_slope = gate * (1.0 + conv * (1.0 - gate))
    writes = factors[:, :LANES].astype(BF16)
    reads = factors[:, LANES:].astype(BF16)
    raw = proj_ref[:, width:] + head_ref[0:1]
    size = softplus(raw)
    decay = -size * head_ref[1:2]
    row = lax.broadcasted_iota(jnp.int32, (span, span), 0)
    col = lax.broadcasted_iota(jnp.int32, (span, span), 1)
    lower = jnp.where(row >= col, 1.0, 0.0)
    upper = jnp.where(row <= col, 1.0, 0.0)
    total = jnp.dot(lower, decay, precision=lax.Precision.HIGHEST, preferred_element_type=F32)
    total_t = total.T
    start_t = start_of(base + col[0:1], lens_ref)
    inside_t = (row <= col) & (row + base >= start_t)
    scores_t = jnp.where(inside_t, mm_t(writes, reads), 0.0)
    spread = spread_ref[...]
    size_wide = widen(size, spread)
    scaled = values * size_wide
    scaled_low = scaled.astype(BF16)
    grad = grad_ref[...].astype(F32)
    grad_low = grad.astype(BF16)
    state_low = kept_ref[0]
    later = memory_grad[...]
    later_low = later.astype(BF16)
    entering = jnp.exp(total) * jnp.where(start < base, 1.0, 0.0)
    entered = (grad * widen(entering, spread)).astype(BF16)
    end = total[span - 1 : span]
    closing = jnp.exp(end - total) * jnp.where(place >= last_start, 1.0, 0.0)
    closing_wide = widen(closing, spread)
    keeping = jnp.exp(end) * jnp.where(last_start < base, 1.0, 0.0)
    keeping_wide = widen(jnp.broadcast_to(keeping, (8, LANES)), spread)[0:1]
    closed = mm(writes, later_low) * closing_wide
    low_lanes = lax.broadcasted_iota(jnp.int32, (span, LANES), 1) < LANES // 2
    scores_grad_t = jnp.zeros((span, span), F32)
    local = []
    for pair in range(pairs):
        lanes = slice(pair * LANES, (pair + 1) * LANES)
        halved = stacked(grad_low[:, lanes], low_lanes)
        mixing_grad = mm_t(scaled_low[:, lanes], halved)
        mixing = []
        for which, head in enumerate((2 * pair, 2 * pair + 1)):
            fade = jnp.exp(jnp.minimum(total_t[head : head + 1, :] - total[:, head : head + 1], 0.0))
            mixing.append((scores_t * fade).astype(BF16))
            scores_grad_t = scores_grad_t + mixing_grad[:, which * span : (which + 1) * span] * fade
        local.append(mm(jnp.concatenate(mixing, axis=1), halved))
    scaled_grad = jnp.concatenate(local, axis=1) + closed
    scores_grad_t = jnp.where(inside_t, scores_grad_t, 0.0).astype(BF16)
    kept_closing = (scaled * closing_wide).astype(BF16)
    reads_grad = mm(scores_grad_t.T, writes) + mm_t(entered, state_low)
    writes_grad = mm(scores_grad_t, reads) + mm_t(kept_closing, later_low)
    memory_grad[...] = later * keeping_wide + mm(reads.T, entered)
    skip = skip_ref[...]
    size_grad = head_sum(values * scaled_grad, spread)
    paid = head_sum(
        grad_low.astype(F32) * (out_ref[...] - skip * values) - scaled_low.astype(F32) * scaled_grad, spread
    )
    tail = jnp.sum(scaled_low.astype(F32) * closed, axis=0, keepdims=True) + keeping_wide * jnp.sum(
        later * state_low.astype(F32), axis=0, keepdims=True
    )
    tail = head_sum(jnp.broadcast_to(tail, (8, width)), spread)[0:1]
    total_grad = paid + jnp.where(place == base + span - 1, tail, 0.0)
    decay_grad = jnp.dot(upper, total_grad, precision=lax.Precision.HIGHEST, preferred_element_type=F32)
    raw_grad = (size_grad - decay_grad * head_ref[1:2]) * jax.nn.sigmoid(raw)
    raw_grad_ref[...] = raw_grad.astype(raw_grad_ref.dtype)
    hsum_ref[0:1] += jnp.sum(raw_grad, axis=0, keepdims=True)
    hsum_ref[1:2] += jnp.sum(decay_grad * decay, axis=0, keepdims=True)
    conv_grad = (size_wide * scaled_grad + skip * grad) * slope
    shared_conv_grad = jnp.concatenate([writes_grad, reads_grad], axis=1) * shared_slope
    fsum_ref[reach : reach + 1] += jnp.sum(conv_grad, axis=0, keepdims=True)
    fsum_ref[reach + 1 : reach + 2] += jnp.sum(grad * values, axis=0, keepdims=True)
    ssum_ref[reach : reach + 1] += jnp.sum(shared_conv_grad, axis=0, keepdims=True)
    late = base + lax.broadcasted_iota(jnp.int32, (span + HALO, LANES), 0)
    late_allowed = permitted(late, start_of(late, lens_ref), reach, width)
    whole = jnp.concatenate([conv_grad, after[...]], axis=0)
    shared_whole = jnp.concatenate([shared_conv_grad, shared_after[...]], axis=0)
    result = fw_ref[0:1] * conv_grad
    shared_result = sf_ref[0:1] * shared_conv_grad
    fsum_ref[0:1] += jnp.sum(conv_grad * shifted[0], axis=0, keepdims=True)
    ssum_ref[0:1] += jnp.sum(shared_conv_grad * shared_shifted[0], axis=0, keepdims=True)
    for k in range(1, reach):
        masked = whole * late_allowed[k]
        fsum_ref[k : k + 1] += jnp.sum(masked[:span] * shifted[k], axis=0, keepdims=True)
        result = result + fw_ref[k : k + 1] * masked[k : k + span]
        masked = shared_whole * late_allowed[k]
        ssum_ref[k : k + 1] += jnp.sum(masked[:span] * shared_shifted[k], axis=0, keepdims=True)
        shared_result = shared_result + sf_ref[k : k + 1] * masked[k : k + span]
    after[...] = conv_grad[:HALO]
    shared_after[...] = shared_conv_grad[:HALO]
    inputs_grad_ref[...] = result.astype(inputs_grad_ref.dtype)
    shared_grad_ref[...] = shared_result.astype(shared_grad_ref.dtype)


def head_rows(step_bias, decay_log, skip_gain, width):
    heads = step_bias.shape[0]
    table = jnp.zeros((8, LANES), F32)
    table = table.at[0, :heads].set(step_bias).at[1, :heads].set(jnp.exp(decay_log))
    skip = jnp.repeat(skip_gain, width // heads)[None, :]
    spread = (jnp.arange(LANES)[:, None] == (jnp.arange(width) // (width // heads))[None, :]).astype(BF16)
    return table, skip, spread


def fixed(shape):
    return pl.BlockSpec(shape, lambda *_: (0,) * len(shape))


def mixer_forward(lens, proj, shared, fw, fb, sf, sb, table, skip, spread):
    rows = proj.shape[0]
    width = fw.shape[1]
    steps = rows // SPAN
    block = lambda cols: pl.BlockSpec((SPAN, cols), lambda i, *_: (i, 0))
    return pl.pallas_call(
        forward_kernel,
        grid_spec=pltpu.PrefetchScalarGridSpec(
            num_scalar_prefetch=1,
            grid=(steps,),
            in_specs=[
                block(proj.shape[1]), block(shared.shape[1]), fixed(fw.shape), fixed(fb.shape), fixed(sf.shape),
                fixed(sb.shape), fixed(table.shape), fixed(skip.shape), fixed(spread.shape),
            ],
            out_specs=[block(width), pl.BlockSpec((1, LANES, width), lambda i, *_: (i, 0, 0))],
            scratch_shapes=[
                pltpu.VMEM((LANES, width), F32),
                pltpu.VMEM((HALO, width), F32),
                pltpu.VMEM((HALO, shared.shape[1]), F32),
            ],
        ),
        out_shape=[
            jax.ShapeDtypeStruct((rows, width), F32),
            jax.ShapeDtypeStruct((steps, LANES, width), BF16),
        ],
        cost_estimate=pl.CostEstimate(flops=20 * 10**9, bytes_accessed=30 * 10**6, transcendentals=0),
        name="mixer_forward",
    )(lens, proj, shared, fw, fb, sf, sb, table, skip, spread)


def mixer_backward(lens, proj, shared, grad, out, kept, fw, fb, sf, sb, table, skip, spread):
    rows = proj.shape[0]
    width = fw.shape[1]
    steps = rows // SPAN
    lead = SPAN // HALO
    block = lambda cols: pl.BlockSpec((SPAN, cols), lambda i, *_: (steps - 1 - i, 0))
    ahead = lambda cols: pl.BlockSpec((HALO, cols), lambda i, *_: (jnp.maximum((steps - 1 - i) * lead - 1, 0), 0))
    return pl.pallas_call(
        backward_kernel,
        grid_spec=pltpu.PrefetchScalarGridSpec(
            num_scalar_prefetch=1,
            grid=(steps,),
            in_specs=[
                block(proj.shape[1]), ahead(proj.shape[1]), block(shared.shape[1]), ahead(shared.shape[1]),
                block(width), block(width), pl.BlockSpec((1, LANES, width), lambda i, *_: (steps - 1 - i, 0, 0)),
                fixed(fw.shape), fixed(fb.shape), fixed(sf.shape),
                fixed(sb.shape), fixed(table.shape), fixed(skip.shape), fixed(spread.shape),
            ],
            out_specs=[
                block(width), block(shared.shape[1]), block(LANES),
                fixed((8, width)), fixed((8, shared.shape[1])), fixed((8, LANES)),
            ],
            scratch_shapes=[
                pltpu.VMEM((LANES, width), F32),
                pltpu.VMEM((HALO, width), F32),
                pltpu.VMEM((HALO, shared.shape[1]), F32),
            ],
        ),
        out_shape=[
            jax.ShapeDtypeStruct((rows, width), BF16),
            jax.ShapeDtypeStruct((rows, shared.shape[1]), F32),
            jax.ShapeDtypeStruct((rows, LANES), BF16),
            jax.ShapeDtypeStruct((8, width), F32),
            jax.ShapeDtypeStruct((8, shared.shape[1]), F32),
            jax.ShapeDtypeStruct((8, LANES), F32),
        ],
        cost_estimate=pl.CostEstimate(flops=40 * 10**9, bytes_accessed=60 * 10**6, transcendentals=0),
        name="mixer_backward",
    )(lens, proj, proj, shared, shared, grad, out, kept, fw, fb, sf, sb, table, skip, spread)


def swap(v, axis, mask=1):
    count = lax.axis_size(axis)
    return lax.ppermute(v, axis, [(i, i ^ mask) for i in range(count)])


def diagonal(v):
    return lax.ppermute(v, ("side", "core"), [(i, i ^ 3) for i in range(4)])


def pick(stack, index, axis=0):
    return lax.dynamic_index_in_dim(stack, index, axis, keepdims=False)


def placed(pieces, spots, shape):
    lead = len(shape)
    tail = pieces[0].shape
    whole = jnp.zeros(shape + tail, pieces[0].dtype)
    for piece, spot in zip(pieces, spots):
        whole = lax.dynamic_update_slice(whole, piece.reshape((1,) * lead + tail), tuple(spot) + (0,) * len(tail))
    return whole


def row_doubling(v):
    pieces = [v]
    count = lax.axis_size("row")
    while len(pieces) < count:
        reach = len(pieces)
        pieces = pieces + [swap(p, "row", reach) for p in pieces]
    return pieces


def row_halving(pieces):
    while len(pieces) > 1:
        reach = len(pieces) // 2
        kept = pieces[:reach]
        pieces = [a + swap(b.astype(BF16), "row", reach).astype(F32) for a, b in zip(kept, pieces[reach:])]
    return pieces[0]


def line_gather(v):
    count = lax.axis_size("tensor")
    left, right = [v], [v]
    for j in range(1, count):
        left.append(lax.ppermute(left[-1], "tensor", [(i, i + 1) for i in range(j - 1, count - 1)]))
        right.append(lax.ppermute(right[-1], "tensor", [(i + 1, i) for i in range(0, count - j)]))
    return jnp.stack(left[:0:-1] + right)


def line_scatter(stack):
    count = lax.axis_size("tensor")
    plane = lax.axis_index("tensor")
    from_left = from_right = None
    for t in range(1, count):
        send_right = pick(stack, jnp.clip(count - t + plane, 0, count - 1))
        send_left = pick(stack, jnp.clip(plane - count + t, 0, count - 1))
        if t > 1:
            send_right = (send_right.astype(F32) + from_left.astype(F32)).astype(BF16)
            send_left = (send_left.astype(F32) + from_right.astype(F32)).astype(BF16)
        from_left = lax.ppermute(send_right, "tensor", [(i, i + 1) for i in range(t)])
        from_right = lax.ppermute(send_left, "tensor", [(count - 1 - i, count - 2 - i) for i in range(t)])
    return pick(stack, plane).astype(F32) + from_left.astype(F32) + from_right.astype(F32)


def whole_weight(piece, row, side, core):
    planes = line_gather(piece)
    plane = lax.axis_index("tensor")
    count = lax.axis_size("tensor")

    def shard(dx, dk):
        return pick(planes, (side ^ dx) * 2 + (core ^ dk) - plane + count - 1)

    pieces = [
        shard(0, 0),
        swap(shard(0, 1), "core"),
        swap(shard(1, 0), "side"),
        diagonal(shard(1, 1)),
    ]
    spots = [(side, core), (side, 1 - core), (1 - side, core), (1 - side, 1 - core)]
    return rows_joined(placed(pieces, spots, (2, 2)), row)


def rows_joined(block, row):
    blocks = row_doubling(block)
    count = len(blocks)
    whole = placed(blocks, [(row ^ d,) for d in range(count)], (count,))
    return whole.reshape(-1, whole.shape[-1])


def scattered_weight(grad, row, side, core):
    count = lax.axis_size("row")
    blocks = grad.reshape(count, 2, 2, -1, grad.shape[-1])
    mine = row_halving([pick(blocks, row ^ d) for d in range(count)]).astype(BF16)

    def part(dx, dk):
        return pick(pick(mine, side ^ dx), core ^ dk)

    pieces = [
        part(0, 0),
        swap(part(0, 1), "core"),
        swap(part(1, 0), "side"),
        diagonal(part(1, 1)),
    ]
    spots = [
        (side * 2 + core,),
        (side * 2 + 1 - core,),
        ((1 - side) * 2 + core,),
        ((1 - side) * 2 + 1 - core,),
    ]
    return line_scatter(placed(pieces, spots, (4,)))


def everywhere(v):
    for mask in (1, 2):
        v = v + swap(v, "tensor", mask)
    return v


def on_device(
    tokens, cotangent, destination, lengths, norm_gain, inner_weight, shared_weight, step_weight, filter_weight,
    filter_bias, shared_filter, shared_filter_bias, step_bias, decay_log, skip_gain, gate_gain, out_weight,
):
    row_count, model_width = tokens.shape
    width = filter_weight.shape[1]
    heads = step_bias.shape[0]
    rows_n, planes = lax.axis_size("row"), lax.axis_size("tensor")
    row, side, core, plane = (lax.axis_index(a) for a in ("row", "side", "core", "tensor"))
    group_rows = row_count // (rows_n * 4)
    source = (row * 2 + side) * 2 + core

    step_low = jnp.pad(step_weight.astype(BF16), ((0, 0), (0, LANES - heads)))
    in_piece = jnp.concatenate([inner_weight[:, 1].astype(BF16), step_low], axis=1)
    in_full = whole_weight(in_piece, row, side, core)
    shared_piece = shared_weight.astype(BF16)
    shared_pair = jnp.stack([shared_piece, swap(shared_piece, "core")])
    shared_side = swap(shared_pair, "side")
    shared_full = rows_joined(
        placed(
            [shared_pair[0], shared_pair[1], shared_side[0], shared_side[1]],
            [(side, core), (side, 1 - core), (1 - side, core), (1 - side, 1 - core)],
            (2, 2),
        ),
        row,
    )
    gate_full = whole_weight(inner_weight[:, 0].astype(BF16), row, side, core)
    out_full = whole_weight(out_weight.astype(BF16), row, side, core)

    params = jnp.concatenate(
        [
            filter_weight,
            filter_bias[None],
            gate_gain[None],
            jnp.pad(jnp.concatenate([step_bias, decay_log, skip_gain]), (0, width - 3 * heads))[None],
            jnp.zeros((1, width), F32),
        ],
        axis=0,
    )
    shards = line_gather(params)
    params = pick(shards, side * 2 + core - plane + planes - 1)
    fw, fb, gain = params[:4], params[4:5], params[5:6]
    bias_here, decay_here, skip_here = (params[6, i * heads : (i + 1) * heads] for i in range(3))
    sf, sb = shared_filter, shared_filter_bias[None]
    table, skip, spread = head_rows(bias_here, decay_here, skip_here, width)

    pair = jnp.stack([lengths[0], swap(lengths, "core")[0]])
    four = jnp.stack([pair, swap(pair, "side")])
    lens = pick(pick(four, (plane // 2) ^ side), (plane % 2) ^ core)

    block_of = lambda r: r * planes + plane
    wanted = jnp.concatenate(
        [
            block_of(row ^ d) * row_count + source * group_rows + jnp.arange(group_rows, dtype=jnp.int32)
            for d in range(rows_n)
        ]
    )
    chosen = (wanted[:, None] == destination[None, :]).astype(BF16)
    sent_tokens = jnp.dot(chosen, tokens, preferred_element_type=F32).astype(BF16).reshape(rows_n, group_rows, -1)
    sent_cot = jnp.dot(chosen, cotangent, preferred_element_type=F32).astype(BF16).reshape(rows_n, group_rows, -1)

    def exchanged(sent):
        pieces = [sent[0]] + [swap(sent[d], "row", d) for d in range(1, rows_n)]
        return placed(pieces, [(row ^ d,) for d in range(rows_n)], (rows_n,))

    def gathered(own):
        beside = swap(own, "side")
        pairs = [own, beside]
        others = [swap(p, "core") for p in pairs]
        whole = jnp.zeros((rows_n, 2, 2) + own.shape[1:], own.dtype)
        for dx in range(2):
            for dk, p in ((0, pairs[dx]), (1, others[dx])):
                whole = lax.dynamic_update_slice(whole, p[:, None, None], (0, side ^ dx, core ^ dk, 0, 0))
        return whole.reshape(-1, own.shape[-1])

    own_tokens = exchanged(sent_tokens)
    hidden = own_tokens.astype(F32)
    scale = lax.rsqrt(jnp.mean(hidden * hidden, axis=-1, keepdims=True) + EPSILON)
    own_normed = (hidden * scale * norm_gain).astype(BF16)
    normed = gathered(own_normed)
    own_cot = exchanged(sent_cot)
    cot = gathered(own_cot)

    proj = jnp.dot(normed, in_full, preferred_element_type=F32)
    shared = jnp.dot(normed, shared_full, preferred_element_type=F32)
    mixed, kept = mixer_forward(lens, proj, shared, fw, fb, sf, sb, table, skip, spread)
    gate_in = jnp.dot(normed, gate_full, preferred_element_type=F32)
    gate_sig = jax.nn.sigmoid(gate_in)
    gate_act = gate_in * gate_sig
    gated = mixed * gate_act
    square_sum = jnp.sum(gated * gated, axis=1)
    square_sum = square_sum + swap(square_sum, "core")
    square_sum = square_sum + swap(square_sum, "side")
    gate_scale = lax.rsqrt(square_sum / (4 * width) + EPSILON)[:, None]
    gate_normed = (gated * gate_scale * gain).astype(BF16)

    def part_rows(v, dx, dk):
        v = v.reshape(rows_n, 2, 2, group_rows, v.shape[-1])
        return pick(pick(v, side ^ dx, 1), core ^ dk, 1).reshape(rows_n * group_rows, v.shape[-1])

    def summed_rows(part):
        far = swap(part(1, 1).astype(BF16), "core")
        beside = swap((part(1, 0) + far.astype(F32)).astype(BF16), "side")
        near = swap(part(0, 1).astype(BF16), "core")
        return part(0, 0) + near.astype(F32) + beside.astype(F32)

    branch = summed_rows(lambda dx, dk: lax.dot_general(
        part_rows(gate_normed, dx, dk), out_full, (((1,), (1,)), ((), ())), preferred_element_type=F32))
    flat = lambda v: v.reshape(rows_n * group_rows, -1)

    lines = target_slots(destination, row_count, source, group_rows, planes, rows_n, plane)

    def returned(rows):
        rows = rows.reshape(rows_n, group_rows, -1)
        back = exchanged(jnp.stack([pick(rows, row ^ d) for d in range(rows_n)]))
        return line_gather(flat(back)).reshape(-1, rows.shape[-1])[lines]

    layer_out = returned((flat(hidden) + branch).astype(BF16))

    normed_grad = jnp.dot(cot, out_full, preferred_element_type=F32)
    out_grad = lax.dot_general(cot, gate_normed, (((0,), (0,)), ((), ())), preferred_element_type=F32)
    out_grad = scattered_weight(out_grad, row, side, core)
    gate_gain_grad = jnp.sum(normed_grad * gated * gate_scale, axis=0)
    scaled_grad = normed_grad * gain
    cross_sum = jnp.sum(scaled_grad * gated, axis=1)
    cross_sum = cross_sum + swap(cross_sum, "core")
    cross_sum = cross_sum + swap(cross_sum, "side")
    gated_grad = gate_scale * scaled_grad - gated * gate_scale**3 * (cross_sum / (4 * width))[:, None]
    mixed_grad = gated_grad * gate_act
    gate_in_grad = (gated_grad * mixed * gate_sig * (1.0 + gate_in * (1.0 - gate_sig))).astype(BF16)
    gate_grad = lax.dot_general(normed, gate_in_grad, (((0,), (0,)), ((), ())), preferred_element_type=F32)
    gate_grad = scattered_weight(gate_grad, row, side, core)
    inputs_grad, shared_part, raw_grad, fsum, ssum, hsum = mixer_backward(
        lens, proj, shared, mixed_grad, mixed, kept, fw, fb, sf, sb, table, skip, spread
    )
    proj_grad = jnp.concatenate([inputs_grad, raw_grad], axis=1)
    shared_grad = summed_rows(lambda dx, dk: part_rows(shared_part, dx, dk)).astype(BF16)
    normed_back = summed_rows(lambda dx, dk: (
        lax.dot_general(part_rows(gate_in_grad, dx, dk), gate_full, (((1,), (1,)), ((), ())), preferred_element_type=F32)
        + lax.dot_general(part_rows(proj_grad, dx, dk), in_full, (((1,), (1,)), ((), ())), preferred_element_type=F32)
    ))
    normed_back = normed_back + lax.dot_general(
        shared_grad, shared_full, (((1,), (1,)), ((), ())), preferred_element_type=F32
    )
    x, s = flat(hidden), flat(scale)
    norm_gain_grad = jnp.sum(normed_back * x * s, axis=0)
    gained = normed_back * norm_gain
    along = jnp.mean(gained * x, axis=1, keepdims=True)
    input_work = flat(own_cot).astype(F32) + s * gained - x * (s**3 * along)
    input_grad = returned(input_work.astype(BF16))

    proj_weight_grad = lax.dot_general(normed, proj_grad, (((0,), (0,)), ((), ())), preferred_element_type=F32)
    proj_weight_grad = scattered_weight(proj_weight_grad, row, side, core)
    inner_grad = jnp.stack([gate_grad, proj_weight_grad[:, :width]], axis=1)
    step_weight_grad = proj_weight_grad[:, width : width + heads]
    shared_weight_grad = lax.dot_general(
        flat(own_normed), shared_grad, (((0,), (0,)), ((), ())), preferred_element_type=F32
    ).reshape(rows_n, 2, 2, -1, shared.shape[1])
    shared_weight_grad = row_halving([pick(shared_weight_grad, row ^ d) for d in range(rows_n)])
    mine = pick(shared_weight_grad, core, 1) + swap(pick(shared_weight_grad, 1 - core, 1), "core")
    mine = pick(mine, side) + swap(pick(mine, 1 - side), "side")
    shared_weight_grad = everywhere(mine)

    line = lambda v: jnp.pad(v, (0, -v.shape[0] % width)).reshape(-1, width)
    skip_grad = fsum[5].reshape(heads, -1).sum(axis=1)
    small = jnp.concatenate(
        [
            fsum[:5],
            gate_gain_grad[None],
            jnp.pad(jnp.concatenate([hsum[0, :heads], hsum[1, :heads], skip_grad]), (0, width - 3 * heads))[None],
            jnp.zeros((1, width), F32),
            line(norm_gain_grad),
            line(ssum[:5].reshape(-1)),
        ],
        axis=0,
    )
    reach = 1
    while reach < rows_n:
        small = small + swap(small, "row", reach)
        reach = reach * 2
    small = everywhere(small)
    small = jnp.stack([small, swap(small, "core")])
    small = jnp.stack([small, swap(small, "side")])
    common = (small[0, 0, 8:] + small[0, 1, 8:]) + (small[1, 0, 8:] + small[1, 1, 8:])
    mine = pick(pick(small[:, :, :8], (plane // 2) ^ side), (plane % 2) ^ core)
    lines_n = line(norm_gain_grad).shape[0]
    norm_gain_grad = common[:lines_n].reshape(-1)[:model_width]
    shared_sums = common[lines_n:].reshape(-1)[: 5 * shared.shape[1]].reshape(5, -1)
    return (
        layer_out, input_grad, norm_gain_grad, inner_grad, shared_weight_grad, step_weight_grad,
        mine[:4], mine[4], shared_sums[:4], shared_sums[4],
        mine[6, :heads], mine[6, heads : 2 * heads], mine[6, 2 * heads : 3 * heads], mine[5], out_grad,
    )


def target_slots(destination, row_count, source, group_rows, planes, rows_n, plane):
    block = destination // row_count
    row_of, plane_of = block // planes, block % planes
    place = destination - block * row_count - source * group_rows
    return ((plane_of - plane + planes - 1) * rows_n + row_of) * group_rows + place


def solution(mesh):
    count, planes = mesh.devices.shape
    names = ("row", "side", "core", "tensor")
    inner = jax.sharding.Mesh(mesh.devices.reshape(count // 4, 2, 2, planes), names)
    dp = ("row", "side", "core")
    in_specs = (
        P(dp, None), P(dp, None), P(dp), P(dp, None), P(), P(dp, None, "tensor"), P(dp, None), P(dp, "tensor"),
        P(None, "tensor"), P("tensor"), P(), P(), P("tensor"), P("tensor"), P("tensor"), P("tensor"), P(dp, "tensor"),
    )
    out_specs = (
        P(dp, None), P(dp, None), P(), P(dp, None, "tensor"), P(dp, None), P(dp, "tensor"),
        P(None, "tensor"), P("tensor"), P(), P(), P("tensor"), P("tensor"), P("tensor"), P("tensor"), P(dp, "tensor"),
    )
    return jax.shard_map(on_device, mesh=inner, in_specs=in_specs, out_specs=out_specs, check_vma=False)
```

```python
import jax
import jax.numpy as jnp
from jax import lax
from jax.experimental import pallas as pl
from jax.experimental.pallas import tpu as pltpu
from jax.sharding import PartitionSpec as P

SPAN = 128
HALO = 8
LANES = 128
F32 = jnp.float32
BF16 = jnp.bfloat16
EPSILON = 1e-05


def mm(a, b):
    return jnp.dot(a, b, preferred_element_type=F32)


def mm_t(a, b):
    return lax.dot_general(a, b, (((1,), (1,)), ((), ())), preferred_element_type=F32)


def halves(v):
    high = v.astype(BF16)
    return high, (v - high.astype(F32)).astype(BF16)


def widen(v, spread):
    high, rest = halves(v)
    return mm(high, spread) + mm(rest, spread)


def head_sum(v, spread):
    high, rest = halves(v)
    return mm_t(high, spread) + mm_t(rest, spread)


def start_of(place, lens_ref):
    end, start = jnp.int32(0), jnp.zeros_like(place)
    for i in range(lens_ref.shape[0]):
        start = jnp.where(place >= end, end, start)
        end = end + lens_ref[i]
    return start


def taps(current, before, reach):
    whole = jnp.concatenate([before, current], axis=0)
    rows = current.shape[0]
    return [whole[HALO - k : HALO - k + rows] for k in range(reach)]


def filtered(shifted, allowed, kernel, bias):
    result = bias + kernel[0:1] * shifted[0]
    for k in range(1, len(shifted)):
        result = result + kernel[k : k + 1] * shifted[k] * allowed[k]
    return result


def permitted(place, start, reach, width):
    flags = [None]
    for k in range(1, reach):
        flags.append(jnp.where(place - k >= start, 1.0, 0.0)[:, :1])
    return flags


def softplus(v):
    return jnp.maximum(v, 0.0) + jnp.log1p(jnp.exp(-jnp.abs(v)))


def chunk_setup(base, lens_ref, span):
    place = base + lax.broadcasted_iota(jnp.int32, (span, LANES), 0)
    start = start_of(place, lens_ref)
    last_start = start_of(jnp.full((1, LANES), base + span - 1, jnp.int32), lens_ref)
    return place, start, last_start


def stacked(pair, low_lanes):
    zero = jnp.zeros_like(pair)
    return jnp.concatenate([jnp.where(low_lanes, pair, zero), jnp.where(low_lanes, zero, pair)], axis=0)


def forward_kernel(
    lens_ref, order_ref, proj_ref, fw_ref, fb_ref, sf_ref, sb_ref, head_ref, skip_ref, spread_ref,
    out_ref, kept_ref, memory, before, shared_before,
):
    step = pl.program_id(0)
    span = proj_ref.shape[0]
    width = out_ref.shape[1]
    reach = fw_ref.shape[0]
    pairs = width // LANES
    base = step * span

    @pl.when(step == 0)
    def _():
        memory[...] = jnp.zeros_like(memory)
        before[...] = jnp.zeros_like(before)
        shared_before[...] = jnp.zeros_like(shared_before)

    place, start, last_start = chunk_setup(base, lens_ref, span)
    allowed = permitted(place, start, reach, width)
    inputs = proj_ref[:, :width]
    shared = proj_ref[:, width + LANES :]
    conv = filtered(taps(inputs, before[...], reach), allowed, fw_ref, fb_ref[...])
    values = conv * jax.nn.sigmoid(conv)
    conv = filtered(taps(shared, shared_before[...], reach), allowed, sf_ref, sb_ref[...])
    factors = conv * jax.nn.sigmoid(conv)
    before[...] = inputs[span - HALO :]
    shared_before[...] = shared[span - HALO :]
    writes = factors[:, :LANES].astype(BF16)
    reads = factors[:, LANES:].astype(BF16)
    size = softplus(proj_ref[:, width : width + LANES] + head_ref[0:1])
    decay = -size * head_ref[1:2]
    row = lax.broadcasted_iota(jnp.int32, (span, span), 0)
    col = lax.broadcasted_iota(jnp.int32, (span, span), 1)
    lower = jnp.where(row >= col, 1.0, 0.0)
    total = jnp.dot(lower, decay, precision=lax.Precision.HIGHEST, preferred_element_type=F32)
    total_t = total.T
    inside = (col <= row) & (col + base >= start)
    scores = jnp.where(inside, mm_t(reads, writes), 0.0)
    spread = spread_ref[...]
    scaled = values * widen(size, spread)
    scaled_low = scaled.astype(BF16)
    entering = jnp.exp(total) * jnp.where(start < base, 1.0, 0.0)
    state = memory[...]
    state_low = state.astype(BF16)
    kept_ref[0] = state_low
    remote = mm(reads, state_low) * widen(entering, spread) + skip_ref[...] * values
    low_lanes = lax.broadcasted_iota(jnp.int32, (span, LANES), 1) < LANES // 2
    for pair in range(pairs):
        lanes = slice(pair * LANES, (pair + 1) * LANES)
        mixing = []
        for head in (2 * pair, 2 * pair + 1):
            fade = jnp.exp(jnp.minimum(total[:, head : head + 1] - total_t[head : head + 1, :], 0.0))
            mixing.append((scores * fade).astype(BF16))
        local = mm(jnp.concatenate(mixing, axis=1), stacked(scaled_low[:, lanes], low_lanes))
        out_ref[:, lanes] = (local + remote[:, lanes]).astype(out_ref.dtype)
    end = total[span - 1 : span]
    closing = jnp.exp(end - total) * jnp.where(place >= last_start, 1.0, 0.0)
    added = mm(writes.T, (scaled * widen(closing, spread)).astype(BF16))
    keeping = jnp.exp(end) * jnp.where(last_start < base, 1.0, 0.0)
    memory[...] = state * widen(jnp.broadcast_to(keeping, (8, LANES)), spread)[0:1] + added


def backward_kernel(
    lens_ref, order_ref, proj_ref, proj_before_ref, grad_ref, out_ref, kept_ref,
    fw_ref, fb_ref, sf_ref, sb_ref, head_ref, skip_ref, spread_ref,
    proj_grad_ref, shared_grad_ref, fsum_ref, ssum_ref, hsum_ref,
    memory_grad, after, shared_after,
):
    step = pl.program_id(0)
    steps = pl.num_programs(0)
    span = proj_ref.shape[0]
    width = out_ref.shape[1]
    reach = fw_ref.shape[0]
    pairs = width // LANES
    chunk = steps - 1 - step
    base = chunk * span

    @pl.when(step == 0)
    def _():
        memory_grad[...] = jnp.zeros_like(memory_grad)
        after[...] = jnp.zeros_like(after)
        shared_after[...] = jnp.zeros_like(shared_after)
        fsum_ref[...] = jnp.zeros_like(fsum_ref)
        ssum_ref[...] = jnp.zeros_like(ssum_ref)
        hsum_ref[...] = jnp.zeros_like(hsum_ref)

    place, start, last_start = chunk_setup(base, lens_ref, span)
    allowed = permitted(place, start, reach, width)
    first = jnp.where(chunk > 0, 1.0, 0.0)
    inputs = proj_ref[:, :width]
    shifted = taps(inputs, proj_before_ref[:, :width] * first, reach)
    conv = filtered(shifted, allowed, fw_ref, fb_ref[...])
    gate = jax.nn.sigmoid(conv)
    values = conv * gate
    slope = gate * (1.0 + conv * (1.0 - gate))
    shared_shifted = taps(proj_ref[:, width + LANES :], proj_before_ref[:, width + LANES :] * first, reach)
    conv = filtered(shared_shifted, allowed, sf_ref, sb_ref[...])
    gate = jax.nn.sigmoid(conv)
    factors = conv * gate
    shared_slope = gate * (1.0 + conv * (1.0 - gate))
    writes = factors[:, :LANES].astype(BF16)
    reads = factors[:, LANES:].astype(BF16)
    raw = proj_ref[:, width : width + LANES] + head_ref[0:1]
    size = softplus(raw)
    decay = -size * head_ref[1:2]
    row = lax.broadcasted_iota(jnp.int32, (span, span), 0)
    col = lax.broadcasted_iota(jnp.int32, (span, span), 1)
    lower = jnp.where(row >= col, 1.0, 0.0)
    upper = jnp.where(row <= col, 1.0, 0.0)
    total = jnp.dot(lower, decay, precision=lax.Precision.HIGHEST, preferred_element_type=F32)
    total_t = total.T
    start_t = start_of(base + col[0:1], lens_ref)
    inside_t = (row <= col) & (row + base >= start_t)
    scores_t = jnp.where(inside_t, mm_t(writes, reads), 0.0)
    spread = spread_ref[...]
    size_wide = widen(size, spread)
    scaled = values * size_wide
    scaled_low = scaled.astype(BF16)
    grad = grad_ref[...].astype(F32)
    grad_low = grad.astype(BF16)
    state_low = kept_ref[0]
    later = memory_grad[...]
    later_low = later.astype(BF16)
    entering = jnp.exp(total) * jnp.where(start < base, 1.0, 0.0)
    entered = (grad * widen(entering, spread)).astype(BF16)
    end = total[span - 1 : span]
    closing = jnp.exp(end - total) * jnp.where(place >= last_start, 1.0, 0.0)
    closing_wide = widen(closing, spread)
    keeping = jnp.exp(end) * jnp.where(last_start < base, 1.0, 0.0)
    keeping_wide = widen(jnp.broadcast_to(keeping, (8, LANES)), spread)[0:1]
    closed = mm(writes, later_low) * closing_wide
    low_lanes = lax.broadcasted_iota(jnp.int32, (span, LANES), 1) < LANES // 2
    scores_grad_t = jnp.zeros((span, span), F32)
    local = []
    for pair in range(pairs):
        lanes = slice(pair * LANES, (pair + 1) * LANES)
        halved = stacked(grad_low[:, lanes], low_lanes)
        mixing_grad = mm_t(scaled_low[:, lanes], halved)
        mixing = []
        for which, head in enumerate((2 * pair, 2 * pair + 1)):
            fade = jnp.exp(jnp.minimum(total_t[head : head + 1, :] - total[:, head : head + 1], 0.0))
            mixing.append((scores_t * fade).astype(BF16))
            scores_grad_t = scores_grad_t + mixing_grad[:, which * span : (which + 1) * span] * fade
        local.append(mm(jnp.concatenate(mixing, axis=1), halved))
    scaled_grad = jnp.concatenate(local, axis=1) + closed
    scores_grad_t = jnp.where(inside_t, scores_grad_t, 0.0).astype(BF16)
    kept_closing = (scaled * closing_wide).astype(BF16)
    reads_grad = mm(scores_grad_t.T, writes) + mm_t(entered, state_low)
    writes_grad = mm(scores_grad_t, reads) + mm_t(kept_closing, later_low)
    memory_grad[...] = later * keeping_wide + mm(reads.T, entered)
    skip = skip_ref[...]
    size_grad = head_sum(values * scaled_grad, spread)
    paid = head_sum(
        grad_low.astype(F32) * (out_ref[...] - skip * values) - scaled_low.astype(F32) * scaled_grad, spread
    )
    tail = jnp.sum(scaled_low.astype(F32) * closed, axis=0, keepdims=True) + keeping_wide * jnp.sum(
        later * state_low.astype(F32), axis=0, keepdims=True
    )
    tail = head_sum(jnp.broadcast_to(tail, (8, width)), spread)[0:1]
    total_grad = paid + jnp.where(place == base + span - 1, tail, 0.0)
    decay_grad = jnp.dot(upper, total_grad, precision=lax.Precision.HIGHEST, preferred_element_type=F32)
    raw_grad = (size_grad - decay_grad * head_ref[1:2]) * jax.nn.sigmoid(raw)
    proj_grad_ref[:, width:] = raw_grad.astype(proj_grad_ref.dtype)
    hsum_ref[0:1] += jnp.sum(raw_grad, axis=0, keepdims=True)
    hsum_ref[1:2] += jnp.sum(decay_grad * decay, axis=0, keepdims=True)
    conv_grad = (size_wide * scaled_grad + skip * grad) * slope
    shared_conv_grad = jnp.concatenate([writes_grad, reads_grad], axis=1) * shared_slope
    fsum_ref[reach : reach + 1] += jnp.sum(conv_grad, axis=0, keepdims=True)
    fsum_ref[reach + 1 : reach + 2] += jnp.sum(grad * values, axis=0, keepdims=True)
    ssum_ref[reach : reach + 1] += jnp.sum(shared_conv_grad, axis=0, keepdims=True)
    late = base + lax.broadcasted_iota(jnp.int32, (span + HALO, LANES), 0)
    late_allowed = permitted(late, start_of(late, lens_ref), reach, width)
    whole = jnp.concatenate([conv_grad, after[...]], axis=0)
    shared_whole = jnp.concatenate([shared_conv_grad, shared_after[...]], axis=0)
    result = fw_ref[0:1] * conv_grad
    shared_result = sf_ref[0:1] * shared_conv_grad
    fsum_ref[0:1] += jnp.sum(conv_grad * shifted[0], axis=0, keepdims=True)
    ssum_ref[0:1] += jnp.sum(shared_conv_grad * shared_shifted[0], axis=0, keepdims=True)
    for k in range(1, reach):
        masked = whole * late_allowed[k]
        fsum_ref[k : k + 1] += jnp.sum(masked[:span] * shifted[k], axis=0, keepdims=True)
        result = result + fw_ref[k : k + 1] * masked[k : k + span]
        masked = shared_whole * late_allowed[k]
        ssum_ref[k : k + 1] += jnp.sum(masked[:span] * shared_shifted[k], axis=0, keepdims=True)
        shared_result = shared_result + sf_ref[k : k + 1] * masked[k : k + span]
    after[...] = conv_grad[:HALO]
    shared_after[...] = shared_conv_grad[:HALO]
    proj_grad_ref[:, :width] = result.astype(proj_grad_ref.dtype)
    shared_grad_ref[...] = shared_result.astype(shared_grad_ref.dtype)


def head_rows(step_bias, decay_log, skip_gain, width):
    heads = step_bias.shape[0]
    table = jnp.zeros((8, LANES), F32)
    table = table.at[0, :heads].set(step_bias).at[1, :heads].set(jnp.exp(decay_log))
    skip = jnp.repeat(skip_gain, width // heads)[None, :]
    spread = (jnp.arange(LANES)[:, None] == (jnp.arange(width) // (width // heads))[None, :]).astype(BF16)
    return table, skip, spread


def fixed(shape):
    return pl.BlockSpec(shape, lambda *_: (0,) * len(shape))


def mixer_forward(lens, order, proj, fw, fb, sf, sb, table, skip, spread):
    rows = proj.shape[0]
    width = fw.shape[1]
    steps = rows // SPAN
    block = lambda cols: pl.BlockSpec((SPAN, cols), lambda i, lens_ref, order_ref: (order_ref[i], 0))
    return pl.pallas_call(
        forward_kernel,
        grid_spec=pltpu.PrefetchScalarGridSpec(
            num_scalar_prefetch=2,
            grid=(steps,),
            in_specs=[
                block(proj.shape[1]), fixed(fw.shape), fixed(fb.shape), fixed(sf.shape),
                fixed(sb.shape), fixed(table.shape), fixed(skip.shape), fixed(spread.shape),
            ],
            out_specs=[block(width), pl.BlockSpec((1, LANES, width), lambda i, *_: (i, 0, 0))],
            scratch_shapes=[
                pltpu.VMEM((LANES, width), F32),
                pltpu.VMEM((HALO, width), F32),
                pltpu.VMEM((HALO, sf.shape[1]), F32),
            ],
        ),
        out_shape=[
            jax.ShapeDtypeStruct((rows, width), F32),
            jax.ShapeDtypeStruct((steps, LANES, width), BF16),
        ],
        cost_estimate=pl.CostEstimate(flops=20 * 10**9, bytes_accessed=30 * 10**6, transcendentals=0),
        name="mixer_forward",
    )(lens, order, proj, fw, fb, sf, sb, table, skip, spread)


def mixer_backward(lens, order, proj, grad, out, kept, fw, fb, sf, sb, table, skip, spread):
    rows = proj.shape[0]
    width = fw.shape[1]
    steps = rows // SPAN
    lead = SPAN // HALO
    block = lambda cols: pl.BlockSpec((SPAN, cols), lambda i, lens_ref, order_ref: (order_ref[steps - 1 - i], 0))
    ahead = lambda cols: pl.BlockSpec(
        (HALO, cols),
        lambda i, lens_ref, order_ref: (order_ref[jnp.maximum(steps - 2 - i, 0)] * lead + lead - 1, 0),
    )
    return pl.pallas_call(
        backward_kernel,
        grid_spec=pltpu.PrefetchScalarGridSpec(
            num_scalar_prefetch=2,
            grid=(steps,),
            in_specs=[
                block(proj.shape[1]), ahead(proj.shape[1]),
                block(width), block(width), pl.BlockSpec((1, LANES, width), lambda i, *_: (steps - 1 - i, 0, 0)),
                fixed(fw.shape), fixed(fb.shape), fixed(sf.shape),
                fixed(sb.shape), fixed(table.shape), fixed(skip.shape), fixed(spread.shape),
            ],
            out_specs=[
                block(width + LANES), block(sf.shape[1]),
                fixed((8, width)), fixed((8, sf.shape[1])), fixed((8, LANES)),
            ],
            scratch_shapes=[
                pltpu.VMEM((LANES, width), F32),
                pltpu.VMEM((HALO, width), F32),
                pltpu.VMEM((HALO, sf.shape[1]), F32),
            ],
        ),
        out_shape=[
            jax.ShapeDtypeStruct((rows, width + LANES), BF16),
            jax.ShapeDtypeStruct((rows, sf.shape[1]), F32),
            jax.ShapeDtypeStruct((8, width), F32),
            jax.ShapeDtypeStruct((8, sf.shape[1]), F32),
            jax.ShapeDtypeStruct((8, LANES), F32),
        ],
        cost_estimate=pl.CostEstimate(flops=40 * 10**9, bytes_accessed=60 * 10**6, transcendentals=0),
        name="mixer_backward",
    )(lens, order, proj, proj, grad, out, kept, fw, fb, sf, sb, table, skip, spread)


def swap(v, axis, mask=1):
    count = lax.axis_size(axis)
    return lax.ppermute(v, axis, [(i, i ^ mask) for i in range(count)])


def crossed(v):
    pairs = [(a * 4 + b, b * 4 + a) for a in range(4) for b in range(4)]
    return lax.ppermute(v, ("side", "core", "tensor"), pairs)


def pick(stack, index, axis=0):
    return lax.dynamic_index_in_dim(stack, index, axis, keepdims=False)


def in_order(pieces, index):
    if len(pieces) == 2:
        first, second = pieces
        even = index == 0
        return jnp.stack([jnp.where(even, first, second), jnp.where(even, second, first)])
    whole = jnp.stack(pieces)
    return jnp.stack([pick(whole, index ^ i) for i in range(len(pieces))])


def row_doubling(v):
    pieces = [v]
    while len(pieces) < lax.axis_size("row"):
        reach = len(pieces)
        pieces = pieces + [swap(p, "row", reach) for p in pieces]
    return pieces


def line_flood(v):
    count = lax.axis_size("tensor")
    left, right = [v], [v]
    for j in range(1, count):
        left.append(lax.ppermute(left[-1], "tensor", [(i, i + 1) for i in range(j - 1, count - 1)]))
        right.append(lax.ppermute(right[-1], "tensor", [(i + 1, i) for i in range(0, count - j)]))
    return left[1:], right[1:]


def summed(v, axes):
    for axis in axes:
        reach = 1
        while reach < lax.axis_size(axis):
            v = v + swap(v, axis, reach)
            reach = reach * 2
    return v


def contract_rows(a, b):
    return lax.dot_general(a, b, (((0,), (0,)), ((), ())), preferred_element_type=F32)


def contract_columns(a, b):
    return lax.dot_general(a, b, (((1,), (1,)), ((), ())), preferred_element_type=F32)


def on_device(
    tokens, cotangent, destination, lengths, norm_gain, inner_weight, shared_weight, step_weight, filter_weight,
    filter_bias, shared_filter, shared_filter_bias, step_bias, decay_log, skip_gain, gate_gain, out_weight,
):
    row_count, model_width = tokens.shape
    width = filter_weight.shape[1]
    heads = step_bias.shape[0]
    rows_n, planes = lax.axis_size("row"), lax.axis_size("tensor")
    row, side, core, plane = (lax.axis_index(a) for a in ("row", "side", "core", "tensor"))
    group_rows = row_count // (rows_n * 4)
    owned = rows_n * group_rows
    source = (row * 2 + side) * 2 + core

    wanted = jnp.concatenate(
        [
            ((row ^ d) * planes + plane) * row_count + source * group_rows + jnp.arange(group_rows, dtype=jnp.int32)
            for d in range(rows_n)
        ]
    )
    chosen = (wanted[:, None] == destination[None, :]).astype(BF16)

    def exchanged(sent):
        return jnp.concatenate([sent[:group_rows]] + [
            swap(sent[d * group_rows : (d + 1) * group_rows], "row", d) for d in range(1, rows_n)
        ])

    def gathered(own):
        beside = swap(own, "side")
        return jnp.concatenate([own, swap(own, "core"), beside, swap(beside, "core")])

    own_tokens = exchanged(jnp.dot(chosen, tokens, preferred_element_type=F32).astype(BF16))
    hidden = own_tokens.astype(F32)
    scale = lax.rsqrt(jnp.mean(hidden * hidden, axis=-1, keepdims=True) + EPSILON)
    normed = gathered((hidden * scale * norm_gain).astype(BF16))
    own_cot = exchanged(jnp.dot(chosen, cotangent, preferred_element_type=F32).astype(BF16))
    cot = gathered(own_cot)

    step_low = jnp.pad(step_weight.astype(BF16), ((0, 0), (0, LANES - heads)))
    piece = jnp.concatenate([inner_weight[:, 1].astype(BF16), step_low, shared_weight.astype(BF16)], axis=1)
    blocks = in_order(row_doubling(crossed(piece)), row)
    left, right = line_flood(blocks)
    stack = jnp.stack(left[::-1] + [blocks] + right)
    in_full = lax.dynamic_slice_in_dim(stack, planes - 1 - plane, planes, 0)
    in_full = in_full.transpose(1, 0, 2, 3).reshape(model_width, -1)
    piece = jnp.concatenate([inner_weight[:, 0].astype(BF16), out_weight.astype(BF16)], axis=1)
    both_full = lax.all_gather(crossed(piece), ("row", "tensor"), axis=0, tiled=True)
    gate_full, out_full = both_full[:, :width], both_full[:, width:]

    params = jnp.concatenate(
        [
            filter_weight,
            filter_bias[None],
            gate_gain[None],
            jnp.pad(jnp.concatenate([step_bias, decay_log, skip_gain]), (0, width - 3 * heads))[None],
            jnp.pad(lengths.astype(F32), ((0, 0), (0, width - lengths.shape[1]))),
        ],
        axis=0,
    )
    params = crossed(params)
    fw, fb, gain = params[:4], params[4:5], params[5:6]
    bias_here, decay_here, skip_here = (params[6, i * heads : (i + 1) * heads] for i in range(3))
    lens = params[7, : lengths.shape[1]].astype(jnp.int32)
    sf, sb = shared_filter, shared_filter_bias[None]
    table, skip, spread = head_rows(bias_here, decay_here, skip_here, width)

    if group_rows % SPAN == 0:
        spans = jnp.arange(row_count // SPAN, dtype=jnp.int32)
        part = (spans * SPAN // group_rows) ^ source
        order = (((part // 2) % 2 * 2 + part % 2) * rows_n + part // 4) * (group_rows // SPAN)
        order = order + spans % (group_rows // SPAN)
        sequenced = unsequenced = lambda v: v
    else:
        order = jnp.arange(row_count // SPAN, dtype=jnp.int32)
        groups = jnp.arange(4 * rows_n, dtype=jnp.int32)
        part = groups ^ source
        to = ((part // 2) % 2 * 2 + part % 2) * rows_n + part // 4
        fro = (((groups % rows_n) * 4 + groups // rows_n) ^ source)
        sequenced = lambda v: v.reshape(4 * rows_n, group_rows, -1)[to].reshape(v.shape)
        unsequenced = lambda v: v.reshape(4 * rows_n, group_rows, -1)[fro].reshape(v.shape)

    def summed_over_group(v):
        v = v + swap(v, "core").reshape(2, 2, owned)[:, ::-1].reshape(-1)
        return v + swap(v, "side").reshape(2, 2 * owned)[::-1].reshape(-1)

    proj = sequenced(jnp.dot(normed, in_full, preferred_element_type=F32))
    mixed_seq, kept = mixer_forward(lens, order, proj, fw, fb, sf, sb, table, skip, spread)
    mixed = unsequenced(mixed_seq)
    gate_in = lax.optimization_barrier(jnp.dot(normed, gate_full, preferred_element_type=F32))
    gate_sig = jax.nn.sigmoid(gate_in)
    gate_act = gate_in * gate_sig
    gated = mixed * gate_act
    square_sum = summed_over_group(jnp.sum(gated * gated, axis=1))
    gate_scale = lax.rsqrt(square_sum / (4 * width) + EPSILON)[:, None]
    gate_normed = (gated * gate_scale * gain).astype(BF16)

    def rows_of(v, dx, dk):
        return v[(dx * 2 + dk) * owned : (dx * 2 + dk + 1) * owned]

    def summed_rows(part):
        far = swap(part(1, 1).astype(BF16), "core")
        beside = swap((part(1, 0) + far.astype(F32)).astype(BF16), "side")
        near = swap(part(0, 1).astype(BF16), "core")
        return part(0, 0) + near.astype(F32) + beside.astype(F32)

    block_of = destination // row_count
    row_of, plane_of = (block_of // planes) ^ row, block_of % planes
    slot = row_of * group_rows + destination - block_of * row_count - source * group_rows
    steps_down = (plane - plane_of) % planes

    def returned(rows):
        back = exchanged(rows)
        left, right = line_flood(back)
        held = [back] + [jnp.where(plane >= j, left[j - 1], right[planes - 1 - j]) for j in range(1, planes)]

        def settled(which):
            where = jnp.concatenate([jnp.where(steps_down == j, slot, -1)[:, None] == jnp.arange(owned)[None, :]
                                     for j in which], axis=1)
            return jnp.dot(where.astype(BF16), jnp.concatenate([held[j] for j in which]), preferred_element_type=F32)
        return (settled((0, 2)).astype(BF16) + settled((1, 3)).astype(BF16))

    branch = summed_rows(lambda dx, dk: contract_columns(rows_of(gate_normed, dx, dk), out_full))
    layer_out = returned((hidden + branch).astype(BF16))

    normed_grad = lax.optimization_barrier(jnp.dot(cot, out_full, preferred_element_type=F32))
    out_grad = contract_rows(cot, gate_normed).astype(BF16)
    gate_gain_grad = jnp.sum(normed_grad * gated * gate_scale, axis=0)
    scaled_grad = normed_grad * gain
    cross_sum = summed_over_group(jnp.sum(scaled_grad * gated, axis=1))
    gated_grad = gate_scale * scaled_grad - gated * gate_scale**3 * (cross_sum / (4 * width))[:, None]
    mixed_grad = gated_grad * gate_act
    gate_in_grad = (gated_grad * mixed * gate_sig * (1.0 + gate_in * (1.0 - gate_sig))).astype(BF16)
    gate_grad = contract_rows(normed, gate_in_grad).astype(BF16)
    both_grad = jnp.concatenate([gate_grad, out_grad], axis=1)
    both_grad = lax.psum_scatter(both_grad, ("row", "tensor"), scatter_dimension=0, tiled=True)
    both_grad = crossed(both_grad).astype(F32)
    proj_grad, shared_part, fsum, ssum, hsum = mixer_backward(
        lens, order, proj, sequenced(mixed_grad), mixed_seq, kept, fw, fb, sf, sb, table, skip, spread
    )
    proj_grad, shared_part = unsequenced(proj_grad), unsequenced(shared_part)
    back = summed_rows(lambda dx, dk: jnp.concatenate([
        contract_columns(rows_of(gate_in_grad, dx, dk), gate_full)
        + contract_columns(rows_of(proj_grad, dx, dk), in_full[:, : width + LANES]),
        rows_of(shared_part, dx, dk),
    ], axis=1))
    own_shared = back[:, model_width:].astype(BF16)
    normed_back = back[:, :model_width] + contract_columns(own_shared, in_full[:, width + LANES :])
    norm_gain_grad = jnp.sum(normed_back * hidden * scale, axis=0)
    gained = normed_back * norm_gain
    along = jnp.mean(gained * hidden, axis=1, keepdims=True)
    input_work = own_cot.astype(F32) + scale * gained - hidden * (scale**3 * along)
    input_grad = returned(input_work.astype(BF16))

    in_grad = contract_rows(normed, jnp.concatenate([proj_grad, gathered(own_shared)], axis=1)).astype(BF16)
    in_grad = lax.psum_scatter(in_grad, ("row", "tensor"), scatter_dimension=0, tiled=True)
    in_grad = crossed(in_grad).astype(F32)
    inner_grad = jnp.stack([both_grad[:, :width], in_grad[:, :width]], axis=1)

    line = lambda v: jnp.pad(v, (0, -v.shape[0] % width)).reshape(-1, width)
    skip_grad = fsum[5].reshape(heads, -1).sum(axis=1)
    small = jnp.concatenate(
        [
            fsum[:5],
            gate_gain_grad[None],
            jnp.pad(jnp.concatenate([hsum[0, :heads], hsum[1, :heads], skip_grad]), (0, width - 3 * heads))[None],
            jnp.zeros((1, width), F32),
            line(norm_gain_grad),
            line(ssum[:5].reshape(-1)),
        ],
        axis=0,
    )
    small = summed(small, ("row", "tensor"))
    mine = crossed(small[:8])
    common = summed(small[8:], ("core", "side"))
    lines = line(norm_gain_grad).shape[0]
    norm_gain_grad = common[:lines].reshape(-1)[:model_width]
    shared_sums = common[lines:].reshape(-1)[: 5 * sf.shape[1]].reshape(5, -1)
    return (
        layer_out, input_grad, norm_gain_grad, inner_grad, in_grad[:, width + LANES :],
        in_grad[:, width : width + heads], mine[:4], mine[4], shared_sums[:4], shared_sums[4],
        mine[6, :heads], mine[6, heads : 2 * heads], mine[6, 2 * heads : 3 * heads], mine[5], both_grad[:, width:],
    )


def solution(mesh):
    count, planes = mesh.devices.shape
    assert planes == 4 and count % 4 == 0
    names = ("row", "side", "core", "tensor")
    inner = jax.sharding.Mesh(mesh.devices.reshape(count // 4, 2, 2, planes), names)
    dp = ("row", "side", "core")
    in_specs = (
        P(dp, None), P(dp, None), P(dp), P(dp, None), P(), P(dp, None, "tensor"), P(dp, None), P(dp, "tensor"),
        P(None, "tensor"), P("tensor"), P(), P(), P("tensor"), P("tensor"), P("tensor"), P("tensor"), P(dp, "tensor"),
    )
    out_specs = (
        P(dp, None), P(dp, None), P(), P(dp, None, "tensor"), P(dp, None), P(dp, "tensor"),
        P(None, "tensor"), P("tensor"), P(), P(), P("tensor"), P("tensor"), P("tensor"), P("tensor"), P(dp, "tensor"),
    )
    return jax.shard_map(on_device, mesh=inner, in_specs=in_specs, out_specs=out_specs, check_vma=False)
```

```python
import jax
import jax.numpy as jnp
from jax import lax
from jax.experimental import pallas as pl
from jax.experimental.pallas import tpu as pltpu
from jax.sharding import PartitionSpec as P

SPAN = 128
HALO = 8
LANES = 128
F32 = jnp.float32
BF16 = jnp.bfloat16
EPSILON = 1e-05


def mm(a, b):
    return jnp.dot(a, b, preferred_element_type=F32)


def mm_t(a, b):
    return lax.dot_general(a, b, (((1,), (1,)), ((), ())), preferred_element_type=F32)


def halves(v):
    high = v.astype(BF16)
    return high, (v - high.astype(F32)).astype(BF16)


def widen(v, spread):
    high, rest = halves(v)
    return mm(high, spread) + mm(rest, spread)


def head_sum(v, spread):
    high, rest = halves(v)
    return mm_t(high, spread) + mm_t(rest, spread)


def start_of(place, lens_ref):
    end, start = jnp.int32(0), jnp.zeros_like(place)
    for i in range(lens_ref.shape[0]):
        start = jnp.where(place >= end, end, start)
        end = end + lens_ref[i]
    return start


def taps(current, before, reach):
    whole = jnp.concatenate([before, current], axis=0)
    rows = current.shape[0]
    return [whole[HALO - k : HALO - k + rows] for k in range(reach)]


def filtered(shifted, allowed, kernel, bias):
    result = bias + kernel[0:1] * shifted[0]
    for k in range(1, len(shifted)):
        result = result + kernel[k : k + 1] * shifted[k] * allowed[k]
    return result


def permitted(place, start, reach, width):
    flags = [None]
    for k in range(1, reach):
        flags.append(jnp.where(place - k >= start, 1.0, 0.0)[:, :1])
    return flags


def softplus(v):
    return jnp.maximum(v, 0.0) + jnp.log1p(jnp.exp(-jnp.abs(v)))


def chunk_setup(base, lens_ref, span):
    place = base + lax.broadcasted_iota(jnp.int32, (span, LANES), 0)
    start = start_of(place, lens_ref)
    last_start = start_of(jnp.full((1, LANES), base + span - 1, jnp.int32), lens_ref)
    return place, start, last_start


def stacked(pair, low_lanes):
    zero = jnp.zeros_like(pair)
    return jnp.concatenate([jnp.where(low_lanes, pair, zero), jnp.where(low_lanes, zero, pair)], axis=0)


def forward_kernel(
    lens_ref, order_ref, proj_ref, fw_ref, fb_ref, sf_ref, sb_ref, head_ref, skip_ref, spread_ref,
    out_ref, kept_ref, memory, before, shared_before,
):
    step = pl.program_id(0)
    span = proj_ref.shape[0]
    width = out_ref.shape[1]
    reach = fw_ref.shape[0]
    pairs = width // LANES
    base = step * span

    @pl.when(step == 0)
    def _():
        memory[...] = jnp.zeros_like(memory)
        before[...] = jnp.zeros_like(before)
        shared_before[...] = jnp.zeros_like(shared_before)

    place, start, last_start = chunk_setup(base, lens_ref, span)
    allowed = permitted(place, start, reach, width)
    inputs = proj_ref[:, :width]
    shared = proj_ref[:, width + LANES :]
    conv = filtered(taps(inputs, before[...], reach), allowed, fw_ref, fb_ref[...])
    values = conv * jax.nn.sigmoid(conv)
    conv = filtered(taps(shared, shared_before[...], reach), allowed, sf_ref, sb_ref[...])
    factors = conv * jax.nn.sigmoid(conv)
    before[...] = inputs[span - HALO :]
    shared_before[...] = shared[span - HALO :]
    writes = factors[:, :LANES].astype(BF16)
    reads = factors[:, LANES:].astype(BF16)
    size = softplus(proj_ref[:, width : width + LANES] + head_ref[0:1])
    decay = -size * head_ref[1:2]
    row = lax.broadcasted_iota(jnp.int32, (span, span), 0)
    col = lax.broadcasted_iota(jnp.int32, (span, span), 1)
    lower = jnp.where(row >= col, 1.0, 0.0)
    total = jnp.dot(lower, decay, precision=lax.Precision.HIGHEST, preferred_element_type=F32)
    total_t = total.T
    inside = (col <= row) & (col + base >= start)
    scores = jnp.where(inside, mm_t(reads, writes), 0.0)
    spread = spread_ref[...]
    scaled = values * widen(size, spread)
    scaled_low = scaled.astype(BF16)
    entering = jnp.exp(total) * jnp.where(start < base, 1.0, 0.0)
    state = memory[...]
    state_low = state.astype(BF16)
    kept_ref[0] = state_low
    remote = mm(reads, state_low) * widen(entering, spread) + skip_ref[...] * values
    low_lanes = lax.broadcasted_iota(jnp.int32, (span, LANES), 1) < LANES // 2
    for pair in range(pairs):
        lanes = slice(pair * LANES, (pair + 1) * LANES)
        mixing = []
        for head in (2 * pair, 2 * pair + 1):
            fade = jnp.exp(jnp.minimum(total[:, head : head + 1] - total_t[head : head + 1, :], 0.0))
            mixing.append((scores * fade).astype(BF16))
        local = mm(jnp.concatenate(mixing, axis=1), stacked(scaled_low[:, lanes], low_lanes))
        out_ref[:, lanes] = (local + remote[:, lanes]).astype(out_ref.dtype)
    end = total[span - 1 : span]
    closing = jnp.exp(end - total) * jnp.where(place >= last_start, 1.0, 0.0)
    added = mm(writes.T, (scaled * widen(closing, spread)).astype(BF16))
    keeping = jnp.exp(end) * jnp.where(last_start < base, 1.0, 0.0)
    memory[...] = state * widen(jnp.broadcast_to(keeping, (8, LANES)), spread)[0:1] + added


def backward_kernel(
    lens_ref, order_ref, proj_ref, proj_before_ref, grad_ref, out_ref, kept_ref,
    fw_ref, fb_ref, sf_ref, sb_ref, head_ref, skip_ref, spread_ref,
    proj_grad_ref, shared_grad_ref, fsum_ref, ssum_ref, hsum_ref,
    memory_grad, after, shared_after,
):
    step = pl.program_id(0)
    steps = pl.num_programs(0)
    span = proj_ref.shape[0]
    width = out_ref.shape[1]
    reach = fw_ref.shape[0]
    pairs = width // LANES
    chunk = steps - 1 - step
    base = chunk * span

    @pl.when(step == 0)
    def _():
        memory_grad[...] = jnp.zeros_like(memory_grad)
        after[...] = jnp.zeros_like(after)
        shared_after[...] = jnp.zeros_like(shared_after)
        fsum_ref[...] = jnp.zeros_like(fsum_ref)
        ssum_ref[...] = jnp.zeros_like(ssum_ref)
        hsum_ref[...] = jnp.zeros_like(hsum_ref)

    place, start, last_start = chunk_setup(base, lens_ref, span)
    allowed = permitted(place, start, reach, width)
    first = jnp.where(chunk > 0, 1.0, 0.0)
    inputs = proj_ref[:, :width]
    shifted = taps(inputs, proj_before_ref[:, :width] * first, reach)
    conv = filtered(shifted, allowed, fw_ref, fb_ref[...])
    gate = jax.nn.sigmoid(conv)
    values = conv * gate
    slope = gate * (1.0 + conv * (1.0 - gate))
    shared_shifted = taps(proj_ref[:, width + LANES :], proj_before_ref[:, width + LANES :] * first, reach)
    conv = filtered(shared_shifted, allowed, sf_ref, sb_ref[...])
    gate = jax.nn.sigmoid(conv)
    factors = conv * gate
    shared_slope = gate * (1.0 + conv * (1.0 - gate))
    writes = factors[:, :LANES].astype(BF16)
    reads = factors[:, LANES:].astype(BF16)
    raw = proj_ref[:, width : width + LANES] + head_ref[0:1]
    size = softplus(raw)
    decay = -size * head_ref[1:2]
    row = lax.broadcasted_iota(jnp.int32, (span, span), 0)
    col = lax.broadcasted_iota(jnp.int32, (span, span), 1)
    lower = jnp.where(row >= col, 1.0, 0.0)
    upper = jnp.where(row <= col, 1.0, 0.0)
    total = jnp.dot(lower, decay, precision=lax.Precision.HIGHEST, preferred_element_type=F32)
    total_t = total.T
    start_t = start_of(base + col[0:1], lens_ref)
    inside_t = (row <= col) & (row + base >= start_t)
    scores_t = jnp.where(inside_t, mm_t(writes, reads), 0.0)
    spread = spread_ref[...]
    size_wide = widen(size, spread)
    scaled = values * size_wide
    scaled_low = scaled.astype(BF16)
    grad = grad_ref[...].astype(F32)
    grad_low = grad.astype(BF16)
    state_low = kept_ref[0]
    later = memory_grad[...]
    later_low = later.astype(BF16)
    entering = jnp.exp(total) * jnp.where(start < base, 1.0, 0.0)
    entered = (grad * widen(entering, spread)).astype(BF16)
    end = total[span - 1 : span]
    closing = jnp.exp(end - total) * jnp.where(place >= last_start, 1.0, 0.0)
    closing_wide = widen(closing, spread)
    keeping = jnp.exp(end) * jnp.where(last_start < base, 1.0, 0.0)
    keeping_wide = widen(jnp.broadcast_to(keeping, (8, LANES)), spread)[0:1]
    closed = mm(writes, later_low) * closing_wide
    low_lanes = lax.broadcasted_iota(jnp.int32, (span, LANES), 1) < LANES // 2
    scores_grad_t = jnp.zeros((span, span), F32)
    local = []
    for pair in range(pairs):
        lanes = slice(pair * LANES, (pair + 1) * LANES)
        halved = stacked(grad_low[:, lanes], low_lanes)
        mixing_grad = mm_t(scaled_low[:, lanes], halved)
        mixing = []
        for which, head in enumerate((2 * pair, 2 * pair + 1)):
            fade = jnp.exp(jnp.minimum(total_t[head : head + 1, :] - total[:, head : head + 1], 0.0))
            mixing.append((scores_t * fade).astype(BF16))
            scores_grad_t = scores_grad_t + mixing_grad[:, which * span : (which + 1) * span] * fade
        local.append(mm(jnp.concatenate(mixing, axis=1), halved))
    scaled_grad = jnp.concatenate(local, axis=1) + closed
    scores_grad_t = jnp.where(inside_t, scores_grad_t, 0.0).astype(BF16)
    kept_closing = (scaled * closing_wide).astype(BF16)
    reads_grad = mm(scores_grad_t.T, writes) + mm_t(entered, state_low)
    writes_grad = mm(scores_grad_t, reads) + mm_t(kept_closing, later_low)
    memory_grad[...] = later * keeping_wide + mm(reads.T, entered)
    skip = skip_ref[...]
    size_grad = head_sum(values * scaled_grad, spread)
    paid = head_sum(
        grad_low.astype(F32) * (out_ref[...] - skip * values) - scaled_low.astype(F32) * scaled_grad, spread
    )
    tail = jnp.sum(scaled_low.astype(F32) * closed, axis=0, keepdims=True) + keeping_wide * jnp.sum(
        later * state_low.astype(F32), axis=0, keepdims=True
    )
    tail = head_sum(jnp.broadcast_to(tail, (8, width)), spread)[0:1]
    total_grad = paid + jnp.where(place == base + span - 1, tail, 0.0)
    decay_grad = jnp.dot(upper, total_grad, precision=lax.Precision.HIGHEST, preferred_element_type=F32)
    raw_grad = (size_grad - decay_grad * head_ref[1:2]) * jax.nn.sigmoid(raw)
    proj_grad_ref[:, width:] = raw_grad.astype(proj_grad_ref.dtype)
    hsum_ref[0:1] += jnp.sum(raw_grad, axis=0, keepdims=True)
    hsum_ref[1:2] += jnp.sum(decay_grad * decay, axis=0, keepdims=True)
    conv_grad = (size_wide * scaled_grad + skip * grad) * slope
    shared_conv_grad = jnp.concatenate([writes_grad, reads_grad], axis=1) * shared_slope
    fsum_ref[reach : reach + 1] += jnp.sum(conv_grad, axis=0, keepdims=True)
    fsum_ref[reach + 1 : reach + 2] += jnp.sum(grad * values, axis=0, keepdims=True)
    ssum_ref[reach : reach + 1] += jnp.sum(shared_conv_grad, axis=0, keepdims=True)
    late = base + lax.broadcasted_iota(jnp.int32, (span + HALO, LANES), 0)
    late_allowed = permitted(late, start_of(late, lens_ref), reach, width)
    whole = jnp.concatenate([conv_grad, after[...]], axis=0)
    shared_whole = jnp.concatenate([shared_conv_grad, shared_after[...]], axis=0)
    result = fw_ref[0:1] * conv_grad
    shared_result = sf_ref[0:1] * shared_conv_grad
    fsum_ref[0:1] += jnp.sum(conv_grad * shifted[0], axis=0, keepdims=True)
    ssum_ref[0:1] += jnp.sum(shared_conv_grad * shared_shifted[0], axis=0, keepdims=True)
    for k in range(1, reach):
        masked = whole * late_allowed[k]
        fsum_ref[k : k + 1] += jnp.sum(masked[:span] * shifted[k], axis=0, keepdims=True)
        result = result + fw_ref[k : k + 1] * masked[k : k + span]
        masked = shared_whole * late_allowed[k]
        ssum_ref[k : k + 1] += jnp.sum(masked[:span] * shared_shifted[k], axis=0, keepdims=True)
        shared_result = shared_result + sf_ref[k : k + 1] * masked[k : k + span]
    after[...] = conv_grad[:HALO]
    shared_after[...] = shared_conv_grad[:HALO]
    proj_grad_ref[:, :width] = result.astype(proj_grad_ref.dtype)
    shared_grad_ref[...] = shared_result.astype(shared_grad_ref.dtype)


def head_rows(step_bias, decay_log, skip_gain, width):
    heads = step_bias.shape[0]
    table = jnp.zeros((8, LANES), F32)
    table = table.at[0, :heads].set(step_bias).at[1, :heads].set(jnp.exp(decay_log))
    skip = jnp.repeat(skip_gain, width // heads)[None, :]
    spread = (jnp.arange(LANES)[:, None] == (jnp.arange(width) // (width // heads))[None, :]).astype(BF16)
    return table, skip, spread


def fixed(shape):
    return pl.BlockSpec(shape, lambda *_: (0,) * len(shape))


def mixer_forward(lens, order, proj, fw, fb, sf, sb, table, skip, spread):
    rows = proj.shape[0]
    width = fw.shape[1]
    steps = rows // SPAN
    block = lambda cols: pl.BlockSpec((SPAN, cols), lambda i, lens_ref, order_ref: (order_ref[i], 0))
    return pl.pallas_call(
        forward_kernel,
        grid_spec=pltpu.PrefetchScalarGridSpec(
            num_scalar_prefetch=2,
            grid=(steps,),
            in_specs=[
                block(proj.shape[1]), fixed(fw.shape), fixed(fb.shape), fixed(sf.shape),
                fixed(sb.shape), fixed(table.shape), fixed(skip.shape), fixed(spread.shape),
            ],
            out_specs=[block(width), pl.BlockSpec((1, LANES, width), lambda i, *_: (i, 0, 0))],
            scratch_shapes=[
                pltpu.VMEM((LANES, width), F32),
                pltpu.VMEM((HALO, width), F32),
                pltpu.VMEM((HALO, sf.shape[1]), F32),
            ],
        ),
        out_shape=[
            jax.ShapeDtypeStruct((rows, width), F32),
            jax.ShapeDtypeStruct((steps, LANES, width), BF16),
        ],
        cost_estimate=pl.CostEstimate(flops=20 * 10**9, bytes_accessed=30 * 10**6, transcendentals=0),
        name="mixer_forward",
    )(lens, order, proj, fw, fb, sf, sb, table, skip, spread)


def mixer_backward(lens, order, proj, grad, out, kept, fw, fb, sf, sb, table, skip, spread):
    rows = proj.shape[0]
    width = fw.shape[1]
    steps = rows // SPAN
    lead = SPAN // HALO
    block = lambda cols: pl.BlockSpec((SPAN, cols), lambda i, lens_ref, order_ref: (order_ref[steps - 1 - i], 0))
    ahead = lambda cols: pl.BlockSpec(
        (HALO, cols),
        lambda i, lens_ref, order_ref: (order_ref[jnp.maximum(steps - 2 - i, 0)] * lead + lead - 1, 0),
    )
    return pl.pallas_call(
        backward_kernel,
        grid_spec=pltpu.PrefetchScalarGridSpec(
            num_scalar_prefetch=2,
            grid=(steps,),
            in_specs=[
                block(proj.shape[1]), ahead(proj.shape[1]),
                block(width), block(width), pl.BlockSpec((1, LANES, width), lambda i, *_: (steps - 1 - i, 0, 0)),
                fixed(fw.shape), fixed(fb.shape), fixed(sf.shape),
                fixed(sb.shape), fixed(table.shape), fixed(skip.shape), fixed(spread.shape),
            ],
            out_specs=[
                block(width + LANES), block(sf.shape[1]),
                fixed((8, width)), fixed((8, sf.shape[1])), fixed((8, LANES)),
            ],
            scratch_shapes=[
                pltpu.VMEM((LANES, width), F32),
                pltpu.VMEM((HALO, width), F32),
                pltpu.VMEM((HALO, sf.shape[1]), F32),
            ],
        ),
        out_shape=[
            jax.ShapeDtypeStruct((rows, width + LANES), BF16),
            jax.ShapeDtypeStruct((rows, sf.shape[1]), F32),
            jax.ShapeDtypeStruct((8, width), F32),
            jax.ShapeDtypeStruct((8, sf.shape[1]), F32),
            jax.ShapeDtypeStruct((8, LANES), F32),
        ],
        cost_estimate=pl.CostEstimate(flops=40 * 10**9, bytes_accessed=60 * 10**6, transcendentals=0),
        name="mixer_backward",
    )(lens, order, proj, proj, grad, out, kept, fw, fb, sf, sb, table, skip, spread)


def swap(v, axis, mask=1):
    count = lax.axis_size(axis)
    return lax.ppermute(v, axis, [(i, i ^ mask) for i in range(count)])


def crossed(v):
    pairs = [(a * 4 + b, b * 4 + a) for a in range(4) for b in range(4)]
    return lax.ppermute(v, ("side", "core", "tensor"), pairs)


def pick(stack, index, axis=0):
    return lax.dynamic_index_in_dim(stack, index, axis, keepdims=False)


def row_doubling(v):
    pieces = [v]
    while len(pieces) < lax.axis_size("row"):
        reach = len(pieces)
        pieces = pieces + [swap(p, "row", reach) for p in pieces]
    return pieces


SLOT_PLANES = ((0, 1, 2, 3), (1, 0, 2, 3), (2, 1, 3, 0), (3, 2, 1, 0))
PLANE_SLOTS = ((0, 1, 2, 3), (1, 0, 2, 3), (3, 1, 0, 2), (3, 2, 1, 0))


def line_step(pair, j):
    left, right = pair
    return (
        lax.ppermute(left, "tensor", [(i, i + 1) for i in range(j - 1, 3)]),
        lax.ppermute(right, "tensor", [(i + 1, i) for i in range(0, 4 - j)]),
    )


def slots_of(v, one, two, three):
    plane = lax.axis_index("tensor")
    return [
        v,
        jnp.where(plane == 0, one[1], one[0]),
        jnp.where(plane == 0, two[1], jnp.where(plane == 3, two[0], one[1])),
        jnp.where(plane == 0, three[1], jnp.where(plane == 1, two[1], jnp.where(plane == 2, two[0], three[0]))),
    ]


def summed(v, axes):
    for axis in axes:
        reach = 1
        while reach < lax.axis_size(axis):
            v = v + swap(v, axis, reach)
            reach = reach * 2
    return v


def contract_rows(a, b):
    return lax.dot_general(a, b, (((0,), (0,)), ((), ())), preferred_element_type=F32)


def contract_columns(a, b):
    return lax.dot_general(a, b, (((1,), (1,)), ((), ())), preferred_element_type=F32)


def on_device(
    tokens, cotangent, destination, lengths, norm_gain, inner_weight, shared_weight, step_weight, filter_weight,
    filter_bias, shared_filter, shared_filter_bias, step_bias, decay_log, skip_gain, gate_gain, out_weight,
):
    row_count, model_width = tokens.shape
    width = filter_weight.shape[1]
    heads = step_bias.shape[0]
    rows_n, planes = lax.axis_size("row"), lax.axis_size("tensor")
    row, side, core, plane = (lax.axis_index(a) for a in ("row", "side", "core", "tensor"))
    group_rows = row_count // (rows_n * 4)
    owned = rows_n * group_rows
    source = (row * 2 + side) * 2 + core

    wanted = jnp.concatenate(
        [
            ((row ^ d) * planes + plane) * row_count + source * group_rows + jnp.arange(group_rows, dtype=jnp.int32)
            for d in range(rows_n)
        ]
    )
    chosen = (wanted[:, None] == destination[None, :]).astype(BF16)

    def exchanged(sent):
        return jnp.concatenate([sent[:group_rows]] + [
            swap(sent[d * group_rows : (d + 1) * group_rows], "row", d) for d in range(1, rows_n)
        ])

    def gathered(own):
        beside = swap(own, "side")
        return jnp.concatenate([own, swap(own, "core"), beside, swap(beside, "core")])

    own_tokens = exchanged(jnp.dot(chosen, tokens, preferred_element_type=F32).astype(BF16))
    hidden = own_tokens.astype(F32)
    scale = lax.rsqrt(jnp.mean(hidden * hidden, axis=-1, keepdims=True) + EPSILON)
    normed = gathered((hidden * scale * norm_gain).astype(BF16))
    own_cot = exchanged(jnp.dot(chosen, cotangent, preferred_element_type=F32).astype(BF16))
    cot = gathered(own_cot)

    step_low = jnp.pad(step_weight.astype(BF16), ((0, 0), (0, LANES - heads)))
    piece = jnp.concatenate([inner_weight[:, 1].astype(BF16), step_low, shared_weight.astype(BF16)], axis=1)
    own_piece = crossed(piece)
    one = line_step((own_piece, own_piece), 1)
    two = line_step(one, 2)
    whole = jnp.stack([p for slot in slots_of(own_piece, one, two, line_step(two, 3)) for p in row_doubling(slot)])
    slots = jnp.array(PLANE_SLOTS, jnp.int32)[plane]
    in_full = jnp.concatenate(
        [pick(whole, slots[q] * rows_n + (r ^ row)) for r in range(rows_n) for q in range(planes)], axis=0
    )
    piece = jnp.concatenate([inner_weight[:, 0].astype(BF16), out_weight.astype(BF16)], axis=1)
    both_full = lax.all_gather(crossed(piece), ("row", "tensor"), axis=0, tiled=True)
    gate_full, out_full = both_full[:, :width], both_full[:, width:]

    params = jnp.concatenate(
        [
            filter_weight,
            filter_bias[None],
            gate_gain[None],
            jnp.pad(jnp.concatenate([step_bias, decay_log, skip_gain]), (0, width - 3 * heads))[None],
            jnp.pad(lengths.astype(F32), ((0, 0), (0, width - lengths.shape[1]))),
        ],
        axis=0,
    )
    params = crossed(params)
    fw, fb, gain = params[:4], params[4:5], params[5:6]
    bias_here, decay_here, skip_here = (params[6, i * heads : (i + 1) * heads] for i in range(3))
    lens = params[7, : lengths.shape[1]].astype(jnp.int32)
    sf, sb = shared_filter, shared_filter_bias[None]
    table, skip, spread = head_rows(bias_here, decay_here, skip_here, width)

    if group_rows % SPAN == 0:
        spans = jnp.arange(row_count // SPAN, dtype=jnp.int32)
        part = (spans * SPAN // group_rows) ^ source
        order = (((part // 2) % 2 * 2 + part % 2) * rows_n + part // 4) * (group_rows // SPAN)
        order = order + spans % (group_rows // SPAN)
        sequenced = unsequenced = lambda v: v
    else:
        order = jnp.arange(row_count // SPAN, dtype=jnp.int32)
        groups = jnp.arange(4 * rows_n, dtype=jnp.int32)
        part = groups ^ source
        to = ((part // 2) % 2 * 2 + part % 2) * rows_n + part // 4
        fro = (((groups % rows_n) * 4 + groups // rows_n) ^ source)
        sequenced = lambda v: v.reshape(4 * rows_n, group_rows, -1)[to].reshape(v.shape)
        unsequenced = lambda v: v.reshape(4 * rows_n, group_rows, -1)[fro].reshape(v.shape)

    def summed_over_group(v):
        v = v + swap(v, "core").reshape(2, 2, 2, owned)[:, :, ::-1].reshape(2, -1)
        return v + swap(v, "side").reshape(2, 2, 2 * owned)[:, ::-1].reshape(2, -1)

    def rows_of(v, dx, dk):
        return v[(dx * 2 + dk) * owned : (dx * 2 + dk + 1) * owned]

    def group_parts(part):
        return part(1, 1).astype(BF16), part(1, 0), part(0, 1).astype(BF16), part(0, 0)

    def group_sum(parts):
        far, side_part, near, own_part = parts
        beside = swap((side_part + swap(far, "core").astype(F32)).astype(BF16), "side")
        return own_part + swap(near, "core").astype(F32) + beside.astype(F32)

    block_of = destination // row_count
    row_of, plane_of = (block_of // planes) ^ row, block_of % planes
    slot = row_of * group_rows + destination - block_of * row_count - source * group_rows
    slot_planes = jnp.array(SLOT_PLANES, jnp.int32)[plane]

    def returned(held):
        def settled(which):
            where = jnp.concatenate([jnp.where(plane_of == slot_planes[j], slot, -1)[:, None] == jnp.arange(owned)[None, :]
                                     for j in which], axis=1)
            return jnp.dot(where.astype(BF16), jnp.concatenate([held[j] for j in which]), preferred_element_type=F32)
        return settled((0, 1)).astype(BF16) + settled((2, 3)).astype(BF16)

    proj = sequenced(jnp.dot(normed, in_full, preferred_element_type=F32))
    mixed_seq, kept = mixer_forward(lens, order, proj, fw, fb, sf, sb, table, skip, spread)
    mixed = unsequenced(mixed_seq)
    gate_in = lax.optimization_barrier(jnp.dot(normed, gate_full, preferred_element_type=F32))
    normed_grad = lax.optimization_barrier(jnp.dot(cot, out_full, preferred_element_type=F32))
    gate_sig = jax.nn.sigmoid(gate_in)
    gate_act = gate_in * gate_sig
    gated = mixed * gate_act
    scaled_grad = normed_grad * gain
    sums = summed_over_group(jnp.stack([jnp.sum(gated * gated, axis=1), jnp.sum(scaled_grad * gated, axis=1)]))
    gate_scale = lax.rsqrt(sums[0] / (4 * width) + EPSILON)[:, None]
    gate_normed = (gated * gate_scale * gain).astype(BF16)
    far, side_part, near, own_part = group_parts(
        lambda dx, dk: contract_columns(rows_of(gate_normed, dx, dk), out_full)
    )
    sent = (side_part + swap(far, "core").astype(F32)).astype(BF16)
    own_rows = hidden + own_part + swap(near, "core").astype(F32)

    out_grad = contract_rows(cot, gate_normed).astype(BF16)
    gate_gain_grad = jnp.sum(normed_grad * gated * gate_scale, axis=0)
    gated_grad = gate_scale * scaled_grad - gated * gate_scale**3 * (sums[1] / (4 * width))[:, None]
    mixed_grad = gated_grad * gate_act
    gate_in_grad = (gated_grad * mixed * gate_sig * (1.0 + gate_in * (1.0 - gate_sig))).astype(BF16)
    gate_grad = contract_rows(normed, gate_in_grad).astype(BF16)
    both_grad = jnp.concatenate([gate_grad, out_grad], axis=1)
    mixed_grad, both_grad, sent, own_rows = lax.optimization_barrier((mixed_grad, both_grad, sent, own_rows))
    arrived = swap(sent, "side")
    both_grad = lax.psum_scatter(both_grad, ("row", "tensor"), scatter_dimension=0, tiled=True)
    proj_grad, shared_part, fsum, ssum, hsum = mixer_backward(
        lens, order, proj, sequenced(mixed_grad), mixed_seq, kept, fw, fb, sf, sb, table, skip, spread
    )
    proj_grad, shared_part = unsequenced(proj_grad), unsequenced(shared_part)
    proj_grad, shared_part, arrived = lax.optimization_barrier((proj_grad, shared_part, arrived))
    out_rows = exchanged((own_rows + arrived.astype(F32)).astype(BF16))

    def back_part(grads, dx, dk):
        gate_part, proj_part = grads
        return contract_columns(rows_of(gate_part, dx, dk), gate_full) + contract_columns(
            rows_of(proj_part, dx, dk), in_full[:, : width + LANES]
        )

    shared_far, shared_side, shared_near, shared_own = group_parts(lambda dx, dk: rows_of(shared_part, dx, dk))
    own_shared = group_sum((shared_far, shared_side, shared_near, shared_own)).astype(BF16)
    far = swap(back_part((gate_in_grad, proj_grad), 1, 1).astype(BF16), "core")
    near = swap(back_part((gate_in_grad, proj_grad), 0, 1).astype(BF16), "core")
    far, gate_later, proj_later, out_rows = lax.optimization_barrier((far, gate_in_grad, proj_grad, out_rows))
    out_one = line_step((out_rows, out_rows), 1)
    sent = (back_part((gate_later, proj_later), 1, 0) + far.astype(F32)).astype(BF16)
    own_back = back_part((gate_later, proj_later), 0, 0) + near.astype(F32)
    beside = swap(sent, "side")
    in_grad = contract_rows(normed, jnp.concatenate([proj_later, gathered(own_shared)], axis=1)).astype(BF16)
    in_grad, out_one, both_grad, own_back = lax.optimization_barrier((in_grad, out_one, both_grad, own_back))
    out_two = line_step(out_one, 2)
    both_grad = crossed(both_grad).astype(F32)
    in_grad = lax.psum_scatter(in_grad, ("row", "tensor"), scatter_dimension=0, tiled=True)
    normed_back = own_back + beside.astype(F32) + contract_columns(own_shared, in_full[:, width + LANES :])
    norm_gain_grad = jnp.sum(normed_back * hidden * scale, axis=0)
    gained = normed_back * norm_gain
    along = jnp.mean(gained * hidden, axis=1, keepdims=True)
    input_work = own_cot.astype(F32) + scale * gained - hidden * (scale**3 * along)
    back_rows = exchanged(input_work.astype(BF16))
    back_rows, out_two = lax.optimization_barrier((back_rows, out_two))
    layer_out = returned(slots_of(out_rows, out_one, out_two, line_step(out_two, 3)))
    back_one = line_step((back_rows, back_rows), 1)
    back_two = line_step(back_one, 2)
    back_two, in_grad = lax.optimization_barrier((back_two, in_grad))
    input_grad = returned(slots_of(back_rows, back_one, back_two, line_step(back_two, 3)))
    in_grad = crossed(in_grad).astype(F32)
    inner_grad = jnp.stack([both_grad[:, :width], in_grad[:, :width]], axis=1)

    line = lambda v: jnp.pad(v, (0, -v.shape[0] % width)).reshape(-1, width)
    skip_grad = fsum[5].reshape(heads, -1).sum(axis=1)
    small = jnp.concatenate(
        [
            fsum[:5],
            gate_gain_grad[None],
            jnp.pad(jnp.concatenate([hsum[0, :heads], hsum[1, :heads], skip_grad]), (0, width - 3 * heads))[None],
            jnp.zeros((1, width), F32),
            line(norm_gain_grad),
            line(ssum[:5].reshape(-1)),
        ],
        axis=0,
    )
    small = summed(small, ("row", "tensor"))
    mine = crossed(small[:8])
    common = summed(small[8:], ("core", "side"))
    lines = line(norm_gain_grad).shape[0]
    norm_gain_grad = common[:lines].reshape(-1)[:model_width]
    shared_sums = common[lines:].reshape(-1)[: 5 * sf.shape[1]].reshape(5, -1)
    return (
        layer_out, input_grad, norm_gain_grad, inner_grad, in_grad[:, width + LANES :],
        in_grad[:, width : width + heads], mine[:4], mine[4], shared_sums[:4], shared_sums[4],
        mine[6, :heads], mine[6, heads : 2 * heads], mine[6, 2 * heads : 3 * heads], mine[5], both_grad[:, width:],
    )


def solution(mesh):
    count, planes = mesh.devices.shape
    assert planes == 4 and count % 4 == 0
    names = ("row", "side", "core", "tensor")
    inner = jax.sharding.Mesh(mesh.devices.reshape(count // 4, 2, 2, planes), names)
    dp = ("row", "side", "core")
    in_specs = (
        P(dp, None), P(dp, None), P(dp), P(dp, None), P(), P(dp, None, "tensor"), P(dp, None), P(dp, "tensor"),
        P(None, "tensor"), P("tensor"), P(), P(), P("tensor"), P("tensor"), P("tensor"), P("tensor"), P(dp, "tensor"),
    )
    out_specs = (
        P(dp, None), P(dp, None), P(), P(dp, None, "tensor"), P(dp, None), P(dp, "tensor"),
        P(None, "tensor"), P("tensor"), P(), P(), P("tensor"), P("tensor"), P("tensor"), P("tensor"), P(dp, "tensor"),
    )
    return jax.shard_map(on_device, mesh=inner, in_specs=in_specs, out_specs=out_specs, check_vma=False)
```

```python
import jax
import jax.numpy as jnp
from jax import lax
from jax.experimental import pallas as pl
from jax.experimental.pallas import tpu as pltpu
from jax.sharding import PartitionSpec as P

SPAN = 128
HALO = 8
LANES = 128
F32 = jnp.float32
BF16 = jnp.bfloat16
EPSILON = 1e-05


def mm(a, b):
    return jnp.dot(a, b, preferred_element_type=F32)


def mm_t(a, b):
    return lax.dot_general(a, b, (((1,), (1,)), ((), ())), preferred_element_type=F32)


def halves(v):
    high = v.astype(BF16)
    return high, (v - high.astype(F32)).astype(BF16)


def widen(v, spread):
    high, rest = halves(v)
    return mm(high, spread) + mm(rest, spread)


def head_sum(v, spread):
    high, rest = halves(v)
    return mm_t(high, spread) + mm_t(rest, spread)


def start_of(place, lens_ref):
    end, start = jnp.int32(0), jnp.zeros_like(place)
    for i in range(lens_ref.shape[0]):
        start = jnp.where(place >= end, end, start)
        end = end + lens_ref[i]
    return start


def taps(current, before, reach):
    whole = jnp.concatenate([before, current], axis=0)
    rows = current.shape[0]
    return [whole[HALO - k : HALO - k + rows] for k in range(reach)]


def filtered(shifted, allowed, kernel, bias):
    result = bias + kernel[0:1] * shifted[0]
    for k in range(1, len(shifted)):
        result = result + kernel[k : k + 1] * shifted[k] * allowed[k]
    return result


def permitted(place, start, reach, width):
    flags = [None]
    for k in range(1, reach):
        flags.append(jnp.where(place - k >= start, 1.0, 0.0)[:, :1])
    return flags


def softplus(v):
    return jnp.maximum(v, 0.0) + jnp.log1p(jnp.exp(-jnp.abs(v)))


def chunk_setup(base, lens_ref, span):
    place = base + lax.broadcasted_iota(jnp.int32, (span, LANES), 0)
    start = start_of(place, lens_ref)
    last_start = start_of(jnp.full((1, LANES), base + span - 1, jnp.int32), lens_ref)
    return place, start, last_start


def stacked(pair, low_lanes):
    zero = jnp.zeros_like(pair)
    return jnp.concatenate([jnp.where(low_lanes, pair, zero), jnp.where(low_lanes, zero, pair)], axis=0)


def forward_kernel(
    lens_ref, order_ref, proj_ref, fw_ref, fb_ref, sf_ref, sb_ref, head_ref, skip_ref, spread_ref,
    out_ref, kept_ref, memory, before, shared_before,
):
    step = pl.program_id(0)
    span = proj_ref.shape[0]
    width = out_ref.shape[1]
    reach = fw_ref.shape[0]
    pairs = width // LANES
    base = step * span

    @pl.when(step == 0)
    def _():
        memory[...] = jnp.zeros_like(memory)
        before[...] = jnp.zeros_like(before)
        shared_before[...] = jnp.zeros_like(shared_before)

    place, start, last_start = chunk_setup(base, lens_ref, span)
    allowed = permitted(place, start, reach, width)
    inputs = proj_ref[:, :width]
    shared = proj_ref[:, width + LANES :]
    conv = filtered(taps(inputs, before[...], reach), allowed, fw_ref, fb_ref[...])
    values = conv * jax.nn.sigmoid(conv)
    conv = filtered(taps(shared, shared_before[...], reach), allowed, sf_ref, sb_ref[...])
    factors = conv * jax.nn.sigmoid(conv)
    before[...] = inputs[span - HALO :]
    shared_before[...] = shared[span - HALO :]
    writes = factors[:, :LANES].astype(BF16)
    reads = factors[:, LANES:].astype(BF16)
    size = softplus(proj_ref[:, width : width + LANES] + head_ref[0:1])
    decay = -size * head_ref[1:2]
    row = lax.broadcasted_iota(jnp.int32, (span, span), 0)
    col = lax.broadcasted_iota(jnp.int32, (span, span), 1)
    lower = jnp.where(row >= col, 1.0, 0.0)
    total = jnp.dot(lower, decay, precision=lax.Precision.HIGHEST, preferred_element_type=F32)
    total_t = total.T
    inside = (col <= row) & (col + base >= start)
    scores = jnp.where(inside, mm_t(reads, writes), 0.0)
    spread = spread_ref[...]
    scaled = values * widen(size, spread)
    scaled_low = scaled.astype(BF16)
    entering = jnp.exp(total) * jnp.where(start < base, 1.0, 0.0)
    state = memory[...]
    state_low = state.astype(BF16)
    kept_ref[0] = state_low
    remote = mm(reads, state_low) * widen(entering, spread) + skip_ref[...] * values
    low_lanes = lax.broadcasted_iota(jnp.int32, (span, LANES), 1) < LANES // 2
    for pair in range(pairs):
        lanes = slice(pair * LANES, (pair + 1) * LANES)
        mixing = []
        for head in (2 * pair, 2 * pair + 1):
            fade = jnp.exp(jnp.minimum(total[:, head : head + 1] - total_t[head : head + 1, :], 0.0))
            mixing.append((scores * fade).astype(BF16))
        local = mm(jnp.concatenate(mixing, axis=1), stacked(scaled_low[:, lanes], low_lanes))
        out_ref[:, lanes] = (local + remote[:, lanes]).astype(out_ref.dtype)
    end = total[span - 1 : span]
    closing = jnp.exp(end - total) * jnp.where(place >= last_start, 1.0, 0.0)
    added = mm(writes.T, (scaled * widen(closing, spread)).astype(BF16))
    keeping = jnp.exp(end) * jnp.where(last_start < base, 1.0, 0.0)
    memory[...] = state * widen(jnp.broadcast_to(keeping, (8, LANES)), spread)[0:1] + added


def backward_kernel(
    lens_ref, order_ref, proj_ref, proj_before_ref, grad_ref, out_ref, kept_ref,
    fw_ref, fb_ref, sf_ref, sb_ref, head_ref, skip_ref, spread_ref,
    proj_grad_ref, shared_grad_ref, fsum_ref, ssum_ref, hsum_ref,
    memory_grad, after, shared_after,
):
    step = pl.program_id(0)
    steps = pl.num_programs(0)
    span = proj_ref.shape[0]
    width = out_ref.shape[1]
    reach = fw_ref.shape[0]
    pairs = width // LANES
    chunk = steps - 1 - step
    base = chunk * span

    @pl.when(step == 0)
    def _():
        memory_grad[...] = jnp.zeros_like(memory_grad)
        after[...] = jnp.zeros_like(after)
        shared_after[...] = jnp.zeros_like(shared_after)
        fsum_ref[...] = jnp.zeros_like(fsum_ref)
        ssum_ref[...] = jnp.zeros_like(ssum_ref)
        hsum_ref[...] = jnp.zeros_like(hsum_ref)

    place, start, last_start = chunk_setup(base, lens_ref, span)
    allowed = permitted(place, start, reach, width)
    first = jnp.where(chunk > 0, 1.0, 0.0)
    inputs = proj_ref[:, :width]
    shifted = taps(inputs, proj_before_ref[:, :width] * first, reach)
    conv = filtered(shifted, allowed, fw_ref, fb_ref[...])
    gate = jax.nn.sigmoid(conv)
    values = conv * gate
    slope = gate * (1.0 + conv * (1.0 - gate))
    shared_shifted = taps(proj_ref[:, width + LANES :], proj_before_ref[:, width + LANES :] * first, reach)
    conv = filtered(shared_shifted, allowed, sf_ref, sb_ref[...])
    gate = jax.nn.sigmoid(conv)
    factors = conv * gate
    shared_slope = gate * (1.0 + conv * (1.0 - gate))
    writes = factors[:, :LANES].astype(BF16)
    reads = factors[:, LANES:].astype(BF16)
    raw = proj_ref[:, width : width + LANES] + head_ref[0:1]
    size = softplus(raw)
    decay = -size * head_ref[1:2]
    row = lax.broadcasted_iota(jnp.int32, (span, span), 0)
    col = lax.broadcasted_iota(jnp.int32, (span, span), 1)
    lower = jnp.where(row >= col, 1.0, 0.0)
    upper = jnp.where(row <= col, 1.0, 0.0)
    total = jnp.dot(lower, decay, precision=lax.Precision.HIGHEST, preferred_element_type=F32)
    total_t = total.T
    start_t = start_of(base + col[0:1], lens_ref)
    inside_t = (row <= col) & (row + base >= start_t)
    scores_t = jnp.where(inside_t, mm_t(writes, reads), 0.0)
    spread = spread_ref[...]
    size_wide = widen(size, spread)
    scaled = values * size_wide
    scaled_low = scaled.astype(BF16)
    grad = grad_ref[...].astype(F32)
    grad_low = grad.astype(BF16)
    state_low = kept_ref[0]
    later = memory_grad[...]
    later_low = later.astype(BF16)
    entering = jnp.exp(total) * jnp.where(start < base, 1.0, 0.0)
    entered = (grad * widen(entering, spread)).astype(BF16)
    end = total[span - 1 : span]
    closing = jnp.exp(end - total) * jnp.where(place >= last_start, 1.0, 0.0)
    closing_wide = widen(closing, spread)
    keeping = jnp.exp(end) * jnp.where(last_start < base, 1.0, 0.0)
    keeping_wide = widen(jnp.broadcast_to(keeping, (8, LANES)), spread)[0:1]
    closed = mm(writes, later_low) * closing_wide
    low_lanes = lax.broadcasted_iota(jnp.int32, (span, LANES), 1) < LANES // 2
    scores_grad_t = jnp.zeros((span, span), F32)
    local = []
    for pair in range(pairs):
        lanes = slice(pair * LANES, (pair + 1) * LANES)
        halved = stacked(grad_low[:, lanes], low_lanes)
        mixing_grad = mm_t(scaled_low[:, lanes], halved)
        mixing = []
        for which, head in enumerate((2 * pair, 2 * pair + 1)):
            fade = jnp.exp(jnp.minimum(total_t[head : head + 1, :] - total[:, head : head + 1], 0.0))
            mixing.append((scores_t * fade).astype(BF16))
            scores_grad_t = scores_grad_t + mixing_grad[:, which * span : (which + 1) * span] * fade
        local.append(mm(jnp.concatenate(mixing, axis=1), halved))
    scaled_grad = jnp.concatenate(local, axis=1) + closed
    scores_grad_t = jnp.where(inside_t, scores_grad_t, 0.0).astype(BF16)
    kept_closing = (scaled * closing_wide).astype(BF16)
    reads_grad = mm(scores_grad_t.T, writes) + mm_t(entered, state_low)
    writes_grad = mm(scores_grad_t, reads) + mm_t(kept_closing, later_low)
    memory_grad[...] = later * keeping_wide + mm(reads.T, entered)
    skip = skip_ref[...]
    size_grad = head_sum(values * scaled_grad, spread)
    paid = head_sum(
        grad_low.astype(F32) * (out_ref[...] - skip * values) - scaled_low.astype(F32) * scaled_grad, spread
    )
    tail = jnp.sum(scaled_low.astype(F32) * closed, axis=0, keepdims=True) + keeping_wide * jnp.sum(
        later * state_low.astype(F32), axis=0, keepdims=True
    )
    tail = head_sum(jnp.broadcast_to(tail, (8, width)), spread)[0:1]
    total_grad = paid + jnp.where(place == base + span - 1, tail, 0.0)
    decay_grad = jnp.dot(upper, total_grad, precision=lax.Precision.HIGHEST, preferred_element_type=F32)
    raw_grad = (size_grad - decay_grad * head_ref[1:2]) * jax.nn.sigmoid(raw)
    proj_grad_ref[:, width:] = raw_grad.astype(proj_grad_ref.dtype)
    hsum_ref[0:1] += jnp.sum(raw_grad, axis=0, keepdims=True)
    hsum_ref[1:2] += jnp.sum(decay_grad * decay, axis=0, keepdims=True)
    conv_grad = (size_wide * scaled_grad + skip * grad) * slope
    shared_conv_grad = jnp.concatenate([writes_grad, reads_grad], axis=1) * shared_slope
    fsum_ref[reach : reach + 1] += jnp.sum(conv_grad, axis=0, keepdims=True)
    fsum_ref[reach + 1 : reach + 2] += jnp.sum(grad * values, axis=0, keepdims=True)
    ssum_ref[reach : reach + 1] += jnp.sum(shared_conv_grad, axis=0, keepdims=True)
    late = base + lax.broadcasted_iota(jnp.int32, (span + HALO, LANES), 0)
    late_allowed = permitted(late, start_of(late, lens_ref), reach, width)
    whole = jnp.concatenate([conv_grad, after[...]], axis=0)
    shared_whole = jnp.concatenate([shared_conv_grad, shared_after[...]], axis=0)
    result = fw_ref[0:1] * conv_grad
    shared_result = sf_ref[0:1] * shared_conv_grad
    fsum_ref[0:1] += jnp.sum(conv_grad * shifted[0], axis=0, keepdims=True)
    ssum_ref[0:1] += jnp.sum(shared_conv_grad * shared_shifted[0], axis=0, keepdims=True)
    for k in range(1, reach):
        masked = whole * late_allowed[k]
        fsum_ref[k : k + 1] += jnp.sum(masked[:span] * shifted[k], axis=0, keepdims=True)
        result = result + fw_ref[k : k + 1] * masked[k : k + span]
        masked = shared_whole * late_allowed[k]
        ssum_ref[k : k + 1] += jnp.sum(masked[:span] * shared_shifted[k], axis=0, keepdims=True)
        shared_result = shared_result + sf_ref[k : k + 1] * masked[k : k + span]
    after[...] = conv_grad[:HALO]
    shared_after[...] = shared_conv_grad[:HALO]
    proj_grad_ref[:, :width] = result.astype(proj_grad_ref.dtype)
    shared_grad_ref[...] = shared_result.astype(shared_grad_ref.dtype)


def head_rows(step_bias, decay_log, skip_gain, width):
    heads = step_bias.shape[0]
    table = jnp.zeros((8, LANES), F32)
    table = table.at[0, :heads].set(step_bias).at[1, :heads].set(jnp.exp(decay_log))
    skip = jnp.repeat(skip_gain, width // heads)[None, :]
    spread = (jnp.arange(LANES)[:, None] == (jnp.arange(width) // (width // heads))[None, :]).astype(BF16)
    return table, skip, spread


def fixed(shape):
    return pl.BlockSpec(shape, lambda *_: (0,) * len(shape))


def mixer_forward(lens, order, proj, fw, fb, sf, sb, table, skip, spread):
    rows = proj.shape[0]
    width = fw.shape[1]
    steps = rows // SPAN
    block = lambda cols: pl.BlockSpec((SPAN, cols), lambda i, lens_ref, order_ref: (order_ref[i], 0))
    return pl.pallas_call(
        forward_kernel,
        grid_spec=pltpu.PrefetchScalarGridSpec(
            num_scalar_prefetch=2,
            grid=(steps,),
            in_specs=[
                block(proj.shape[1]), fixed(fw.shape), fixed(fb.shape), fixed(sf.shape),
                fixed(sb.shape), fixed(table.shape), fixed(skip.shape), fixed(spread.shape),
            ],
            out_specs=[block(width), pl.BlockSpec((1, LANES, width), lambda i, *_: (i, 0, 0))],
            scratch_shapes=[
                pltpu.VMEM((LANES, width), F32),
                pltpu.VMEM((HALO, width), F32),
                pltpu.VMEM((HALO, sf.shape[1]), F32),
            ],
        ),
        out_shape=[
            jax.ShapeDtypeStruct((rows, width), F32),
            jax.ShapeDtypeStruct((steps, LANES, width), BF16),
        ],
        cost_estimate=pl.CostEstimate(flops=20 * 10**9, bytes_accessed=30 * 10**6, transcendentals=0),
        name="mixer_forward",
    )(lens, order, proj, fw, fb, sf, sb, table, skip, spread)


def mixer_backward(lens, order, proj, grad, out, kept, fw, fb, sf, sb, table, skip, spread):
    rows = proj.shape[0]
    width = fw.shape[1]
    steps = rows // SPAN
    lead = SPAN // HALO
    block = lambda cols: pl.BlockSpec((SPAN, cols), lambda i, lens_ref, order_ref: (order_ref[steps - 1 - i], 0))
    ahead = lambda cols: pl.BlockSpec(
        (HALO, cols),
        lambda i, lens_ref, order_ref: (order_ref[jnp.maximum(steps - 2 - i, 0)] * lead + lead - 1, 0),
    )
    return pl.pallas_call(
        backward_kernel,
        grid_spec=pltpu.PrefetchScalarGridSpec(
            num_scalar_prefetch=2,
            grid=(steps,),
            in_specs=[
                block(proj.shape[1]), ahead(proj.shape[1]),
                block(width), block(width), pl.BlockSpec((1, LANES, width), lambda i, *_: (steps - 1 - i, 0, 0)),
                fixed(fw.shape), fixed(fb.shape), fixed(sf.shape),
                fixed(sb.shape), fixed(table.shape), fixed(skip.shape), fixed(spread.shape),
            ],
            out_specs=[
                block(width + LANES), block(sf.shape[1]),
                fixed((8, width)), fixed((8, sf.shape[1])), fixed((8, LANES)),
            ],
            scratch_shapes=[
                pltpu.VMEM((LANES, width), F32),
                pltpu.VMEM((HALO, width), F32),
                pltpu.VMEM((HALO, sf.shape[1]), F32),
            ],
        ),
        out_shape=[
            jax.ShapeDtypeStruct((rows, width + LANES), BF16),
            jax.ShapeDtypeStruct((rows, sf.shape[1]), F32),
            jax.ShapeDtypeStruct((8, width), F32),
            jax.ShapeDtypeStruct((8, sf.shape[1]), F32),
            jax.ShapeDtypeStruct((8, LANES), F32),
        ],
        cost_estimate=pl.CostEstimate(flops=40 * 10**9, bytes_accessed=60 * 10**6, transcendentals=0),
        name="mixer_backward",
    )(lens, order, proj, proj, grad, out, kept, fw, fb, sf, sb, table, skip, spread)


def swap(v, axis, mask=1):
    count = lax.axis_size(axis)
    return lax.ppermute(v, axis, [(i, i ^ mask) for i in range(count)])


def crossed(v):
    pairs = [(a * 4 + b, b * 4 + a) for a in range(4) for b in range(4)]
    return lax.ppermute(v, ("side", "core", "tensor"), pairs)


def row_doubling(v):
    pieces = [v]
    while len(pieces) < lax.axis_size("row"):
        reach = len(pieces)
        pieces = pieces + [swap(p, "row", reach) for p in pieces]
    return pieces


SLOT_PLANES = ((0, 1, 2, 3), (1, 0, 2, 3), (2, 1, 3, 0), (3, 2, 1, 0))


def tie(*values):
    return lax.optimization_barrier(values)


def line_step(pair, j):
    left, right = pair
    return (
        lax.ppermute(left, "tensor", [(i, i + 1) for i in range(j - 1, 3)]),
        lax.ppermute(right, "tensor", [(i + 1, i) for i in range(0, 4 - j)]),
    )


def slot_one(one):
    return jnp.where(lax.axis_index("tensor") == 0, one[1], one[0])


def slot_two(one, two):
    plane = lax.axis_index("tensor")
    return jnp.where(plane == 0, two[1], jnp.where(plane == 3, two[0], one[1]))


def slot_three(two, three):
    plane = lax.axis_index("tensor")
    return jnp.where(
        plane == 0, three[1], jnp.where(plane == 1, two[1], jnp.where(plane == 2, two[0], three[0]))
    )


def slots_of(v, one, two, three):
    return [v, slot_one(one), slot_two(one, two), slot_three(two, three)]


def summed(v, axes):
    for axis in axes:
        reach = 1
        while reach < lax.axis_size(axis):
            v = v + swap(v, axis, reach)
            reach = reach * 2
    return v


def contract_rows(a, b):
    return lax.dot_general(a, b, (((0,), (0,)), ((), ())), preferred_element_type=F32)


def contract_columns(a, b):
    return lax.dot_general(a, b, (((1,), (1,)), ((), ())), preferred_element_type=F32)


def on_device(
    tokens, cotangent, destination, lengths, norm_gain, inner_weight, shared_weight, step_weight, filter_weight,
    filter_bias, shared_filter, shared_filter_bias, step_bias, decay_log, skip_gain, gate_gain, out_weight,
):
    row_count, model_width = tokens.shape
    width = filter_weight.shape[1]
    heads = step_bias.shape[0]
    rows_n, planes = lax.axis_size("row"), lax.axis_size("tensor")
    row, side, core, plane = (lax.axis_index(a) for a in ("row", "side", "core", "tensor"))
    group_rows = row_count // (rows_n * 4)
    owned = rows_n * group_rows
    source = (row * 2 + side) * 2 + core

    wanted = jnp.concatenate(
        [
            ((row ^ d) * planes + plane) * row_count + source * group_rows + jnp.arange(group_rows, dtype=jnp.int32)
            for d in range(rows_n)
        ]
    )
    chosen = (wanted[:, None] == destination[None, :]).astype(BF16)

    def exchanged(sent):
        return jnp.concatenate([sent[:group_rows]] + [
            swap(sent[d * group_rows : (d + 1) * group_rows], "row", d) for d in range(1, rows_n)
        ])

    def gathered(own):
        beside = swap(own, "side")
        return jnp.concatenate([own, swap(own, "core"), beside, swap(beside, "core")])

    slot_planes = jnp.array(SLOT_PLANES, jnp.int32)[plane]

    def assembled(doubled):
        rows, columns = doubled[0][0].shape
        whole = jnp.zeros((planes * rows_n * rows, columns), BF16)
        for i, pieces in enumerate(doubled):
            for d, p in enumerate(pieces):
                whole = lax.dynamic_update_slice(whole, p, (((row ^ d) * planes + slot_planes[i]) * rows, 0))
        return whole

    picked = jnp.dot(chosen, tokens, preferred_element_type=F32).astype(BF16)
    step_low = jnp.pad(step_weight.astype(BF16), ((0, 0), (0, LANES - heads)))
    piece = jnp.concatenate([inner_weight[:, 1].astype(BF16), step_low, shared_weight.astype(BF16)], axis=1)
    gate_piece = jnp.concatenate([inner_weight[:, 0].astype(BF16), out_weight.astype(BF16)], axis=1)
    own_tokens, piece, gate_piece = tie(exchanged(picked), crossed(piece), gate_piece)
    one = line_step((piece, piece), 1)
    in_slots = [row_doubling(piece)]
    gate_piece = crossed(gate_piece)
    hidden = own_tokens.astype(F32)
    scale = lax.rsqrt(jnp.mean(hidden * hidden, axis=-1, keepdims=True) + EPSILON)
    own_normed = (hidden * scale * norm_gain).astype(BF16)
    beside, near = swap(own_normed, "side"), swap(own_normed, "core")
    picked_cot = jnp.dot(chosen, cotangent, preferred_element_type=F32).astype(BF16)
    one, in_slots, near = tie(one, in_slots, near)
    two = line_step(one, 2)
    in_slots = in_slots + [row_doubling(slot_one(one))]
    two, in_slots, gate_piece, picked_cot = tie(two, in_slots, gate_piece, picked_cot)
    three = line_step(two, 3)
    in_slots = in_slots + [row_doubling(slot_two(one, two))]
    three, in_slots, beside = tie(three, in_slots, beside)
    in_slots = in_slots + [row_doubling(slot_three(two, three))]
    far = swap(beside, "core")
    one = line_step((gate_piece, gate_piece), 1)
    own_cot = exchanged(picked_cot)
    in_slots, far, one, own_cot = tie(in_slots, far, one, own_cot)
    two = line_step(one, 2)
    gate_slots = [row_doubling(gate_piece), row_doubling(slot_one(one))]
    cot_beside, cot_near = swap(own_cot, "side"), swap(own_cot, "core")
    normed = jnp.concatenate([own_normed, near, beside, far])
    in_full = assembled(in_slots)

    params = jnp.concatenate(
        [
            filter_weight,
            filter_bias[None],
            gate_gain[None],
            jnp.pad(jnp.concatenate([step_bias, decay_log, skip_gain]), (0, width - 3 * heads))[None],
            jnp.pad(lengths.astype(F32), ((0, 0), (0, width - lengths.shape[1]))),
        ],
        axis=0,
    )
    params = crossed(params)
    fw, fb, gain = params[:4], params[4:5], params[5:6]
    bias_here, decay_here, skip_here = (params[6, i * heads : (i + 1) * heads] for i in range(3))
    lens = params[7, : lengths.shape[1]].astype(jnp.int32)
    sf, sb = shared_filter, shared_filter_bias[None]
    table, skip, spread = head_rows(bias_here, decay_here, skip_here, width)

    if group_rows % SPAN == 0:
        spans = jnp.arange(row_count // SPAN, dtype=jnp.int32)
        part = (spans * SPAN // group_rows) ^ source
        order = (((part // 2) % 2 * 2 + part % 2) * rows_n + part // 4) * (group_rows // SPAN)
        order = order + spans % (group_rows // SPAN)
        sequenced = unsequenced = lambda v: v
    else:
        order = jnp.arange(row_count // SPAN, dtype=jnp.int32)
        groups = jnp.arange(4 * rows_n, dtype=jnp.int32)
        part = groups ^ source
        to = ((part // 2) % 2 * 2 + part % 2) * rows_n + part // 4
        fro = (((groups % rows_n) * 4 + groups // rows_n) ^ source)
        sequenced = lambda v: v.reshape(4 * rows_n, group_rows, -1)[to].reshape(v.shape)
        unsequenced = lambda v: v.reshape(4 * rows_n, group_rows, -1)[fro].reshape(v.shape)

    def summed_over_group(v):
        v = v + swap(v, "core").reshape(2, 2, 2, owned)[:, :, ::-1].reshape(2, -1)
        return v + swap(v, "side").reshape(2, 2, 2 * owned)[:, ::-1].reshape(2, -1)

    def rows_of(v, dx, dk):
        return v[(dx * 2 + dk) * owned : (dx * 2 + dk + 1) * owned]

    def group_parts(part):
        return part(1, 1).astype(BF16), part(1, 0), part(0, 1).astype(BF16), part(0, 0)

    def group_sum(parts):
        far, side_part, near, own_part = parts
        beside = swap((side_part + swap(far, "core").astype(F32)).astype(BF16), "side")
        return own_part + swap(near, "core").astype(F32) + beside.astype(F32)

    block_of = destination // row_count
    row_of, plane_of = (block_of // planes) ^ row, block_of % planes
    slot = row_of * group_rows + destination - block_of * row_count - source * group_rows

    def returned(held):
        def settled(which):
            where = jnp.concatenate([jnp.where(plane_of == slot_planes[j], slot, -1)[:, None] == jnp.arange(owned)[None, :]
                                     for j in which], axis=1)
            return jnp.dot(where.astype(BF16), jnp.concatenate([held[j] for j in which]), preferred_element_type=F32)
        return settled((0, 1)).astype(BF16) + settled((2, 3)).astype(BF16)

    proj = jnp.dot(normed, in_full, preferred_element_type=F32)
    proj, two, gate_slots, cot_near = tie(proj, two, gate_slots, cot_near)
    three = line_step(two, 3)
    gate_slots = gate_slots + [row_doubling(slot_two(one, two))]
    proj = sequenced(proj)
    mixed_seq, kept = mixer_forward(lens, order, proj, fw, fb, sf, sb, table, skip, spread)
    mixed_seq, three, gate_slots, cot_beside = tie(mixed_seq, three, gate_slots, cot_beside)
    both_full = assembled(gate_slots + [row_doubling(slot_three(two, three))])
    gate_full, out_full = both_full[:, :width], both_full[:, width:]
    cot = jnp.concatenate([own_cot, cot_near, cot_beside, swap(cot_beside, "core")])
    mixed = unsequenced(mixed_seq)
    gate_in = lax.optimization_barrier(jnp.dot(normed, gate_full, preferred_element_type=F32))
    normed_grad = lax.optimization_barrier(jnp.dot(cot, out_full, preferred_element_type=F32))
    gate_sig = jax.nn.sigmoid(gate_in)
    gate_act = gate_in * gate_sig
    gated = mixed * gate_act
    scaled_grad = normed_grad * gain
    sums = summed_over_group(jnp.stack([jnp.sum(gated * gated, axis=1), jnp.sum(scaled_grad * gated, axis=1)]))
    gate_scale = lax.rsqrt(sums[0] / (4 * width) + EPSILON)[:, None]
    gate_normed = (gated * gate_scale * gain).astype(BF16)
    far, side_part, near, own_part = group_parts(
        lambda dx, dk: contract_columns(rows_of(gate_normed, dx, dk), out_full)
    )
    sent = (side_part + swap(far, "core").astype(F32)).astype(BF16)
    own_rows = hidden + own_part + swap(near, "core").astype(F32)

    out_grad = contract_rows(cot, gate_normed).astype(BF16)
    gate_gain_grad = jnp.sum(normed_grad * gated * gate_scale, axis=0)
    gated_grad = gate_scale * scaled_grad - gated * gate_scale**3 * (sums[1] / (4 * width))[:, None]
    mixed_grad = gated_grad * gate_act
    gate_in_grad = (gated_grad * mixed * gate_sig * (1.0 + gate_in * (1.0 - gate_sig))).astype(BF16)
    gate_grad = contract_rows(normed, gate_in_grad).astype(BF16)
    both_grad = jnp.concatenate([gate_grad, out_grad], axis=1)
    mixed_grad, both_grad, sent, own_rows = lax.optimization_barrier((mixed_grad, both_grad, sent, own_rows))
    arrived = swap(sent, "side")
    both_grad = lax.psum_scatter(both_grad, ("row", "tensor"), scatter_dimension=0, tiled=True)
    proj_grad, shared_part, fsum, ssum, hsum = mixer_backward(
        lens, order, proj, sequenced(mixed_grad), mixed_seq, kept, fw, fb, sf, sb, table, skip, spread
    )
    proj_grad, shared_part = unsequenced(proj_grad), unsequenced(shared_part)
    proj_grad, shared_part, arrived = lax.optimization_barrier((proj_grad, shared_part, arrived))
    out_rows = exchanged((own_rows + arrived.astype(F32)).astype(BF16))

    def back_part(grads, dx, dk):
        gate_part, proj_part = grads
        return contract_columns(rows_of(gate_part, dx, dk), gate_full) + contract_columns(
            rows_of(proj_part, dx, dk), in_full[:, : width + LANES]
        )

    shared_far, shared_side, shared_near, shared_own = group_parts(lambda dx, dk: rows_of(shared_part, dx, dk))
    own_shared = group_sum((shared_far, shared_side, shared_near, shared_own)).astype(BF16)
    far = swap(back_part((gate_in_grad, proj_grad), 1, 1).astype(BF16), "core")
    near = swap(back_part((gate_in_grad, proj_grad), 0, 1).astype(BF16), "core")
    far, gate_later, proj_later, out_rows = lax.optimization_barrier((far, gate_in_grad, proj_grad, out_rows))
    out_one = line_step((out_rows, out_rows), 1)
    sent = (back_part((gate_later, proj_later), 1, 0) + far.astype(F32)).astype(BF16)
    own_back = back_part((gate_later, proj_later), 0, 0) + near.astype(F32)
    beside = swap(sent, "side")
    in_grad = contract_rows(normed, jnp.concatenate([proj_later, gathered(own_shared)], axis=1)).astype(BF16)
    in_grad, out_one, both_grad, own_back = lax.optimization_barrier((in_grad, out_one, both_grad, own_back))
    out_two = line_step(out_one, 2)
    both_grad = crossed(both_grad).astype(F32)
    in_grad = lax.psum_scatter(in_grad, ("row", "tensor"), scatter_dimension=0, tiled=True)
    normed_back = own_back + beside.astype(F32) + contract_columns(own_shared, in_full[:, width + LANES :])
    norm_gain_grad = jnp.sum(normed_back * hidden * scale, axis=0)
    gained = normed_back * norm_gain
    along = jnp.mean(gained * hidden, axis=1, keepdims=True)
    input_work = own_cot.astype(F32) + scale * gained - hidden * (scale**3 * along)
    line = lambda v: jnp.pad(v, (0, -v.shape[0] % width)).reshape(-1, width)
    skip_grad = fsum[5].reshape(heads, -1).sum(axis=1)
    small = jnp.concatenate(
        [
            fsum[:5],
            gate_gain_grad[None],
            jnp.pad(jnp.concatenate([hsum[0, :heads], hsum[1, :heads], skip_grad]), (0, width - 3 * heads))[None],
            jnp.zeros((1, width), F32),
            line(norm_gain_grad),
            line(ssum[:5].reshape(-1)),
        ],
        axis=0,
    )
    small = summed(small, ("row",))
    small = jnp.concatenate([small[:8], summed(small[8:], ("core", "side"))], axis=0)
    back_rows = exchanged(input_work.astype(BF16))
    back_rows, out_two, small = tie(back_rows, out_two, small)
    small_added = swap(small, "tensor", 1)
    out_three = line_step(out_two, 3)
    back_one = line_step((back_rows, back_rows), 1)
    back_one, out_three, small_added = tie(back_one, out_three, small_added)
    small = small + small_added
    small_added = swap(small, "tensor", 2)
    back_two = line_step(back_one, 2)
    layer_out = returned(slots_of(out_rows, out_one, out_two, out_three))
    back_two, in_grad, small_added = tie(back_two, in_grad, small_added)
    small = small + small_added
    mine, common = crossed(small[:8]), small[8:]
    input_grad = returned(slots_of(back_rows, back_one, back_two, line_step(back_two, 3)))
    in_grad = crossed(in_grad).astype(F32)
    inner_grad = jnp.stack([both_grad[:, :width], in_grad[:, :width]], axis=1)

    lines = line(norm_gain_grad).shape[0]
    norm_gain_grad = common[:lines].reshape(-1)[:model_width]
    shared_sums = common[lines:].reshape(-1)[: 5 * sf.shape[1]].reshape(5, -1)
    return (
        layer_out, input_grad, norm_gain_grad, inner_grad, in_grad[:, width + LANES :],
        in_grad[:, width : width + heads], mine[:4], mine[4], shared_sums[:4], shared_sums[4],
        mine[6, :heads], mine[6, heads : 2 * heads], mine[6, 2 * heads : 3 * heads], mine[5], both_grad[:, width:],
    )


def solution(mesh):
    count, planes = mesh.devices.shape
    assert planes == 4 and count % 4 == 0
    names = ("row", "side", "core", "tensor")
    inner = jax.sharding.Mesh(mesh.devices.reshape(count // 4, 2, 2, planes), names)
    dp = ("row", "side", "core")
    in_specs = (
        P(dp, None), P(dp, None), P(dp), P(dp, None), P(), P(dp, None, "tensor"), P(dp, None), P(dp, "tensor"),
        P(None, "tensor"), P("tensor"), P(), P(), P("tensor"), P("tensor"), P("tensor"), P("tensor"), P(dp, "tensor"),
    )
    out_specs = (
        P(dp, None), P(dp, None), P(), P(dp, None, "tensor"), P(dp, None), P(dp, "tensor"),
        P(None, "tensor"), P("tensor"), P(), P(), P("tensor"), P("tensor"), P("tensor"), P("tensor"), P(dp, "tensor"),
    )
    return jax.shard_map(on_device, mesh=inner, in_specs=in_specs, out_specs=out_specs, check_vma=False)
```

```python
import jax
import jax.numpy as jnp
from jax import lax
from jax.experimental import pallas as pl
from jax.experimental.pallas import tpu as pltpu
from jax.sharding import PartitionSpec as P

SPAN = 128
HALO = 8
LANES = 128
F32 = jnp.float32
BF16 = jnp.bfloat16
EPSILON = 1e-05


def mm(a, b):
    return jnp.dot(a, b, preferred_element_type=F32)


def mm_t(a, b):
    return lax.dot_general(a, b, (((1,), (1,)), ((), ())), preferred_element_type=F32)


def halves(v):
    high = v.astype(BF16)
    return high, (v - high.astype(F32)).astype(BF16)


def widen(v, spread):
    high, rest = halves(v)
    return mm(high, spread) + mm(rest, spread)


def head_sum(v, spread):
    high, rest = halves(v)
    return mm_t(high, spread) + mm_t(rest, spread)


def start_of(place, lens_ref):
    end, start = jnp.int32(0), jnp.zeros_like(place)
    for i in range(lens_ref.shape[0]):
        start = jnp.where(place >= end, end, start)
        end = end + lens_ref[i]
    return start


def taps(current, before, reach):
    whole = jnp.concatenate([before, current], axis=0)
    rows = current.shape[0]
    return [whole[HALO - k : HALO - k + rows] for k in range(reach)]


def filtered(shifted, allowed, kernel, bias):
    result = bias + kernel[0:1] * shifted[0]
    for k in range(1, len(shifted)):
        result = result + kernel[k : k + 1] * shifted[k] * allowed[k]
    return result


def permitted(place, start, reach, width):
    flags = [None]
    for k in range(1, reach):
        flags.append(jnp.where(place - k >= start, 1.0, 0.0)[:, :1])
    return flags


def softplus(v):
    return jnp.maximum(v, 0.0) + jnp.log1p(jnp.exp(-jnp.abs(v)))


def chunk_setup(base, lens_ref, span):
    place = base + lax.broadcasted_iota(jnp.int32, (span, LANES), 0)
    start = start_of(place, lens_ref)
    last_start = start_of(jnp.full((1, LANES), base + span - 1, jnp.int32), lens_ref)
    return place, start, last_start


def stacked(pair, low_lanes):
    zero = jnp.zeros_like(pair)
    return jnp.concatenate([jnp.where(low_lanes, pair, zero), jnp.where(low_lanes, zero, pair)], axis=0)


def forward_kernel(
    lens_ref, order_ref, proj_ref, fw_ref, fb_ref, sf_ref, sb_ref, head_ref, skip_ref, spread_ref,
    out_ref, kept_ref, memory, before, shared_before,
):
    step = pl.program_id(0)
    span = proj_ref.shape[0]
    width = out_ref.shape[1]
    reach = fw_ref.shape[0]
    pairs = width // LANES
    base = step * span

    @pl.when(step == 0)
    def _():
        memory[...] = jnp.zeros_like(memory)
        before[...] = jnp.zeros_like(before)
        shared_before[...] = jnp.zeros_like(shared_before)

    place, start, last_start = chunk_setup(base, lens_ref, span)
    allowed = permitted(place, start, reach, width)
    inputs = proj_ref[:, :width]
    shared = proj_ref[:, width + LANES :]
    conv = filtered(taps(inputs, before[...], reach), allowed, fw_ref, fb_ref[...])
    values = conv * jax.nn.sigmoid(conv)
    conv = filtered(taps(shared, shared_before[...], reach), allowed, sf_ref, sb_ref[...])
    factors = conv * jax.nn.sigmoid(conv)
    before[...] = inputs[span - HALO :]
    shared_before[...] = shared[span - HALO :]
    writes = factors[:, :LANES].astype(BF16)
    reads = factors[:, LANES:].astype(BF16)
    size = softplus(proj_ref[:, width : width + LANES] + head_ref[0:1])
    decay = -size * head_ref[1:2]
    row = lax.broadcasted_iota(jnp.int32, (span, span), 0)
    col = lax.broadcasted_iota(jnp.int32, (span, span), 1)
    lower = jnp.where(row >= col, 1.0, 0.0)
    total = jnp.dot(lower, decay, precision=lax.Precision.HIGHEST, preferred_element_type=F32)
    total_t = total.T
    inside = (col <= row) & (col + base >= start)
    scores = jnp.where(inside, mm_t(reads, writes), 0.0)
    spread = spread_ref[...]
    scaled = values * widen(size, spread)
    scaled_low = scaled.astype(BF16)
    entering = jnp.exp(total) * jnp.where(start < base, 1.0, 0.0)
    state = memory[...]
    state_low = state.astype(BF16)
    kept_ref[0] = state_low
    remote = mm(reads, state_low) * widen(entering, spread) + skip_ref[...] * values
    low_lanes = lax.broadcasted_iota(jnp.int32, (span, LANES), 1) < LANES // 2
    for pair in range(pairs):
        lanes = slice(pair * LANES, (pair + 1) * LANES)
        mixing = []
        for head in (2 * pair, 2 * pair + 1):
            fade = jnp.exp(jnp.minimum(total[:, head : head + 1] - total_t[head : head + 1, :], 0.0))
            mixing.append((scores * fade).astype(BF16))
        local = mm(jnp.concatenate(mixing, axis=1), stacked(scaled_low[:, lanes], low_lanes))
        out_ref[:, lanes] = (local + remote[:, lanes]).astype(out_ref.dtype)
    end = total[span - 1 : span]
    closing = jnp.exp(end - total) * jnp.where(place >= last_start, 1.0, 0.0)
    added = mm(writes.T, (scaled * widen(closing, spread)).astype(BF16))
    keeping = jnp.exp(end) * jnp.where(last_start < base, 1.0, 0.0)
    memory[...] = state * widen(jnp.broadcast_to(keeping, (8, LANES)), spread)[0:1] + added


def backward_kernel(
    lens_ref, order_ref, proj_ref, proj_before_ref, grad_ref, out_ref, kept_ref,
    fw_ref, fb_ref, sf_ref, sb_ref, head_ref, skip_ref, spread_ref,
    proj_grad_ref, shared_grad_ref, fsum_ref, ssum_ref, hsum_ref,
    memory_grad, after, shared_after,
):
    step = pl.program_id(0)
    steps = pl.num_programs(0)
    span = proj_ref.shape[0]
    width = out_ref.shape[1]
    reach = fw_ref.shape[0]
    pairs = width // LANES
    chunk = steps - 1 - step
    base = chunk * span

    @pl.when(step == 0)
    def _():
        memory_grad[...] = jnp.zeros_like(memory_grad)
        after[...] = jnp.zeros_like(after)
        shared_after[...] = jnp.zeros_like(shared_after)
        fsum_ref[...] = jnp.zeros_like(fsum_ref)
        ssum_ref[...] = jnp.zeros_like(ssum_ref)
        hsum_ref[...] = jnp.zeros_like(hsum_ref)

    place, start, last_start = chunk_setup(base, lens_ref, span)
    allowed = permitted(place, start, reach, width)
    first = jnp.where(chunk > 0, 1.0, 0.0)
    inputs = proj_ref[:, :width]
    shifted = taps(inputs, proj_before_ref[:, :width] * first, reach)
    conv = filtered(shifted, allowed, fw_ref, fb_ref[...])
    gate = jax.nn.sigmoid(conv)
    values = conv * gate
    slope = gate * (1.0 + conv * (1.0 - gate))
    shared_shifted = taps(proj_ref[:, width + LANES :], proj_before_ref[:, width + LANES :] * first, reach)
    conv = filtered(shared_shifted, allowed, sf_ref, sb_ref[...])
    gate = jax.nn.sigmoid(conv)
    factors = conv * gate
    shared_slope = gate * (1.0 + conv * (1.0 - gate))
    writes = factors[:, :LANES].astype(BF16)
    reads = factors[:, LANES:].astype(BF16)
    raw = proj_ref[:, width : width + LANES] + head_ref[0:1]
    size = softplus(raw)
    decay = -size * head_ref[1:2]
    row = lax.broadcasted_iota(jnp.int32, (span, span), 0)
    col = lax.broadcasted_iota(jnp.int32, (span, span), 1)
    lower = jnp.where(row >= col, 1.0, 0.0)
    upper = jnp.where(row <= col, 1.0, 0.0)
    total = jnp.dot(lower, decay, precision=lax.Precision.HIGHEST, preferred_element_type=F32)
    total_t = total.T
    start_t = start_of(base + col[0:1], lens_ref)
    inside_t = (row <= col) & (row + base >= start_t)
    scores_t = jnp.where(inside_t, mm_t(writes, reads), 0.0)
    spread = spread_ref[...]
    size_wide = widen(size, spread)
    scaled = values * size_wide
    scaled_low = scaled.astype(BF16)
    grad = grad_ref[...].astype(F32)
    grad_low = grad.astype(BF16)
    state_low = kept_ref[0]
    later = memory_grad[...]
    later_low = later.astype(BF16)
    entering = jnp.exp(total) * jnp.where(start < base, 1.0, 0.0)
    entered = (grad * widen(entering, spread)).astype(BF16)
    end = total[span - 1 : span]
    closing = jnp.exp(end - total) * jnp.where(place >= last_start, 1.0, 0.0)
    closing_wide = widen(closing, spread)
    keeping = jnp.exp(end) * jnp.where(last_start < base, 1.0, 0.0)
    keeping_wide = widen(jnp.broadcast_to(keeping, (8, LANES)), spread)[0:1]
    closed = mm(writes, later_low) * closing_wide
    low_lanes = lax.broadcasted_iota(jnp.int32, (span, LANES), 1) < LANES // 2
    scores_grad_t = jnp.zeros((span, span), F32)
    local = []
    for pair in range(pairs):
        lanes = slice(pair * LANES, (pair + 1) * LANES)
        halved = stacked(grad_low[:, lanes], low_lanes)
        mixing_grad = mm_t(scaled_low[:, lanes], halved)
        mixing = []
        for which, head in enumerate((2 * pair, 2 * pair + 1)):
            fade = jnp.exp(jnp.minimum(total_t[head : head + 1, :] - total[:, head : head + 1], 0.0))
            mixing.append((scores_t * fade).astype(BF16))
            scores_grad_t = scores_grad_t + mixing_grad[:, which * span : (which + 1) * span] * fade
        local.append(mm(jnp.concatenate(mixing, axis=1), halved))
    scaled_grad = jnp.concatenate(local, axis=1) + closed
    scores_grad_t = jnp.where(inside_t, scores_grad_t, 0.0).astype(BF16)
    kept_closing = (scaled * closing_wide).astype(BF16)
    reads_grad = mm(scores_grad_t.T, writes) + mm_t(entered, state_low)
    writes_grad = mm(scores_grad_t, reads) + mm_t(kept_closing, later_low)
    memory_grad[...] = later * keeping_wide + mm(reads.T, entered)
    skip = skip_ref[...]
    size_grad = head_sum(values * scaled_grad, spread)
    paid = head_sum(
        grad_low.astype(F32) * (out_ref[...] - skip * values) - scaled_low.astype(F32) * scaled_grad, spread
    )
    tail = jnp.sum(scaled_low.astype(F32) * closed, axis=0, keepdims=True) + keeping_wide * jnp.sum(
        later * state_low.astype(F32), axis=0, keepdims=True
    )
    tail = head_sum(jnp.broadcast_to(tail, (8, width)), spread)[0:1]
    total_grad = paid + jnp.where(place == base + span - 1, tail, 0.0)
    decay_grad = jnp.dot(upper, total_grad, precision=lax.Precision.HIGHEST, preferred_element_type=F32)
    raw_grad = (size_grad - decay_grad * head_ref[1:2]) * jax.nn.sigmoid(raw)
    proj_grad_ref[:, width:] = raw_grad.astype(proj_grad_ref.dtype)
    hsum_ref[0:1] += jnp.sum(raw_grad, axis=0, keepdims=True)
    hsum_ref[1:2] += jnp.sum(decay_grad * decay, axis=0, keepdims=True)
    conv_grad = (size_wide * scaled_grad + skip * grad) * slope
    shared_conv_grad = jnp.concatenate([writes_grad, reads_grad], axis=1) * shared_slope
    fsum_ref[reach : reach + 1] += jnp.sum(conv_grad, axis=0, keepdims=True)
    fsum_ref[reach + 1 : reach + 2] += jnp.sum(grad * values, axis=0, keepdims=True)
    ssum_ref[reach : reach + 1] += jnp.sum(shared_conv_grad, axis=0, keepdims=True)
    late = base + lax.broadcasted_iota(jnp.int32, (span + HALO, LANES), 0)
    late_allowed = permitted(late, start_of(late, lens_ref), reach, width)
    whole = jnp.concatenate([conv_grad, after[...]], axis=0)
    shared_whole = jnp.concatenate([shared_conv_grad, shared_after[...]], axis=0)
    result = fw_ref[0:1] * conv_grad
    shared_result = sf_ref[0:1] * shared_conv_grad
    fsum_ref[0:1] += jnp.sum(conv_grad * shifted[0], axis=0, keepdims=True)
    ssum_ref[0:1] += jnp.sum(shared_conv_grad * shared_shifted[0], axis=0, keepdims=True)
    for k in range(1, reach):
        masked = whole * late_allowed[k]
        fsum_ref[k : k + 1] += jnp.sum(masked[:span] * shifted[k], axis=0, keepdims=True)
        result = result + fw_ref[k : k + 1] * masked[k : k + span]
        masked = shared_whole * late_allowed[k]
        ssum_ref[k : k + 1] += jnp.sum(masked[:span] * shared_shifted[k], axis=0, keepdims=True)
        shared_result = shared_result + sf_ref[k : k + 1] * masked[k : k + span]
    after[...] = conv_grad[:HALO]
    shared_after[...] = shared_conv_grad[:HALO]
    proj_grad_ref[:, :width] = result.astype(proj_grad_ref.dtype)
    shared_grad_ref[...] = shared_result.astype(shared_grad_ref.dtype)


def head_rows(step_bias, decay_log, skip_gain, width):
    heads = step_bias.shape[0]
    table = jnp.zeros((8, LANES), F32)
    table = table.at[0, :heads].set(step_bias).at[1, :heads].set(jnp.exp(decay_log))
    skip = jnp.repeat(skip_gain, width // heads)[None, :]
    spread = (jnp.arange(LANES)[:, None] == (jnp.arange(width) // (width // heads))[None, :]).astype(BF16)
    return table, skip, spread


def fixed(shape):
    return pl.BlockSpec(shape, lambda *_: (0,) * len(shape))


def mixer_forward(lens, order, proj, fw, fb, sf, sb, table, skip, spread):
    rows = proj.shape[0]
    width = fw.shape[1]
    steps = rows // SPAN
    block = lambda cols: pl.BlockSpec((SPAN, cols), lambda i, lens_ref, order_ref: (order_ref[i], 0))
    return pl.pallas_call(
        forward_kernel,
        grid_spec=pltpu.PrefetchScalarGridSpec(
            num_scalar_prefetch=2,
            grid=(steps,),
            in_specs=[
                block(proj.shape[1]), fixed(fw.shape), fixed(fb.shape), fixed(sf.shape),
                fixed(sb.shape), fixed(table.shape), fixed(skip.shape), fixed(spread.shape),
            ],
            out_specs=[block(width), pl.BlockSpec((1, LANES, width), lambda i, *_: (i, 0, 0))],
            scratch_shapes=[
                pltpu.VMEM((LANES, width), F32),
                pltpu.VMEM((HALO, width), F32),
                pltpu.VMEM((HALO, sf.shape[1]), F32),
            ],
        ),
        out_shape=[
            jax.ShapeDtypeStruct((rows, width), F32),
            jax.ShapeDtypeStruct((steps, LANES, width), BF16),
        ],
        cost_estimate=pl.CostEstimate(flops=20 * 10**9, bytes_accessed=30 * 10**6, transcendentals=0),
        name="mixer_forward",
    )(lens, order, proj, fw, fb, sf, sb, table, skip, spread)


def mixer_backward(lens, order, proj, grad, out, kept, fw, fb, sf, sb, table, skip, spread):
    rows = proj.shape[0]
    width = fw.shape[1]
    steps = rows // SPAN
    lead = SPAN // HALO
    block = lambda cols: pl.BlockSpec((SPAN, cols), lambda i, lens_ref, order_ref: (order_ref[steps - 1 - i], 0))
    ahead = lambda cols: pl.BlockSpec(
        (HALO, cols),
        lambda i, lens_ref, order_ref: (order_ref[jnp.maximum(steps - 2 - i, 0)] * lead + lead - 1, 0),
    )
    return pl.pallas_call(
        backward_kernel,
        grid_spec=pltpu.PrefetchScalarGridSpec(
            num_scalar_prefetch=2,
            grid=(steps,),
            in_specs=[
                block(proj.shape[1]), ahead(proj.shape[1]),
                block(width), block(width), pl.BlockSpec((1, LANES, width), lambda i, *_: (steps - 1 - i, 0, 0)),
                fixed(fw.shape), fixed(fb.shape), fixed(sf.shape),
                fixed(sb.shape), fixed(table.shape), fixed(skip.shape), fixed(spread.shape),
            ],
            out_specs=[
                block(width + LANES), block(sf.shape[1]),
                fixed((8, width)), fixed((8, sf.shape[1])), fixed((8, LANES)),
            ],
            scratch_shapes=[
                pltpu.VMEM((LANES, width), F32),
                pltpu.VMEM((HALO, width), F32),
                pltpu.VMEM((HALO, sf.shape[1]), F32),
            ],
        ),
        out_shape=[
            jax.ShapeDtypeStruct((rows, width + LANES), BF16),
            jax.ShapeDtypeStruct((rows, sf.shape[1]), F32),
            jax.ShapeDtypeStruct((8, width), F32),
            jax.ShapeDtypeStruct((8, sf.shape[1]), F32),
            jax.ShapeDtypeStruct((8, LANES), F32),
        ],
        cost_estimate=pl.CostEstimate(flops=40 * 10**9, bytes_accessed=60 * 10**6, transcendentals=0),
        name="mixer_backward",
    )(lens, order, proj, proj, grad, out, kept, fw, fb, sf, sb, table, skip, spread)


def swap(v, axis, mask=1):
    count = lax.axis_size(axis)
    return lax.ppermute(v, axis, [(i, i ^ mask) for i in range(count)])


def crossed(v):
    pairs = [(a * 4 + b, b * 4 + a) for a in range(4) for b in range(4)]
    return lax.ppermute(v, ("side", "core", "tensor"), pairs)


def row_doubling(v):
    pieces = [v]
    while len(pieces) < lax.axis_size("row"):
        reach = len(pieces)
        pieces = pieces + [swap(p, "row", reach) for p in pieces]
    return pieces


SLOT_PLANES = ((0, 1, 2, 3), (1, 0, 2, 3), (2, 1, 3, 0), (3, 2, 1, 0))


def tie(*values):
    return lax.optimization_barrier(values)


def line_step(pair, j):
    left, right = pair
    return (
        lax.ppermute(left, "tensor", [(i, i + 1) for i in range(j - 1, 3)]),
        lax.ppermute(right, "tensor", [(i + 1, i) for i in range(0, 4 - j)]),
    )


def slot_one(one):
    return jnp.where(lax.axis_index("tensor") == 0, one[1], one[0])


def slot_two(one, two):
    plane = lax.axis_index("tensor")
    return jnp.where(plane == 0, two[1], jnp.where(plane == 3, two[0], one[1]))


def slot_three(two, three):
    plane = lax.axis_index("tensor")
    return jnp.where(
        plane == 0, three[1], jnp.where(plane == 1, two[1], jnp.where(plane == 2, two[0], three[0]))
    )


def summed(v, axes):
    for axis in axes:
        reach = 1
        while reach < lax.axis_size(axis):
            v = v + swap(v, axis, reach)
            reach = reach * 2
    return v


def contract_rows(a, b):
    return lax.dot_general(a, b, (((0,), (0,)), ((), ())), preferred_element_type=F32)


def contract_columns(a, b):
    return lax.dot_general(a, b, (((1,), (1,)), ((), ())), preferred_element_type=F32)


def on_device(
    tokens, cotangent, destination, lengths, norm_gain, inner_weight, shared_weight, step_weight, filter_weight,
    filter_bias, shared_filter, shared_filter_bias, step_bias, decay_log, skip_gain, gate_gain, out_weight,
):
    row_count, model_width = tokens.shape
    width = filter_weight.shape[1]
    heads = step_bias.shape[0]
    rows_n, planes = lax.axis_size("row"), lax.axis_size("tensor")
    row, side, core, plane = (lax.axis_index(a) for a in ("row", "side", "core", "tensor"))
    group_rows = row_count // (rows_n * 4)
    owned = rows_n * group_rows
    source = (row * 2 + side) * 2 + core

    wanted = jnp.concatenate(
        [
            ((row ^ d) * planes + plane) * row_count + source * group_rows + jnp.arange(group_rows, dtype=jnp.int32)
            for d in range(rows_n)
        ]
    )
    chosen = (wanted[:, None] == destination[None, :]).astype(BF16)

    def exchanged(sent):
        return jnp.concatenate([sent[:group_rows]] + [
            swap(sent[d * group_rows : (d + 1) * group_rows], "row", d) for d in range(1, rows_n)
        ])

    def gathered(own):
        beside = swap(own, "side")
        return jnp.concatenate([own, swap(own, "core"), beside, swap(beside, "core")])

    slot_planes = jnp.array(SLOT_PLANES, jnp.int32)[plane]

    def assembled(doubled):
        rows, columns = doubled[0][0].shape
        whole = jnp.zeros((planes * rows_n * rows, columns), BF16)
        for i, pieces in enumerate(doubled):
            for d, p in enumerate(pieces):
                whole = lax.dynamic_update_slice(whole, p, (((row ^ d) * planes + slot_planes[i]) * rows, 0))
        return whole

    picked = jnp.dot(chosen, tokens, preferred_element_type=F32).astype(BF16)
    step_low = jnp.pad(step_weight.astype(BF16), ((0, 0), (0, LANES - heads)))
    piece = jnp.concatenate([inner_weight[:, 1].astype(BF16), step_low, shared_weight.astype(BF16)], axis=1)
    gate_piece = jnp.concatenate([inner_weight[:, 0].astype(BF16), out_weight.astype(BF16)], axis=1)
    picked_cot = jnp.dot(chosen, cotangent, preferred_element_type=F32).astype(BF16)
    own_tokens, piece, picked_cot = tie(exchanged(picked), crossed(piece), picked_cot)
    own_cot = exchanged(picked_cot)
    one = line_step((piece, piece), 1)
    in_slots = [row_doubling(piece)]
    hidden = own_tokens.astype(F32)
    scale = lax.rsqrt(jnp.mean(hidden * hidden, axis=-1, keepdims=True) + EPSILON)
    own_normed = (hidden * scale * norm_gain).astype(BF16)
    beside, near = swap(own_normed, "side"), swap(own_normed, "core")
    one, near, gate_piece = tie(one, near, gate_piece)
    two = line_step(one, 2)
    gate_piece = crossed(gate_piece)
    in_slots = in_slots + [row_doubling(slot_one(one))]
    two, own_cot = tie(two, own_cot)
    three = line_step(two, 3)
    in_slots = in_slots + [row_doubling(slot_two(one, two))]
    three, beside, gate_piece = tie(three, beside, gate_piece)
    in_slots = in_slots + [row_doubling(slot_three(two, three))]
    far = swap(beside, "core")
    one = line_step((gate_piece, gate_piece), 1)
    cot_beside, cot_near = swap(own_cot, "side"), swap(own_cot, "core")
    in_slots, far, one = tie(in_slots, far, one)
    two = line_step(one, 2)
    gate_slots = [row_doubling(gate_piece), row_doubling(slot_one(one))]
    normed = jnp.concatenate([own_normed, near, beside, far])
    in_full = assembled(in_slots)

    params = jnp.concatenate(
        [
            filter_weight,
            filter_bias[None],
            gate_gain[None],
            jnp.pad(jnp.concatenate([step_bias, decay_log, skip_gain]), (0, width - 3 * heads))[None],
            jnp.pad(lengths.astype(F32), ((0, 0), (0, width - lengths.shape[1]))),
        ],
        axis=0,
    )
    params = crossed(params)
    fw, fb, gain = params[:4], params[4:5], params[5:6]
    bias_here, decay_here, skip_here = (params[6, i * heads : (i + 1) * heads] for i in range(3))
    lens = params[7, : lengths.shape[1]].astype(jnp.int32)
    sf, sb = shared_filter, shared_filter_bias[None]
    table, skip, spread = head_rows(bias_here, decay_here, skip_here, width)

    if group_rows % SPAN == 0:
        spans = jnp.arange(row_count // SPAN, dtype=jnp.int32)
        part = (spans * SPAN // group_rows) ^ source
        order = (((part // 2) % 2 * 2 + part % 2) * rows_n + part // 4) * (group_rows // SPAN)
        order = order + spans % (group_rows // SPAN)
        sequenced = unsequenced = lambda v: v
    else:
        order = jnp.arange(row_count // SPAN, dtype=jnp.int32)
        groups = jnp.arange(4 * rows_n, dtype=jnp.int32)
        part = groups ^ source
        to = ((part // 2) % 2 * 2 + part % 2) * rows_n + part // 4
        fro = (((groups % rows_n) * 4 + groups // rows_n) ^ source)
        sequenced = lambda v: v.reshape(4 * rows_n, group_rows, -1)[to].reshape(v.shape)
        unsequenced = lambda v: v.reshape(4 * rows_n, group_rows, -1)[fro].reshape(v.shape)

    def summed_over_group(v):
        v = v + swap(v, "core").reshape(2, 2, 2, owned)[:, :, ::-1].reshape(2, -1)
        return v + swap(v, "side").reshape(2, 2, 2 * owned)[:, ::-1].reshape(2, -1)

    def rows_of(v, dx, dk):
        return v[(dx * 2 + dk) * owned : (dx * 2 + dk + 1) * owned]

    def group_parts(part):
        return part(1, 1).astype(BF16), part(1, 0), part(0, 1).astype(BF16), part(0, 0)

    def group_sum(parts):
        far, side_part, near, own_part = parts
        beside = swap((side_part + swap(far, "core").astype(F32)).astype(BF16), "side")
        return own_part + swap(near, "core").astype(F32) + beside.astype(F32)

    block_of = destination // row_count
    row_of, plane_of = (block_of // planes) ^ row, block_of % planes
    slot = row_of * group_rows + destination - block_of * row_count - source * group_rows

    def settled(held, which):
        where = jnp.concatenate([jnp.where(plane_of == slot_planes[j], slot, -1)[:, None] == jnp.arange(owned)[None, :]
                                 for j in which], axis=1)
        return jnp.dot(where.astype(BF16), jnp.concatenate(held), preferred_element_type=F32).astype(BF16)

    proj = jnp.dot(normed, in_full, preferred_element_type=F32)
    proj, two, gate_slots, cot_near = tie(proj, two, gate_slots, cot_near)
    three = line_step(two, 3)
    gate_slots = gate_slots + [row_doubling(slot_two(one, two))]
    proj = sequenced(proj)
    mixed_seq, kept = mixer_forward(lens, order, proj, fw, fb, sf, sb, table, skip, spread)
    mixed_seq, three, gate_slots, cot_beside = tie(mixed_seq, three, gate_slots, cot_beside)
    both_full = assembled(gate_slots + [row_doubling(slot_three(two, three))])
    gate_full, out_full = both_full[:, :width], both_full[:, width:]
    cot = jnp.concatenate([own_cot, cot_near, cot_beside, swap(cot_beside, "core")])
    mixed = unsequenced(mixed_seq)
    gate_in = lax.optimization_barrier(jnp.dot(normed, gate_full, preferred_element_type=F32))
    normed_grad = lax.optimization_barrier(jnp.dot(cot, out_full, preferred_element_type=F32))
    gate_sig = jax.nn.sigmoid(gate_in)
    gate_act = gate_in * gate_sig
    gated = mixed * gate_act
    scaled_grad = normed_grad * gain
    sums = summed_over_group(jnp.stack([jnp.sum(gated * gated, axis=1), jnp.sum(scaled_grad * gated, axis=1)]))
    gate_scale = lax.rsqrt(sums[0] / (4 * width) + EPSILON)[:, None]
    gate_normed = (gated * gate_scale * gain).astype(BF16)
    far, side_part, near, own_part = group_parts(
        lambda dx, dk: contract_columns(rows_of(gate_normed, dx, dk), out_full)
    )
    sent = (side_part + swap(far, "core").astype(F32)).astype(BF16)
    own_rows = hidden + own_part + swap(near, "core").astype(F32)

    out_grad = contract_rows(cot, gate_normed).astype(BF16)
    gate_gain_grad = jnp.sum(normed_grad * gated * gate_scale, axis=0)
    gated_grad = gate_scale * scaled_grad - gated * gate_scale**3 * (sums[1] / (4 * width))[:, None]
    mixed_grad = gated_grad * gate_act
    gate_in_grad = (gated_grad * mixed * gate_sig * (1.0 + gate_in * (1.0 - gate_sig))).astype(BF16)
    gate_grad = contract_rows(normed, gate_in_grad).astype(BF16)
    both_grad = jnp.concatenate([gate_grad, out_grad], axis=1)
    mixed_grad, both_grad, sent, own_rows = lax.optimization_barrier((mixed_grad, both_grad, sent, own_rows))
    arrived = swap(sent, "side")
    both_grad = lax.psum_scatter(both_grad, ("row", "tensor"), scatter_dimension=0, tiled=True)
    proj_grad, shared_part, fsum, ssum, hsum = mixer_backward(
        lens, order, proj, sequenced(mixed_grad), mixed_seq, kept, fw, fb, sf, sb, table, skip, spread
    )
    proj_grad, shared_part = unsequenced(proj_grad), unsequenced(shared_part)
    proj_grad, shared_part, arrived = lax.optimization_barrier((proj_grad, shared_part, arrived))
    out_rows = exchanged((own_rows + arrived.astype(F32)).astype(BF16))

    def back_part(grads, dx, dk):
        gate_part, proj_part = grads
        return contract_columns(rows_of(gate_part, dx, dk), gate_full) + contract_columns(
            rows_of(proj_part, dx, dk), in_full[:, : width + LANES]
        )

    shared_far, shared_side, shared_near, shared_own = group_parts(lambda dx, dk: rows_of(shared_part, dx, dk))
    own_shared = group_sum((shared_far, shared_side, shared_near, shared_own)).astype(BF16)
    far = swap(back_part((gate_in_grad, proj_grad), 1, 1).astype(BF16), "core")
    near = swap(back_part((gate_in_grad, proj_grad), 0, 1).astype(BF16), "core")
    far, gate_later, proj_later, out_rows = lax.optimization_barrier((far, gate_in_grad, proj_grad, out_rows))
    out_one = line_step((out_rows, out_rows), 1)
    sent = (back_part((gate_later, proj_later), 1, 0) + far.astype(F32)).astype(BF16)
    own_back = back_part((gate_later, proj_later), 0, 0) + near.astype(F32)
    beside = swap(sent, "side")
    in_grad = contract_rows(normed, jnp.concatenate([proj_later, gathered(own_shared)], axis=1)).astype(BF16)
    in_grad, out_one, both_grad, own_back = lax.optimization_barrier((in_grad, out_one, both_grad, own_back))
    out_two = line_step(out_one, 2)
    both_grad = crossed(both_grad)
    in_grad = lax.psum_scatter(in_grad, ("row", "tensor"), scatter_dimension=0, tiled=True)
    normed_back = own_back + beside.astype(F32) + contract_columns(own_shared, in_full[:, width + LANES :])
    norm_gain_grad = jnp.sum(normed_back * hidden * scale, axis=0)
    gained = normed_back * norm_gain
    along = jnp.mean(gained * hidden, axis=1, keepdims=True)
    input_work = own_cot.astype(F32) + scale * gained - hidden * (scale**3 * along)
    line = lambda v: jnp.pad(v, (0, -v.shape[0] % width)).reshape(-1, width)
    skip_grad = fsum[5].reshape(heads, -1).sum(axis=1)
    small = jnp.concatenate(
        [
            fsum[:5],
            gate_gain_grad[None],
            jnp.pad(jnp.concatenate([hsum[0, :heads], hsum[1, :heads], skip_grad]), (0, width - 3 * heads))[None],
            jnp.zeros((1, width), F32),
            line(norm_gain_grad),
            line(ssum[:5].reshape(-1)),
        ],
        axis=0,
    )
    small = summed(small, ("row",))
    small = jnp.concatenate([small[:8], summed(small[8:], ("core", "side"))], axis=0)
    back_rows = exchanged(input_work.astype(BF16))
    back_rows, out_two, small, both_grad = tie(back_rows, out_two, small, both_grad)
    back_one = line_step((back_rows, back_rows), 1)
    out_three = line_step(out_two, 3)
    back_two = line_step(back_one, 2)
    back_two, in_grad = tie(back_two, in_grad)
    back_three = line_step(back_two, 3)
    out_three, _ = tie(out_three, back_two)
    layer_out = settled([out_rows, slot_one(out_one)], (0, 1))
    layer_out = layer_out + settled([slot_two(out_one, out_two), slot_three(out_two, out_three)], (2, 3))
    input_grad = settled([back_rows, slot_one(back_one)], (0, 1))
    layer_out, input_grad, back_three, small = tie(layer_out, input_grad, back_three, small)
    input_grad = input_grad + settled([slot_two(back_one, back_two), slot_three(back_two, back_three)], (2, 3))
    small = small + swap(small, "tensor", 1)
    small = small + swap(small, "tensor", 2)
    mine, common = crossed(small[:8]), small[8:]
    in_grad = crossed(in_grad).astype(F32)
    inner_grad = jnp.stack([both_grad[:, :width].astype(F32), in_grad[:, :width]], axis=1)

    lines = line(norm_gain_grad).shape[0]
    norm_gain_grad = common[:lines].reshape(-1)[:model_width]
    shared_sums = common[lines:].reshape(-1)[: 5 * sf.shape[1]].reshape(5, -1)
    return (
        layer_out, input_grad, norm_gain_grad, inner_grad, in_grad[:, width + LANES :],
        in_grad[:, width : width + heads], mine[:4], mine[4], shared_sums[:4], shared_sums[4],
        mine[6, :heads], mine[6, heads : 2 * heads], mine[6, 2 * heads : 3 * heads], mine[5], both_grad[:, width:].astype(F32),
    )


def solution(mesh):
    count, planes = mesh.devices.shape
    assert planes == 4 and count % 4 == 0
    names = ("row", "side", "core", "tensor")
    inner = jax.sharding.Mesh(mesh.devices.reshape(count // 4, 2, 2, planes), names)
    dp = ("row", "side", "core")
    in_specs = (
        P(dp, None), P(dp, None), P(dp), P(dp, None), P(), P(dp, None, "tensor"), P(dp, None), P(dp, "tensor"),
        P(None, "tensor"), P("tensor"), P(), P(), P("tensor"), P("tensor"), P("tensor"), P("tensor"), P(dp, "tensor"),
    )
    out_specs = (
        P(dp, None), P(dp, None), P(), P(dp, None, "tensor"), P(dp, None), P(dp, "tensor"),
        P(None, "tensor"), P("tensor"), P(), P(), P("tensor"), P("tensor"), P("tensor"), P("tensor"), P(dp, "tensor"),
    )
    return jax.shard_map(on_device, mesh=inner, in_specs=in_specs, out_specs=out_specs, check_vma=False)
```

```python
import jax
import jax.numpy as jnp
from jax import lax
from jax.experimental import pallas as pl
from jax.experimental.pallas import tpu as pltpu
from jax.sharding import PartitionSpec as P

SPAN = 128
HALO = 8
LANES = 128
F32 = jnp.float32
BF16 = jnp.bfloat16
EPSILON = 1e-05


def mm(a, b):
    return jnp.dot(a, b, preferred_element_type=F32)


def mm_t(a, b):
    return lax.dot_general(a, b, (((1,), (1,)), ((), ())), preferred_element_type=F32)


def halves(v):
    high = v.astype(BF16)
    return high, (v - high.astype(F32)).astype(BF16)


def widen(v, spread):
    high, rest = halves(v)
    return mm(high, spread) + mm(rest, spread)


def head_sum(v, spread):
    high, rest = halves(v)
    return mm_t(high, spread) + mm_t(rest, spread)


def start_of(place, lens_ref):
    end, start = jnp.int32(0), jnp.zeros_like(place)
    for i in range(lens_ref.shape[0]):
        start = jnp.where(place >= end, end, start)
        end = end + lens_ref[i]
    return start


def taps(current, before, reach):
    whole = jnp.concatenate([before, current], axis=0)
    rows = current.shape[0]
    return [whole[HALO - k : HALO - k + rows] for k in range(reach)]


def filtered(shifted, allowed, kernel, bias):
    result = bias + kernel[0:1] * shifted[0]
    for k in range(1, len(shifted)):
        result = result + kernel[k : k + 1] * shifted[k] * allowed[k]
    return result


def permitted(place, start, reach, width):
    flags = [None]
    for k in range(1, reach):
        flags.append(jnp.where(place - k >= start, 1.0, 0.0)[:, :1])
    return flags


def softplus(v):
    return jnp.maximum(v, 0.0) + jnp.log1p(jnp.exp(-jnp.abs(v)))


def chunk_setup(base, lens_ref, span):
    place = base + lax.broadcasted_iota(jnp.int32, (span, LANES), 0)
    start = start_of(place, lens_ref)
    last_start = start_of(jnp.full((1, LANES), base + span - 1, jnp.int32), lens_ref)
    return place, start, last_start


def stacked(pair, low_lanes):
    zero = jnp.zeros_like(pair)
    return jnp.concatenate([jnp.where(low_lanes, pair, zero), jnp.where(low_lanes, zero, pair)], axis=0)


def forward_kernel(
    lens_ref, order_ref, proj_ref, fw_ref, fb_ref, sf_ref, sb_ref, head_ref, skip_ref, spread_ref,
    out_ref, kept_ref, memory, before, shared_before,
):
    step = pl.program_id(0)
    span = proj_ref.shape[0]
    width = out_ref.shape[1]
    reach = fw_ref.shape[0]
    pairs = width // LANES
    base = step * span

    @pl.when(step == 0)
    def _():
        memory[...] = jnp.zeros_like(memory)
        before[...] = jnp.zeros_like(before)
        shared_before[...] = jnp.zeros_like(shared_before)

    place, start, last_start = chunk_setup(base, lens_ref, span)
    allowed = permitted(place, start, reach, width)
    inputs = proj_ref[:, :width]
    shared = proj_ref[:, width + LANES :]
    conv = filtered(taps(inputs, before[...], reach), allowed, fw_ref, fb_ref[...])
    values = conv * jax.nn.sigmoid(conv)
    conv = filtered(taps(shared, shared_before[...], reach), allowed, sf_ref, sb_ref[...])
    factors = conv * jax.nn.sigmoid(conv)
    before[...] = inputs[span - HALO :]
    shared_before[...] = shared[span - HALO :]
    writes = factors[:, :LANES].astype(BF16)
    reads = factors[:, LANES:].astype(BF16)
    size = softplus(proj_ref[:, width : width + LANES] + head_ref[0:1])
    decay = -size * head_ref[1:2]
    row = lax.broadcasted_iota(jnp.int32, (span, span), 0)
    col = lax.broadcasted_iota(jnp.int32, (span, span), 1)
    lower = jnp.where(row >= col, 1.0, 0.0)
    total = jnp.dot(lower, decay, precision=lax.Precision.HIGHEST, preferred_element_type=F32)
    total_t = total.T
    inside = (col <= row) & (col + base >= start)
    scores = jnp.where(inside, mm_t(reads, writes), 0.0)
    spread = spread_ref[...]
    scaled = values * widen(size, spread)
    scaled_low = scaled.astype(BF16)
    entering = jnp.exp(total) * jnp.where(start < base, 1.0, 0.0)
    state = memory[...]
    state_low = state.astype(BF16)
    kept_ref[0] = state_low
    remote = mm(reads, state_low) * widen(entering, spread) + skip_ref[...] * values
    low_lanes = lax.broadcasted_iota(jnp.int32, (span, LANES), 1) < LANES // 2
    for pair in range(pairs):
        lanes = slice(pair * LANES, (pair + 1) * LANES)
        mixing = []
        for head in (2 * pair, 2 * pair + 1):
            fade = jnp.exp(jnp.minimum(total[:, head : head + 1] - total_t[head : head + 1, :], 0.0))
            mixing.append((scores * fade).astype(BF16))
        local = mm(jnp.concatenate(mixing, axis=1), stacked(scaled_low[:, lanes], low_lanes))
        out_ref[:, lanes] = (local + remote[:, lanes]).astype(out_ref.dtype)
    end = total[span - 1 : span]
    closing = jnp.exp(end - total) * jnp.where(place >= last_start, 1.0, 0.0)
    added = mm(writes.T, (scaled * widen(closing, spread)).astype(BF16))
    keeping = jnp.exp(end) * jnp.where(last_start < base, 1.0, 0.0)
    memory[...] = state * widen(jnp.broadcast_to(keeping, (8, LANES)), spread)[0:1] + added


def backward_kernel(
    lens_ref, order_ref, proj_ref, proj_before_ref, grad_ref, out_ref, kept_ref,
    fw_ref, fb_ref, sf_ref, sb_ref, head_ref, skip_ref, spread_ref,
    proj_grad_ref, shared_grad_ref, fsum_ref, ssum_ref, hsum_ref,
    memory_grad, after, shared_after,
):
    step = pl.program_id(0)
    steps = pl.num_programs(0)
    span = proj_ref.shape[0]
    width = out_ref.shape[1]
    reach = fw_ref.shape[0]
    pairs = width // LANES
    chunk = steps - 1 - step
    base = chunk * span

    @pl.when(step == 0)
    def _():
        memory_grad[...] = jnp.zeros_like(memory_grad)
        after[...] = jnp.zeros_like(after)
        shared_after[...] = jnp.zeros_like(shared_after)
        fsum_ref[...] = jnp.zeros_like(fsum_ref)
        ssum_ref[...] = jnp.zeros_like(ssum_ref)
        hsum_ref[...] = jnp.zeros_like(hsum_ref)

    place, start, last_start = chunk_setup(base, lens_ref, span)
    allowed = permitted(place, start, reach, width)
    first = jnp.where(chunk > 0, 1.0, 0.0)
    inputs = proj_ref[:, :width]
    shifted = taps(inputs, proj_before_ref[:, :width] * first, reach)
    conv = filtered(shifted, allowed, fw_ref, fb_ref[...])
    gate = jax.nn.sigmoid(conv)
    values = conv * gate
    slope = gate * (1.0 + conv * (1.0 - gate))
    shared_shifted = taps(proj_ref[:, width + LANES :], proj_before_ref[:, width + LANES :] * first, reach)
    conv = filtered(shared_shifted, allowed, sf_ref, sb_ref[...])
    gate = jax.nn.sigmoid(conv)
    factors = conv * gate
    shared_slope = gate * (1.0 + conv * (1.0 - gate))
    writes = factors[:, :LANES].astype(BF16)
    reads = factors[:, LANES:].astype(BF16)
    raw = proj_ref[:, width : width + LANES] + head_ref[0:1]
    size = softplus(raw)
    decay = -size * head_ref[1:2]
    row = lax.broadcasted_iota(jnp.int32, (span, span), 0)
    col = lax.broadcasted_iota(jnp.int32, (span, span), 1)
    lower = jnp.where(row >= col, 1.0, 0.0)
    upper = jnp.where(row <= col, 1.0, 0.0)
    total = jnp.dot(lower, decay, precision=lax.Precision.HIGHEST, preferred_element_type=F32)
    total_t = total.T
    start_t = start_of(base + col[0:1], lens_ref)
    inside_t = (row <= col) & (row + base >= start_t)
    scores_t = jnp.where(inside_t, mm_t(writes, reads), 0.0)
    spread = spread_ref[...]
    size_wide = widen(size, spread)
    scaled = values * size_wide
    scaled_low = scaled.astype(BF16)
    grad = grad_ref[...].astype(F32)
    grad_low = grad.astype(BF16)
    state_low = kept_ref[0]
    later = memory_grad[...]
    later_low = later.astype(BF16)
    entering = jnp.exp(total) * jnp.where(start < base, 1.0, 0.0)
    entered = (grad * widen(entering, spread)).astype(BF16)
    end = total[span - 1 : span]
    closing = jnp.exp(end - total) * jnp.where(place >= last_start, 1.0, 0.0)
    closing_wide = widen(closing, spread)
    keeping = jnp.exp(end) * jnp.where(last_start < base, 1.0, 0.0)
    keeping_wide = widen(jnp.broadcast_to(keeping, (8, LANES)), spread)[0:1]
    closed = mm(writes, later_low) * closing_wide
    low_lanes = lax.broadcasted_iota(jnp.int32, (span, LANES), 1) < LANES // 2
    scores_grad_t = jnp.zeros((span, span), F32)
    local = []
    for pair in range(pairs):
        lanes = slice(pair * LANES, (pair + 1) * LANES)
        halved = stacked(grad_low[:, lanes], low_lanes)
        mixing_grad = mm_t(scaled_low[:, lanes], halved)
        mixing = []
        for which, head in enumerate((2 * pair, 2 * pair + 1)):
            fade = jnp.exp(jnp.minimum(total_t[head : head + 1, :] - total[:, head : head + 1], 0.0))
            mixing.append((scores_t * fade).astype(BF16))
            scores_grad_t = scores_grad_t + mixing_grad[:, which * span : (which + 1) * span] * fade
        local.append(mm(jnp.concatenate(mixing, axis=1), halved))
    scaled_grad = jnp.concatenate(local, axis=1) + closed
    scores_grad_t = jnp.where(inside_t, scores_grad_t, 0.0).astype(BF16)
    kept_closing = (scaled * closing_wide).astype(BF16)
    reads_grad = mm(scores_grad_t.T, writes) + mm_t(entered, state_low)
    writes_grad = mm(scores_grad_t, reads) + mm_t(kept_closing, later_low)
    memory_grad[...] = later * keeping_wide + mm(reads.T, entered)
    skip = skip_ref[...]
    size_grad = head_sum(values * scaled_grad, spread)
    paid = head_sum(
        grad_low.astype(F32) * (out_ref[...] - skip * values) - scaled_low.astype(F32) * scaled_grad, spread
    )
    tail = jnp.sum(scaled_low.astype(F32) * closed, axis=0, keepdims=True) + keeping_wide * jnp.sum(
        later * state_low.astype(F32), axis=0, keepdims=True
    )
    tail = head_sum(jnp.broadcast_to(tail, (8, width)), spread)[0:1]
    total_grad = paid + jnp.where(place == base + span - 1, tail, 0.0)
    decay_grad = jnp.dot(upper, total_grad, precision=lax.Precision.HIGHEST, preferred_element_type=F32)
    raw_grad = (size_grad - decay_grad * head_ref[1:2]) * jax.nn.sigmoid(raw)
    proj_grad_ref[:, width:] = raw_grad.astype(proj_grad_ref.dtype)
    hsum_ref[0:1] += jnp.sum(raw_grad, axis=0, keepdims=True)
    hsum_ref[1:2] += jnp.sum(decay_grad * decay, axis=0, keepdims=True)
    conv_grad = (size_wide * scaled_grad + skip * grad) * slope
    shared_conv_grad = jnp.concatenate([writes_grad, reads_grad], axis=1) * shared_slope
    fsum_ref[reach : reach + 1] += jnp.sum(conv_grad, axis=0, keepdims=True)
    fsum_ref[reach + 1 : reach + 2] += jnp.sum(grad * values, axis=0, keepdims=True)
    ssum_ref[reach : reach + 1] += jnp.sum(shared_conv_grad, axis=0, keepdims=True)
    late = base + lax.broadcasted_iota(jnp.int32, (span + HALO, LANES), 0)
    late_allowed = permitted(late, start_of(late, lens_ref), reach, width)
    whole = jnp.concatenate([conv_grad, after[...]], axis=0)
    shared_whole = jnp.concatenate([shared_conv_grad, shared_after[...]], axis=0)
    result = fw_ref[0:1] * conv_grad
    shared_result = sf_ref[0:1] * shared_conv_grad
    fsum_ref[0:1] += jnp.sum(conv_grad * shifted[0], axis=0, keepdims=True)
    ssum_ref[0:1] += jnp.sum(shared_conv_grad * shared_shifted[0], axis=0, keepdims=True)
    for k in range(1, reach):
        masked = whole * late_allowed[k]
        fsum_ref[k : k + 1] += jnp.sum(masked[:span] * shifted[k], axis=0, keepdims=True)
        result = result + fw_ref[k : k + 1] * masked[k : k + span]
        masked = shared_whole * late_allowed[k]
        ssum_ref[k : k + 1] += jnp.sum(masked[:span] * shared_shifted[k], axis=0, keepdims=True)
        shared_result = shared_result + sf_ref[k : k + 1] * masked[k : k + span]
    after[...] = conv_grad[:HALO]
    shared_after[...] = shared_conv_grad[:HALO]
    proj_grad_ref[:, :width] = result.astype(proj_grad_ref.dtype)
    shared_grad_ref[...] = shared_result.astype(shared_grad_ref.dtype)


def head_rows(step_bias, decay_log, skip_gain, width):
    heads = step_bias.shape[0]
    table = jnp.zeros((8, LANES), F32)
    table = table.at[0, :heads].set(step_bias).at[1, :heads].set(jnp.exp(decay_log))
    skip = jnp.repeat(skip_gain, width // heads)[None, :]
    spread = (jnp.arange(LANES)[:, None] == (jnp.arange(width) // (width // heads))[None, :]).astype(BF16)
    return table, skip, spread


def fixed(shape):
    return pl.BlockSpec(shape, lambda *_: (0,) * len(shape))


def mixer_forward(lens, order, proj, fw, fb, sf, sb, table, skip, spread):
    rows = proj.shape[0]
    width = fw.shape[1]
    steps = rows // SPAN
    block = lambda cols: pl.BlockSpec((SPAN, cols), lambda i, lens_ref, order_ref: (order_ref[i], 0))
    return pl.pallas_call(
        forward_kernel,
        grid_spec=pltpu.PrefetchScalarGridSpec(
            num_scalar_prefetch=2,
            grid=(steps,),
            in_specs=[
                block(proj.shape[1]), fixed(fw.shape), fixed(fb.shape), fixed(sf.shape),
                fixed(sb.shape), fixed(table.shape), fixed(skip.shape), fixed(spread.shape),
            ],
            out_specs=[block(width), pl.BlockSpec((1, LANES, width), lambda i, *_: (i, 0, 0))],
            scratch_shapes=[
                pltpu.VMEM((LANES, width), F32),
                pltpu.VMEM((HALO, width), F32),
                pltpu.VMEM((HALO, sf.shape[1]), F32),
            ],
        ),
        out_shape=[
            jax.ShapeDtypeStruct((rows, width), F32),
            jax.ShapeDtypeStruct((steps, LANES, width), BF16),
        ],
        cost_estimate=pl.CostEstimate(flops=20 * 10**9, bytes_accessed=30 * 10**6, transcendentals=0),
        name="mixer_forward",
    )(lens, order, proj, fw, fb, sf, sb, table, skip, spread)


def mixer_backward(lens, order, proj, grad, out, kept, fw, fb, sf, sb, table, skip, spread):
    rows = proj.shape[0]
    width = fw.shape[1]
    steps = rows // SPAN
    lead = SPAN // HALO
    block = lambda cols: pl.BlockSpec((SPAN, cols), lambda i, lens_ref, order_ref: (order_ref[steps - 1 - i], 0))
    ahead = lambda cols: pl.BlockSpec(
        (HALO, cols),
        lambda i, lens_ref, order_ref: (order_ref[jnp.maximum(steps - 2 - i, 0)] * lead + lead - 1, 0),
    )
    return pl.pallas_call(
        backward_kernel,
        grid_spec=pltpu.PrefetchScalarGridSpec(
            num_scalar_prefetch=2,
            grid=(steps,),
            in_specs=[
                block(proj.shape[1]), ahead(proj.shape[1]),
                block(width), block(width), pl.BlockSpec((1, LANES, width), lambda i, *_: (steps - 1 - i, 0, 0)),
                fixed(fw.shape), fixed(fb.shape), fixed(sf.shape),
                fixed(sb.shape), fixed(table.shape), fixed(skip.shape), fixed(spread.shape),
            ],
            out_specs=[
                block(width + LANES), block(sf.shape[1]),
                fixed((8, width)), fixed((8, sf.shape[1])), fixed((8, LANES)),
            ],
            scratch_shapes=[
                pltpu.VMEM((LANES, width), F32),
                pltpu.VMEM((HALO, width), F32),
                pltpu.VMEM((HALO, sf.shape[1]), F32),
            ],
        ),
        out_shape=[
            jax.ShapeDtypeStruct((rows, width + LANES), BF16),
            jax.ShapeDtypeStruct((rows, sf.shape[1]), F32),
            jax.ShapeDtypeStruct((8, width), F32),
            jax.ShapeDtypeStruct((8, sf.shape[1]), F32),
            jax.ShapeDtypeStruct((8, LANES), F32),
        ],
        cost_estimate=pl.CostEstimate(flops=40 * 10**9, bytes_accessed=60 * 10**6, transcendentals=0),
        name="mixer_backward",
    )(lens, order, proj, proj, grad, out, kept, fw, fb, sf, sb, table, skip, spread)


def swap(v, axis, mask=1):
    count = lax.axis_size(axis)
    return lax.ppermute(v, axis, [(i, i ^ mask) for i in range(count)])


def crossed(v):
    pairs = [(a * 4 + b, b * 4 + a) for a in range(4) for b in range(4)]
    return lax.ppermute(v, ("side", "core", "tensor"), pairs)


def row_doubling(v):
    pieces = [v]
    while len(pieces) < lax.axis_size("row"):
        reach = len(pieces)
        pieces = pieces + [swap(p, "row", reach) for p in pieces]
    return pieces


SLOT_PLANES = ((0, 1, 2, 3), (1, 0, 2, 3), (2, 1, 3, 0), (3, 2, 1, 0))


def tie(*values):
    return lax.optimization_barrier(values)


def line_step(pair, j):
    left, right = pair
    return (
        lax.ppermute(left, "tensor", [(i, i + 1) for i in range(j - 1, 3)]),
        lax.ppermute(right, "tensor", [(i + 1, i) for i in range(0, 4 - j)]),
    )


def slot_one(one):
    return jnp.where(lax.axis_index("tensor") == 0, one[1], one[0])


def slot_two(one, two):
    plane = lax.axis_index("tensor")
    return jnp.where(plane == 0, two[1], jnp.where(plane == 3, two[0], one[1]))


def slot_three(two, three):
    plane = lax.axis_index("tensor")
    return jnp.where(
        plane == 0, three[1], jnp.where(plane == 1, two[1], jnp.where(plane == 2, two[0], three[0]))
    )


def summed(v, axes):
    for axis in axes:
        reach = 1
        while reach < lax.axis_size(axis):
            v = v + swap(v, axis, reach)
            reach = reach * 2
    return v


def row_scattered(v):
    row, reach = lax.axis_index("row"), lax.axis_size("row") // 2
    while reach:
        half = v.shape[0] // 2
        high = (row // reach) % 2
        kept = lax.dynamic_slice_in_dim(v, high * half, half, 0)
        given = lax.dynamic_slice_in_dim(v, (1 - high) * half, half, 0)
        v = (kept.astype(F32) + swap(given, "row", reach).astype(F32)).astype(BF16)
        reach = reach // 2
    return v


def contract_rows(a, b):
    return lax.dot_general(a, b, (((0,), (0,)), ((), ())), preferred_element_type=F32)


def contract_columns(a, b):
    return lax.dot_general(a, b, (((1,), (1,)), ((), ())), preferred_element_type=F32)


def on_device(
    tokens, cotangent, destination, lengths, norm_gain, inner_weight, shared_weight, step_weight, filter_weight,
    filter_bias, shared_filter, shared_filter_bias, step_bias, decay_log, skip_gain, gate_gain, out_weight,
):
    row_count, model_width = tokens.shape
    width = filter_weight.shape[1]
    heads = step_bias.shape[0]
    rows_n, planes = lax.axis_size("row"), lax.axis_size("tensor")
    row, side, core, plane = (lax.axis_index(a) for a in ("row", "side", "core", "tensor"))
    group_rows = row_count // (rows_n * 4)
    owned = rows_n * group_rows
    source = (row * 2 + side) * 2 + core

    wanted = jnp.concatenate(
        [
            ((row ^ d) * planes + plane) * row_count + source * group_rows + jnp.arange(group_rows, dtype=jnp.int32)
            for d in range(rows_n)
        ]
    )
    chosen = (wanted[:, None] == destination[None, :]).astype(BF16)

    def exchanged(sent):
        return jnp.concatenate([sent[:group_rows]] + [
            swap(sent[d * group_rows : (d + 1) * group_rows], "row", d) for d in range(1, rows_n)
        ])

    def gathered(own):
        beside = swap(own, "side")
        return jnp.concatenate([own, swap(own, "core"), beside, swap(beside, "core")])

    slot_planes = jnp.array(SLOT_PLANES, jnp.int32)[plane]

    def assembled(doubled):
        rows, columns = doubled[0][0].shape
        whole = jnp.zeros((planes * rows_n * rows, columns), BF16)
        for i, pieces in enumerate(doubled):
            for d, p in enumerate(pieces):
                whole = lax.dynamic_update_slice(whole, p, (((row ^ d) * planes + slot_planes[i]) * rows, 0))
        return whole

    picked = jnp.dot(chosen, tokens, preferred_element_type=F32).astype(BF16)
    step_low = jnp.pad(step_weight.astype(BF16), ((0, 0), (0, LANES - heads)))
    piece = jnp.concatenate([inner_weight[:, 1].astype(BF16), step_low, shared_weight.astype(BF16)], axis=1)
    gate_piece = jnp.concatenate([inner_weight[:, 0].astype(BF16), out_weight.astype(BF16)], axis=1)
    picked_cot = jnp.dot(chosen, cotangent, preferred_element_type=F32).astype(BF16)
    own_tokens, piece, picked_cot = tie(exchanged(picked), crossed(piece), picked_cot)
    own_cot = exchanged(picked_cot)
    one = line_step((piece, piece), 1)
    in_slots = [row_doubling(piece)]
    hidden = own_tokens.astype(F32)
    scale = lax.rsqrt(jnp.mean(hidden * hidden, axis=-1, keepdims=True) + EPSILON)
    own_normed = (hidden * scale * norm_gain).astype(BF16)
    beside, near = swap(own_normed, "side"), swap(own_normed, "core")
    one, near, gate_piece = tie(one, near, gate_piece)
    two = line_step(one, 2)
    gate_piece = crossed(gate_piece)
    in_slots = in_slots + [row_doubling(slot_one(one))]
    two, own_cot, in_slots = tie(two, own_cot, in_slots)
    three = line_step(two, 3)
    in_slots = in_slots + [row_doubling(slot_two(one, two))]
    three, beside, gate_piece, in_slots = tie(three, beside, gate_piece, in_slots)
    in_slots = in_slots + [row_doubling(slot_three(two, three))]
    far = swap(beside, "core")
    one = line_step((gate_piece, gate_piece), 1)
    cot_beside, cot_near = swap(own_cot, "side"), swap(own_cot, "core")
    in_slots, far, one = tie(in_slots, far, one)
    two = line_step(one, 2)
    gate_slots = [row_doubling(gate_piece), row_doubling(slot_one(one))]
    normed = jnp.concatenate([own_normed, near, beside, far])
    in_full = assembled(in_slots)

    params = jnp.concatenate(
        [
            filter_weight,
            filter_bias[None],
            gate_gain[None],
            jnp.pad(jnp.concatenate([step_bias, decay_log, skip_gain]), (0, width - 3 * heads))[None],
            jnp.pad(lengths.astype(F32), ((0, 0), (0, width - lengths.shape[1]))),
        ],
        axis=0,
    )
    params = crossed(params)
    fw, fb, gain = params[:4], params[4:5], params[5:6]
    bias_here, decay_here, skip_here = (params[6, i * heads : (i + 1) * heads] for i in range(3))
    lens = params[7, : lengths.shape[1]].astype(jnp.int32)
    sf, sb = shared_filter, shared_filter_bias[None]
    table, skip, spread = head_rows(bias_here, decay_here, skip_here, width)

    if group_rows % SPAN == 0:
        spans = jnp.arange(row_count // SPAN, dtype=jnp.int32)
        part = (spans * SPAN // group_rows) ^ source
        order = (((part // 2) % 2 * 2 + part % 2) * rows_n + part // 4) * (group_rows // SPAN)
        order = order + spans % (group_rows // SPAN)
        sequenced = unsequenced = lambda v: v
    else:
        order = jnp.arange(row_count // SPAN, dtype=jnp.int32)
        groups = jnp.arange(4 * rows_n, dtype=jnp.int32)
        part = groups ^ source
        to = ((part // 2) % 2 * 2 + part % 2) * rows_n + part // 4
        fro = (((groups % rows_n) * 4 + groups // rows_n) ^ source)
        sequenced = lambda v: v.reshape(4 * rows_n, group_rows, -1)[to].reshape(v.shape)
        unsequenced = lambda v: v.reshape(4 * rows_n, group_rows, -1)[fro].reshape(v.shape)

    def summed_over_group(v):
        v = v + swap(v, "core").reshape(2, 2, 2, owned)[:, :, ::-1].reshape(2, -1)
        return v + swap(v, "side").reshape(2, 2, 2 * owned)[:, ::-1].reshape(2, -1)

    def rows_of(v, dx, dk):
        return v[(dx * 2 + dk) * owned : (dx * 2 + dk + 1) * owned]

    def group_parts(part):
        return part(1, 1).astype(BF16), part(1, 0), part(0, 1).astype(BF16), part(0, 0)

    def group_sum(parts):
        far, side_part, near, own_part = parts
        beside = swap((side_part + swap(far, "core").astype(F32)).astype(BF16), "side")
        return own_part + swap(near, "core").astype(F32) + beside.astype(F32)

    block_of = destination // row_count
    row_of, plane_of = (block_of // planes) ^ row, block_of % planes
    slot = row_of * group_rows + destination - block_of * row_count - source * group_rows

    def settled(held, which):
        where = jnp.concatenate([jnp.where(plane_of == slot_planes[j], slot, -1)[:, None] == jnp.arange(owned)[None, :]
                                 for j in which], axis=1)
        return jnp.dot(where.astype(BF16), jnp.concatenate(held), preferred_element_type=F32).astype(BF16)

    proj = jnp.dot(normed, in_full, preferred_element_type=F32)
    proj, two, gate_slots, cot_near = tie(proj, two, gate_slots, cot_near)
    three = line_step(two, 3)
    gate_slots = gate_slots + [row_doubling(slot_two(one, two))]
    proj = sequenced(proj)
    mixed_seq, kept = mixer_forward(lens, order, proj, fw, fb, sf, sb, table, skip, spread)
    mixed_seq, three, gate_slots, cot_beside = tie(mixed_seq, three, gate_slots, cot_beside)
    both_full = assembled(gate_slots + [row_doubling(slot_three(two, three))])
    gate_full, out_full = both_full[:, :width], both_full[:, width:]
    cot = jnp.concatenate([own_cot, cot_near, cot_beside, swap(cot_beside, "core")])
    mixed = unsequenced(mixed_seq)
    gate_in = lax.optimization_barrier(jnp.dot(normed, gate_full, preferred_element_type=F32))
    normed_grad = lax.optimization_barrier(jnp.dot(cot, out_full, preferred_element_type=F32))
    gate_sig = jax.nn.sigmoid(gate_in)
    gate_act = gate_in * gate_sig
    gated = mixed * gate_act
    scaled_grad = normed_grad * gain
    sums = summed_over_group(jnp.stack([jnp.sum(gated * gated, axis=1), jnp.sum(scaled_grad * gated, axis=1)]))
    gate_scale = lax.rsqrt(sums[0] / (4 * width) + EPSILON)[:, None]
    gate_normed = (gated * gate_scale * gain).astype(BF16)
    far, side_part, near, own_part = group_parts(
        lambda dx, dk: contract_columns(rows_of(gate_normed, dx, dk), out_full)
    )
    sent = (side_part + swap(far, "core").astype(F32)).astype(BF16)
    own_rows = hidden + own_part + swap(near, "core").astype(F32)

    out_grad = contract_rows(cot, gate_normed).astype(BF16)
    gate_gain_grad = jnp.sum(normed_grad * gated * gate_scale, axis=0)
    gated_grad = gate_scale * scaled_grad - gated * gate_scale**3 * (sums[1] / (4 * width))[:, None]
    mixed_grad = gated_grad * gate_act
    gate_in_grad = (gated_grad * mixed * gate_sig * (1.0 + gate_in * (1.0 - gate_sig))).astype(BF16)
    gate_grad = contract_rows(normed, gate_in_grad).astype(BF16)
    both_grad = jnp.concatenate([gate_grad, out_grad], axis=1)
    mixed_grad, both_grad, sent, own_rows = lax.optimization_barrier((mixed_grad, both_grad, sent, own_rows))
    arrived = swap(sent, "side")
    both_grad = lax.psum_scatter(both_grad, ("row", "tensor"), scatter_dimension=0, tiled=True)
    proj_grad, shared_part, fsum, ssum, hsum = mixer_backward(
        lens, order, proj, sequenced(mixed_grad), mixed_seq, kept, fw, fb, sf, sb, table, skip, spread
    )
    proj_grad, shared_part = unsequenced(proj_grad), unsequenced(shared_part)
    proj_grad, shared_part, arrived = lax.optimization_barrier((proj_grad, shared_part, arrived))
    out_rows = exchanged((own_rows + arrived.astype(F32)).astype(BF16))

    def back_part(grads, dx, dk):
        gate_part, proj_part = grads
        return contract_columns(rows_of(gate_part, dx, dk), gate_full) + contract_columns(
            rows_of(proj_part, dx, dk), in_full[:, : width + LANES]
        )

    shared_far, shared_side, shared_near, shared_own = group_parts(lambda dx, dk: rows_of(shared_part, dx, dk))
    own_shared = group_sum((shared_far, shared_side, shared_near, shared_own)).astype(BF16)
    far = swap(back_part((gate_in_grad, proj_grad), 1, 1).astype(BF16), "core")
    near = swap(back_part((gate_in_grad, proj_grad), 0, 1).astype(BF16), "core")
    far, gate_later, proj_later, out_rows = lax.optimization_barrier((far, gate_in_grad, proj_grad, out_rows))
    out_one = line_step((out_rows, out_rows), 1)
    sent = (back_part((gate_later, proj_later), 1, 0) + far.astype(F32)).astype(BF16)
    own_back = back_part((gate_later, proj_later), 0, 0) + near.astype(F32)
    beside = swap(sent, "side")
    in_grad = contract_rows(normed, jnp.concatenate([proj_later, gathered(own_shared)], axis=1)).astype(BF16)
    in_grad, out_one, both_grad, own_back = lax.optimization_barrier((in_grad, out_one, both_grad, own_back))
    out_two = line_step(out_one, 2)
    both_grad = crossed(both_grad)
    in_grad = lax.psum_scatter(row_scattered(in_grad), "tensor", scatter_dimension=0, tiled=True)
    normed_back = own_back + beside.astype(F32) + contract_columns(own_shared, in_full[:, width + LANES :])
    norm_gain_grad = jnp.sum(normed_back * hidden * scale, axis=0)
    gained = normed_back * norm_gain
    along = jnp.mean(gained * hidden, axis=1, keepdims=True)
    input_work = own_cot.astype(F32) + scale * gained - hidden * (scale**3 * along)
    line = lambda v: jnp.pad(v, (0, -v.shape[0] % width)).reshape(-1, width)
    skip_grad = fsum[5].reshape(heads, -1).sum(axis=1)
    small = jnp.concatenate(
        [
            fsum[:5],
            gate_gain_grad[None],
            jnp.pad(jnp.concatenate([hsum[0, :heads], hsum[1, :heads], skip_grad]), (0, width - 3 * heads))[None],
            jnp.zeros((1, width), F32),
            line(norm_gain_grad),
            line(ssum[:5].reshape(-1)),
        ],
        axis=0,
    )
    back_rows, small = tie(input_work.astype(BF16), small)
    back_rows = exchanged(back_rows)
    small = summed(small, ("row",))
    small = jnp.concatenate([small[:8], summed(small[8:], ("core", "side"))], axis=0)
    back_rows, out_two, small, both_grad = tie(back_rows, out_two, small, both_grad)
    back_one = line_step((back_rows, back_rows), 1)
    out_three = line_step(out_two, 3)
    back_two = line_step(back_one, 2)
    back_two, in_grad = tie(back_two, in_grad)
    back_three = line_step(back_two, 3)
    out_three, _ = tie(out_three, back_two)
    layer_out = settled([out_rows, slot_one(out_one)], (0, 1))
    layer_out = layer_out + settled([slot_two(out_one, out_two), slot_three(out_two, out_three)], (2, 3))
    input_grad = settled([back_rows, slot_one(back_one)], (0, 1))
    layer_out, input_grad, back_three, small = tie(layer_out, input_grad, back_three, small)
    input_grad = input_grad + settled([slot_two(back_one, back_two), slot_three(back_two, back_three)], (2, 3))
    small = small + swap(small, "tensor", 1)
    small = small + swap(small, "tensor", 2)
    mine, common = crossed(small[:8]), small[8:]
    in_grad = crossed(in_grad).astype(F32)
    inner_grad = jnp.stack([both_grad[:, :width].astype(F32), in_grad[:, :width]], axis=1)

    lines = line(norm_gain_grad).shape[0]
    norm_gain_grad = common[:lines].reshape(-1)[:model_width]
    shared_sums = common[lines:].reshape(-1)[: 5 * sf.shape[1]].reshape(5, -1)
    return (
        layer_out, input_grad, norm_gain_grad, inner_grad, in_grad[:, width + LANES :],
        in_grad[:, width : width + heads], mine[:4], mine[4], shared_sums[:4], shared_sums[4],
        mine[6, :heads], mine[6, heads : 2 * heads], mine[6, 2 * heads : 3 * heads], mine[5], both_grad[:, width:].astype(F32),
    )


def solution(mesh):
    count, planes = mesh.devices.shape
    assert planes == 4 and count % 4 == 0
    names = ("row", "side", "core", "tensor")
    inner = jax.sharding.Mesh(mesh.devices.reshape(count // 4, 2, 2, planes), names)
    dp = ("row", "side", "core")
    in_specs = (
        P(dp, None), P(dp, None), P(dp), P(dp, None), P(), P(dp, None, "tensor"), P(dp, None), P(dp, "tensor"),
        P(None, "tensor"), P("tensor"), P(), P(), P("tensor"), P("tensor"), P("tensor"), P("tensor"), P(dp, "tensor"),
    )
    out_specs = (
        P(dp, None), P(dp, None), P(), P(dp, None, "tensor"), P(dp, None), P(dp, "tensor"),
        P(None, "tensor"), P("tensor"), P(), P(), P("tensor"), P("tensor"), P("tensor"), P("tensor"), P(dp, "tensor"),
    )
    return jax.shard_map(on_device, mesh=inner, in_specs=in_specs, out_specs=out_specs, check_vma=False)
```

```python
import functools

import jax
import jax.numpy as jnp
from jax import lax
from jax.experimental import pallas as pl
from jax.experimental.pallas import tpu as pltpu
from jax.sharding import PartitionSpec as P

SPAN = 128
HALO = 8
LANES = 128
F32 = jnp.float32
BF16 = jnp.bfloat16
EPSILON = 1e-05


def mm(a, b):
    return jnp.dot(a, b, preferred_element_type=F32)


def mm_t(a, b):
    return lax.dot_general(a, b, (((1,), (1,)), ((), ())), preferred_element_type=F32)


def halves(v):
    high = v.astype(BF16)
    return high, (v - high.astype(F32)).astype(BF16)


def widen(v, spread):
    high, rest = halves(v)
    return mm(high, spread) + mm(rest, spread)


def head_sum(v, spread):
    high, rest = halves(v)
    return mm_t(high, spread) + mm_t(rest, spread)


def start_of(place, lens_ref):
    end, start = jnp.int32(0), jnp.zeros_like(place)
    for i in range(lens_ref.shape[0]):
        start = jnp.where(place >= end, end, start)
        end = end + lens_ref[i]
    return start


def taps(current, before, reach):
    whole = jnp.concatenate([before, current], axis=0)
    rows = current.shape[0]
    return [whole[HALO - k : HALO - k + rows] for k in range(reach)]


def filtered(shifted, allowed, kernel, bias):
    result = bias + kernel[0:1] * shifted[0]
    for k in range(1, len(shifted)):
        result = result + kernel[k : k + 1] * shifted[k] * allowed[k]
    return result


def permitted(place, start, reach, width):
    flags = [None]
    for k in range(1, reach):
        flags.append(jnp.where(place - k >= start, 1.0, 0.0)[:, :1])
    return flags


def softplus(v):
    return jnp.maximum(v, 0.0) + jnp.log1p(jnp.exp(-jnp.abs(v)))


def chunk_setup(base, lens_ref, span):
    place = base + lax.broadcasted_iota(jnp.int32, (span, LANES), 0)
    start = start_of(place, lens_ref)
    last_start = start_of(jnp.full((1, LANES), base + span - 1, jnp.int32), lens_ref)
    return place, start, last_start


def stacked(pair, low_lanes):
    zero = jnp.zeros_like(pair)
    return jnp.concatenate([jnp.where(low_lanes, pair, zero), jnp.where(low_lanes, zero, pair)], axis=0)


def forward_kernel(
    lens_ref, order_ref, proj_ref, fw_ref, fb_ref, sf_ref, sb_ref, head_ref, skip_ref, spread_ref,
    out_ref, kept_ref, memory, before, shared_before,
):
    step = pl.program_id(0)
    span = proj_ref.shape[0]
    width = out_ref.shape[1]
    reach = fw_ref.shape[0]
    pairs = width // LANES
    base = step * span

    @pl.when(step == 0)
    def _():
        memory[...] = jnp.zeros_like(memory)
        before[...] = jnp.zeros_like(before)
        shared_before[...] = jnp.zeros_like(shared_before)

    place, start, last_start = chunk_setup(base, lens_ref, span)
    allowed = permitted(place, start, reach, width)
    inputs = proj_ref[:, :width]
    shared = proj_ref[:, width + LANES :]
    conv = filtered(taps(inputs, before[...], reach), allowed, fw_ref, fb_ref[...])
    values = conv * jax.nn.sigmoid(conv)
    conv = filtered(taps(shared, shared_before[...], reach), allowed, sf_ref, sb_ref[...])
    factors = conv * jax.nn.sigmoid(conv)
    before[...] = inputs[span - HALO :]
    shared_before[...] = shared[span - HALO :]
    writes = factors[:, :LANES].astype(BF16)
    reads = factors[:, LANES:].astype(BF16)
    size = softplus(proj_ref[:, width : width + LANES] + head_ref[0:1])
    decay = -size * head_ref[1:2]
    row = lax.broadcasted_iota(jnp.int32, (span, span), 0)
    col = lax.broadcasted_iota(jnp.int32, (span, span), 1)
    lower = jnp.where(row >= col, 1.0, 0.0)
    total = jnp.dot(lower, decay, precision=lax.Precision.HIGHEST, preferred_element_type=F32)
    total_t = total.T
    inside = (col <= row) & (col + base >= start)
    scores = jnp.where(inside, mm_t(reads, writes), 0.0)
    spread = spread_ref[...]
    scaled = values * widen(size, spread)
    scaled_low = scaled.astype(BF16)
    entering = jnp.exp(total) * jnp.where(start < base, 1.0, 0.0)
    state = memory[...]
    state_low = state.astype(BF16)
    kept_ref[0] = state_low
    remote = mm(reads, state_low) * widen(entering, spread) + skip_ref[...] * values
    low_lanes = lax.broadcasted_iota(jnp.int32, (span, LANES), 1) < LANES // 2
    for pair in range(pairs):
        lanes = slice(pair * LANES, (pair + 1) * LANES)
        mixing = []
        for head in (2 * pair, 2 * pair + 1):
            fade = jnp.exp(jnp.minimum(total[:, head : head + 1] - total_t[head : head + 1, :], 0.0))
            mixing.append((scores * fade).astype(BF16))
        local = mm(jnp.concatenate(mixing, axis=1), stacked(scaled_low[:, lanes], low_lanes))
        out_ref[:, lanes] = (local + remote[:, lanes]).astype(out_ref.dtype)
    end = total[span - 1 : span]
    closing = jnp.exp(end - total) * jnp.where(place >= last_start, 1.0, 0.0)
    added = mm(writes.T, (scaled * widen(closing, spread)).astype(BF16))
    keeping = jnp.exp(end) * jnp.where(last_start < base, 1.0, 0.0)
    memory[...] = state * widen(jnp.broadcast_to(keeping, (8, LANES)), spread)[0:1] + added


def backward_kernel(
    first_chunk, lens_ref, order_ref, proj_ref, proj_before_ref, grad_ref, out_ref, kept_ref,
    fw_ref, fb_ref, sf_ref, sb_ref, head_ref, skip_ref, spread_ref,
    memory_from, after_from, shared_after_from, proj_grad_from, shared_grad_from,
    proj_grad_ref, shared_grad_ref, fsum_ref, ssum_ref, hsum_ref, memory_grad, after, shared_after,
):
    step = pl.program_id(0)
    span = proj_ref.shape[0]
    width = out_ref.shape[1]
    reach = fw_ref.shape[0]
    pairs = width // LANES
    chunk = first_chunk - step
    base = chunk * span

    @pl.when(step == 0)
    def _():
        memory_grad[...] = memory_from[...]
        after[...] = after_from[...]
        shared_after[...] = shared_after_from[...]
        fsum_ref[...] = jnp.zeros_like(fsum_ref)
        ssum_ref[...] = jnp.zeros_like(ssum_ref)
        hsum_ref[...] = jnp.zeros_like(hsum_ref)

    place, start, last_start = chunk_setup(base, lens_ref, span)
    allowed = permitted(place, start, reach, width)
    first = jnp.where(chunk > 0, 1.0, 0.0)
    inputs = proj_ref[:, :width]
    shifted = taps(inputs, proj_before_ref[:, :width] * first, reach)
    conv = filtered(shifted, allowed, fw_ref, fb_ref[...])
    gate = jax.nn.sigmoid(conv)
    values = conv * gate
    slope = gate * (1.0 + conv * (1.0 - gate))
    shared_shifted = taps(proj_ref[:, width + LANES :], proj_before_ref[:, width + LANES :] * first, reach)
    conv = filtered(shared_shifted, allowed, sf_ref, sb_ref[...])
    gate = jax.nn.sigmoid(conv)
    factors = conv * gate
    shared_slope = gate * (1.0 + conv * (1.0 - gate))
    writes = factors[:, :LANES].astype(BF16)
    reads = factors[:, LANES:].astype(BF16)
    raw = proj_ref[:, width : width + LANES] + head_ref[0:1]
    size = softplus(raw)
    decay = -size * head_ref[1:2]
    row = lax.broadcasted_iota(jnp.int32, (span, span), 0)
    col = lax.broadcasted_iota(jnp.int32, (span, span), 1)
    lower = jnp.where(row >= col, 1.0, 0.0)
    upper = jnp.where(row <= col, 1.0, 0.0)
    total = jnp.dot(lower, decay, precision=lax.Precision.HIGHEST, preferred_element_type=F32)
    total_t = total.T
    start_t = start_of(base + col[0:1], lens_ref)
    inside_t = (row <= col) & (row + base >= start_t)
    scores_t = jnp.where(inside_t, mm_t(writes, reads), 0.0)
    spread = spread_ref[...]
    size_wide = widen(size, spread)
    scaled = values * size_wide
    scaled_low = scaled.astype(BF16)
    grad = grad_ref[...].astype(F32)
    grad_low = grad.astype(BF16)
    state_low = kept_ref[0]
    later = memory_grad[...]
    later_low = later.astype(BF16)
    entering = jnp.exp(total) * jnp.where(start < base, 1.0, 0.0)
    entered = (grad * widen(entering, spread)).astype(BF16)
    end = total[span - 1 : span]
    closing = jnp.exp(end - total) * jnp.where(place >= last_start, 1.0, 0.0)
    closing_wide = widen(closing, spread)
    keeping = jnp.exp(end) * jnp.where(last_start < base, 1.0, 0.0)
    keeping_wide = widen(jnp.broadcast_to(keeping, (8, LANES)), spread)[0:1]
    closed = mm(writes, later_low) * closing_wide
    low_lanes = lax.broadcasted_iota(jnp.int32, (span, LANES), 1) < LANES // 2
    scores_grad_t = jnp.zeros((span, span), F32)
    local = []
    for pair in range(pairs):
        lanes = slice(pair * LANES, (pair + 1) * LANES)
        halved = stacked(grad_low[:, lanes], low_lanes)
        mixing_grad = mm_t(scaled_low[:, lanes], halved)
        mixing = []
        for which, head in enumerate((2 * pair, 2 * pair + 1)):
            fade = jnp.exp(jnp.minimum(total_t[head : head + 1, :] - total[:, head : head + 1], 0.0))
            mixing.append((scores_t * fade).astype(BF16))
            scores_grad_t = scores_grad_t + mixing_grad[:, which * span : (which + 1) * span] * fade
        local.append(mm(jnp.concatenate(mixing, axis=1), halved))
    scaled_grad = jnp.concatenate(local, axis=1) + closed
    scores_grad_t = jnp.where(inside_t, scores_grad_t, 0.0).astype(BF16)
    kept_closing = (scaled * closing_wide).astype(BF16)
    reads_grad = mm(scores_grad_t.T, writes) + mm_t(entered, state_low)
    writes_grad = mm(scores_grad_t, reads) + mm_t(kept_closing, later_low)
    memory_grad[...] = later * keeping_wide + mm(reads.T, entered)
    skip = skip_ref[...]
    size_grad = head_sum(values * scaled_grad, spread)
    paid = head_sum(
        grad_low.astype(F32) * (out_ref[...] - skip * values) - scaled_low.astype(F32) * scaled_grad, spread
    )
    tail = jnp.sum(scaled_low.astype(F32) * closed, axis=0, keepdims=True) + keeping_wide * jnp.sum(
        later * state_low.astype(F32), axis=0, keepdims=True
    )
    tail = head_sum(jnp.broadcast_to(tail, (8, width)), spread)[0:1]
    total_grad = paid + jnp.where(place == base + span - 1, tail, 0.0)
    decay_grad = jnp.dot(upper, total_grad, precision=lax.Precision.HIGHEST, preferred_element_type=F32)
    raw_grad = (size_grad - decay_grad * head_ref[1:2]) * jax.nn.sigmoid(raw)
    proj_grad_ref[:, width:] = raw_grad.astype(proj_grad_ref.dtype)
    hsum_ref[0:1] += jnp.sum(raw_grad, axis=0, keepdims=True)
    hsum_ref[1:2] += jnp.sum(decay_grad * decay, axis=0, keepdims=True)
    conv_grad = (size_wide * scaled_grad + skip * grad) * slope
    shared_conv_grad = jnp.concatenate([writes_grad, reads_grad], axis=1) * shared_slope
    fsum_ref[reach : reach + 1] += jnp.sum(conv_grad, axis=0, keepdims=True)
    fsum_ref[reach + 1 : reach + 2] += jnp.sum(grad * values, axis=0, keepdims=True)
    ssum_ref[reach : reach + 1] += jnp.sum(shared_conv_grad, axis=0, keepdims=True)
    late = base + lax.broadcasted_iota(jnp.int32, (span + HALO, LANES), 0)
    late_allowed = permitted(late, start_of(late, lens_ref), reach, width)
    whole = jnp.concatenate([conv_grad, after[...]], axis=0)
    shared_whole = jnp.concatenate([shared_conv_grad, shared_after[...]], axis=0)
    result = fw_ref[0:1] * conv_grad
    shared_result = sf_ref[0:1] * shared_conv_grad
    fsum_ref[0:1] += jnp.sum(conv_grad * shifted[0], axis=0, keepdims=True)
    ssum_ref[0:1] += jnp.sum(shared_conv_grad * shared_shifted[0], axis=0, keepdims=True)
    for k in range(1, reach):
        masked = whole * late_allowed[k]
        fsum_ref[k : k + 1] += jnp.sum(masked[:span] * shifted[k], axis=0, keepdims=True)
        result = result + fw_ref[k : k + 1] * masked[k : k + span]
        masked = shared_whole * late_allowed[k]
        ssum_ref[k : k + 1] += jnp.sum(masked[:span] * shared_shifted[k], axis=0, keepdims=True)
        shared_result = shared_result + sf_ref[k : k + 1] * masked[k : k + span]
    after[...] = conv_grad[:HALO]
    shared_after[...] = shared_conv_grad[:HALO]
    proj_grad_ref[:, :width] = result.astype(proj_grad_ref.dtype)
    shared_grad_ref[...] = shared_result.astype(shared_grad_ref.dtype)


def head_rows(step_bias, decay_log, skip_gain, width):
    heads = step_bias.shape[0]
    table = jnp.zeros((8, LANES), F32)
    table = table.at[0, :heads].set(step_bias).at[1, :heads].set(jnp.exp(decay_log))
    skip = jnp.repeat(skip_gain, width // heads)[None, :]
    spread = (jnp.arange(LANES)[:, None] == (jnp.arange(width) // (width // heads))[None, :]).astype(BF16)
    return table, skip, spread


def fixed(shape):
    return pl.BlockSpec(shape, lambda *_: (0,) * len(shape))


def mixer_forward(lens, order, proj, fw, fb, sf, sb, table, skip, spread):
    rows = proj.shape[0]
    width = fw.shape[1]
    steps = rows // SPAN
    block = lambda cols: pl.BlockSpec((SPAN, cols), lambda i, lens_ref, order_ref: (order_ref[i], 0))
    return pl.pallas_call(
        forward_kernel,
        grid_spec=pltpu.PrefetchScalarGridSpec(
            num_scalar_prefetch=2,
            grid=(steps,),
            in_specs=[
                block(proj.shape[1]), fixed(fw.shape), fixed(fb.shape), fixed(sf.shape),
                fixed(sb.shape), fixed(table.shape), fixed(skip.shape), fixed(spread.shape),
            ],
            out_specs=[block(width), pl.BlockSpec((1, LANES, width), lambda i, *_: (i, 0, 0))],
            scratch_shapes=[
                pltpu.VMEM((LANES, width), F32),
                pltpu.VMEM((HALO, width), F32),
                pltpu.VMEM((HALO, sf.shape[1]), F32),
            ],
        ),
        out_shape=[
            jax.ShapeDtypeStruct((rows, width), F32),
            jax.ShapeDtypeStruct((steps, LANES, width), BF16),
        ],
        cost_estimate=pl.CostEstimate(flops=20 * 10**9, bytes_accessed=30 * 10**6, transcendentals=0),
        name="mixer_forward",
    )(lens, order, proj, fw, fb, sf, sb, table, skip, spread)


def mixer_backward(half, carried, lens, order, proj, grad, out, kept, fw, fb, sf, sb, table, skip, spread):
    rows = proj.shape[0]
    width = fw.shape[1]
    steps = rows // SPAN // 2
    first_chunk = (2 - half) * steps - 1
    lead = SPAN // HALO
    block = lambda cols: pl.BlockSpec((SPAN, cols), lambda i, lens_ref, order_ref: (order_ref[first_chunk - i], 0))
    ahead = lambda cols: pl.BlockSpec(
        (HALO, cols),
        lambda i, lens_ref, order_ref: (order_ref[jnp.maximum(first_chunk - 1 - i, 0)] * lead + lead - 1, 0),
    )
    anywhere = pl.BlockSpec(memory_space=pl.ANY)
    out_shape = [
        jax.ShapeDtypeStruct((rows, width + LANES), BF16),
        jax.ShapeDtypeStruct((rows, sf.shape[1]), F32),
        jax.ShapeDtypeStruct((8, width), F32),
        jax.ShapeDtypeStruct((8, sf.shape[1]), F32),
        jax.ShapeDtypeStruct((8, LANES), F32),
        jax.ShapeDtypeStruct((LANES, width), F32),
        jax.ShapeDtypeStruct((HALO, width), F32),
        jax.ShapeDtypeStruct((HALO, sf.shape[1]), F32),
    ]
    if carried is None:
        carried = [jnp.zeros(v.shape, F32) for v in out_shape[5:]] + [jnp.zeros((8, LANES), F32)] * 2
        aliases = {}
    else:
        aliases = {17: 0, 18: 1}
    return pl.pallas_call(
        functools.partial(backward_kernel, first_chunk),
        grid_spec=pltpu.PrefetchScalarGridSpec(
            num_scalar_prefetch=2,
            grid=(steps,),
            in_specs=[
                block(proj.shape[1]), ahead(proj.shape[1]),
                block(width), block(width),
                pl.BlockSpec((1, LANES, width), lambda i, *_: (first_chunk - i, 0, 0)),
                fixed(fw.shape), fixed(fb.shape), fixed(sf.shape),
                fixed(sb.shape), fixed(table.shape), fixed(skip.shape), fixed(spread.shape),
                fixed((LANES, width)), fixed((HALO, width)), fixed((HALO, sf.shape[1])), anywhere, anywhere,
            ],
            out_specs=[
                block(width + LANES), block(sf.shape[1]),
                fixed((8, width)), fixed((8, sf.shape[1])), fixed((8, LANES)),
                fixed((LANES, width)), fixed((HALO, width)), fixed((HALO, sf.shape[1])),
            ],
        ),
        out_shape=out_shape,
        input_output_aliases=aliases,
        cost_estimate=pl.CostEstimate(flops=20 * 10**9, bytes_accessed=30 * 10**6, transcendentals=0),
        name="mixer_backward",
    )(lens, order, proj, proj, grad, out, kept, fw, fb, sf, sb, table, skip, spread, *carried)


def swap(v, axis, mask=1):
    count = lax.axis_size(axis)
    return lax.ppermute(v, axis, [(i, i ^ mask) for i in range(count)])


def crossed(v):
    pairs = [(a * 4 + b, b * 4 + a) for a in range(4) for b in range(4)]
    return lax.ppermute(v, ("side", "core", "tensor"), pairs)


def row_doubling(v):
    pieces = [v]
    while len(pieces) < lax.axis_size("row"):
        reach = len(pieces)
        pieces = pieces + [swap(p, "row", reach) for p in pieces]
    return pieces


SLOT_PLANES = ((0, 1, 2, 3), (1, 0, 2, 3), (2, 1, 3, 0), (3, 2, 1, 0))


def tie(*values):
    return lax.optimization_barrier(values)


def line_step(pair, j):
    left, right = pair
    return (
        lax.ppermute(left, "tensor", [(i, i + 1) for i in range(j - 1, 3)]),
        lax.ppermute(right, "tensor", [(i + 1, i) for i in range(0, 4 - j)]),
    )


def slot_one(one):
    return jnp.where(lax.axis_index("tensor") == 0, one[1], one[0])


def slot_two(one, two):
    plane = lax.axis_index("tensor")
    return jnp.where(plane == 0, two[1], jnp.where(plane == 3, two[0], one[1]))


def slot_three(two, three):
    plane = lax.axis_index("tensor")
    return jnp.where(
        plane == 0, three[1], jnp.where(plane == 1, two[1], jnp.where(plane == 2, two[0], three[0]))
    )


def summed(v, axes):
    for axis in axes:
        reach = 1
        while reach < lax.axis_size(axis):
            v = v + swap(v, axis, reach)
            reach = reach * 2
    return v


def row_scattered(v):
    row, reach = lax.axis_index("row"), lax.axis_size("row") // 2
    while reach:
        half = v.shape[0] // 2
        high = (row // reach) % 2
        kept = lax.dynamic_slice_in_dim(v, high * half, half, 0)
        given = lax.dynamic_slice_in_dim(v, (1 - high) * half, half, 0)
        v = (kept.astype(F32) + swap(given, "row", reach).astype(F32)).astype(BF16)
        reach = reach // 2
    return v


def contract_rows(a, b):
    return lax.dot_general(a, b, (((0,), (0,)), ((), ())), preferred_element_type=F32)


def contract_columns(a, b):
    return lax.dot_general(a, b, (((1,), (1,)), ((), ())), preferred_element_type=F32)


def on_device(
    tokens, cotangent, destination, lengths, norm_gain, inner_weight, shared_weight, step_weight, filter_weight,
    filter_bias, shared_filter, shared_filter_bias, step_bias, decay_log, skip_gain, gate_gain, out_weight,
):
    row_count, model_width = tokens.shape
    width = filter_weight.shape[1]
    heads = step_bias.shape[0]
    rows_n, planes = lax.axis_size("row"), lax.axis_size("tensor")
    row, side, core, plane = (lax.axis_index(a) for a in ("row", "side", "core", "tensor"))
    group_rows = row_count // (rows_n * 4)
    owned = rows_n * group_rows
    source = (row * 2 + side) * 2 + core

    wanted = jnp.concatenate(
        [
            ((row ^ d) * planes + plane) * row_count + source * group_rows + jnp.arange(group_rows, dtype=jnp.int32)
            for d in range(rows_n)
        ]
    )
    chosen = (wanted[:, None] == destination[None, :]).astype(BF16)

    def exchanged(sent):
        return jnp.concatenate([sent[:group_rows]] + [
            swap(sent[d * group_rows : (d + 1) * group_rows], "row", d) for d in range(1, rows_n)
        ])

    def gathered(own):
        beside = swap(own, "side")
        return jnp.concatenate([own, swap(own, "core"), beside, swap(beside, "core")])

    slot_planes = jnp.array(SLOT_PLANES, jnp.int32)[plane]

    def assembled(doubled):
        rows, columns = doubled[0][0].shape
        whole = jnp.zeros((planes * rows_n * rows, columns), BF16)
        for i, pieces in enumerate(doubled):
            for d, p in enumerate(pieces):
                whole = lax.dynamic_update_slice(whole, p, (((row ^ d) * planes + slot_planes[i]) * rows, 0))
        return whole

    picked = jnp.dot(chosen, tokens, preferred_element_type=F32).astype(BF16)
    step_low = jnp.pad(step_weight.astype(BF16), ((0, 0), (0, LANES - heads)))
    piece = jnp.concatenate([inner_weight[:, 1].astype(BF16), step_low, shared_weight.astype(BF16)], axis=1)
    gate_piece = jnp.concatenate([inner_weight[:, 0].astype(BF16), out_weight.astype(BF16)], axis=1)
    picked_cot = jnp.dot(chosen, cotangent, preferred_element_type=F32).astype(BF16)
    own_tokens, piece, picked_cot = tie(exchanged(picked), crossed(piece), picked_cot)
    own_cot = exchanged(picked_cot)
    one = line_step((piece, piece), 1)
    in_slots = [row_doubling(piece)]
    hidden = own_tokens.astype(F32)
    scale = lax.rsqrt(jnp.mean(hidden * hidden, axis=-1, keepdims=True) + EPSILON)
    own_normed = (hidden * scale * norm_gain).astype(BF16)
    beside, near = swap(own_normed, "side"), swap(own_normed, "core")
    one, near, gate_piece = tie(one, near, gate_piece)
    two = line_step(one, 2)
    gate_piece = crossed(gate_piece)
    in_slots = in_slots + [row_doubling(slot_one(one))]
    two, own_cot, in_slots = tie(two, own_cot, in_slots)
    three = line_step(two, 3)
    in_slots = in_slots + [row_doubling(slot_two(one, two))]
    three, beside, gate_piece, in_slots = tie(three, beside, gate_piece, in_slots)
    in_slots = in_slots + [row_doubling(slot_three(two, three))]
    far = swap(beside, "core")
    one = line_step((gate_piece, gate_piece), 1)
    in_slots, far, one = tie(in_slots, far, one)
    two = line_step(one, 2)
    gate_slots = [row_doubling(gate_piece), row_doubling(slot_one(one))]
    normed = jnp.concatenate([own_normed, near, beside, far])
    in_full = assembled(in_slots)

    params = jnp.concatenate(
        [
            filter_weight,
            filter_bias[None],
            gate_gain[None],
            jnp.pad(jnp.concatenate([step_bias, decay_log, skip_gain]), (0, width - 3 * heads))[None],
            jnp.pad(lengths.astype(F32), ((0, 0), (0, width - lengths.shape[1]))),
        ],
        axis=0,
    )
    params = crossed(params)
    fw, fb, gain = params[:4], params[4:5], params[5:6]
    bias_here, decay_here, skip_here = (params[6, i * heads : (i + 1) * heads] for i in range(3))
    lens = params[7, : lengths.shape[1]].astype(jnp.int32)
    sf, sb = shared_filter, shared_filter_bias[None]
    table, skip, spread = head_rows(bias_here, decay_here, skip_here, width)

    if group_rows % SPAN == 0:
        spans = jnp.arange(row_count // SPAN, dtype=jnp.int32)
        part = (spans * SPAN // group_rows) ^ source
        order = (((part // 2) % 2 * 2 + part % 2) * rows_n + part // 4) * (group_rows // SPAN)
        order = order + spans % (group_rows // SPAN)
        sequenced = unsequenced = lambda v: v
    else:
        order = jnp.arange(row_count // SPAN, dtype=jnp.int32)
        groups = jnp.arange(4 * rows_n, dtype=jnp.int32)
        part = groups ^ source
        to = ((part // 2) % 2 * 2 + part % 2) * rows_n + part // 4
        fro = (((groups % rows_n) * 4 + groups // rows_n) ^ source)
        sequenced = lambda v: v.reshape(4 * rows_n, group_rows, -1)[to].reshape(v.shape)
        unsequenced = lambda v: v.reshape(4 * rows_n, group_rows, -1)[fro].reshape(v.shape)

    def summed_over_group(v):
        v = v + swap(v, "core").reshape(2, 2, 2, owned)[:, :, ::-1].reshape(2, -1)
        return v + swap(v, "side").reshape(2, 2, 2 * owned)[:, ::-1].reshape(2, -1)

    def rows_of(v, dx, dk):
        return v[(dx * 2 + dk) * owned : (dx * 2 + dk + 1) * owned]

    def group_parts(part):
        return part(1, 1).astype(BF16), part(1, 0), part(0, 1).astype(BF16), part(0, 0)

    def group_sum(parts):
        far, side_part, near, own_part = parts
        beside = swap((side_part + swap(far, "core").astype(F32)).astype(BF16), "side")
        return own_part + swap(near, "core").astype(F32) + beside.astype(F32)

    block_of = destination // row_count
    row_of, plane_of = (block_of // planes) ^ row, block_of % planes
    slot = row_of * group_rows + destination - block_of * row_count - source * group_rows

    def settled(held, which):
        where = jnp.concatenate([jnp.where(plane_of == slot_planes[j], slot, -1)[:, None] == jnp.arange(owned)[None, :]
                                 for j in which], axis=1)
        return jnp.dot(where.astype(BF16), jnp.concatenate(held), preferred_element_type=F32).astype(BF16)

    proj = jnp.dot(normed, in_full, preferred_element_type=F32)
    proj, two, gate_slots, own_cot = tie(proj, two, gate_slots, own_cot)
    cot_beside, cot_near = swap(own_cot, "side"), swap(own_cot, "core")
    three = line_step(two, 3)
    gate_slots = gate_slots + [row_doubling(slot_two(one, two))]
    proj = sequenced(proj)
    mixed_seq, kept = mixer_forward(lens, order, proj, fw, fb, sf, sb, table, skip, spread)
    mixed_seq, three, gate_slots, cot_beside = tie(mixed_seq, three, gate_slots, cot_beside)
    both_full = assembled(gate_slots + [row_doubling(slot_three(two, three))])
    gate_full, out_full = both_full[:, :width], both_full[:, width:]
    cot = jnp.concatenate([own_cot, cot_near, cot_beside, swap(cot_beside, "core")])
    mixed = unsequenced(mixed_seq)
    gate_in = lax.optimization_barrier(jnp.dot(normed, gate_full, preferred_element_type=F32))
    normed_grad = lax.optimization_barrier(jnp.dot(cot, out_full, preferred_element_type=F32))
    gate_sig = jax.nn.sigmoid(gate_in)
    gate_act = gate_in * gate_sig
    gated = mixed * gate_act
    scaled_grad = normed_grad * gain
    sums = summed_over_group(jnp.stack([jnp.sum(gated * gated, axis=1), jnp.sum(scaled_grad * gated, axis=1)]))
    gate_scale = lax.rsqrt(sums[0] / (4 * width) + EPSILON)[:, None]
    gate_normed = (gated * gate_scale * gain).astype(BF16)
    far, side_part, near, own_part = group_parts(
        lambda dx, dk: contract_columns(rows_of(gate_normed, dx, dk), out_full)
    )
    sent = (side_part + swap(far, "core").astype(F32)).astype(BF16)
    own_rows = hidden + own_part + swap(near, "core").astype(F32)

    out_grad = contract_rows(cot, gate_normed).astype(BF16)
    gate_gain_grad = jnp.sum(normed_grad * gated * gate_scale, axis=0)
    gated_grad = gate_scale * scaled_grad - gated * gate_scale**3 * (sums[1] / (4 * width))[:, None]
    mixed_grad = gated_grad * gate_act
    gate_in_grad = (gated_grad * mixed * gate_sig * (1.0 + gate_in * (1.0 - gate_sig))).astype(BF16)
    gate_grad = contract_rows(normed, gate_in_grad).astype(BF16)
    both_grad = jnp.concatenate([gate_grad, out_grad], axis=1)
    mixed_grad, both_grad, sent, own_rows = lax.optimization_barrier((mixed_grad, both_grad, sent, own_rows))
    arrived = swap(sent, "side")
    both_grad = lax.psum_scatter(both_grad, ("row", "tensor"), scatter_dimension=0, tiled=True)
    shared_inputs = (lens, order, proj, sequenced(mixed_grad), mixed_seq, kept, fw, fb, sf, sb, table, skip, spread)
    proj_grad, shared_part, *sums_late, memory, after, shared_after = mixer_backward(0, None, *shared_inputs)
    memory, arrived = tie(memory, arrived)
    out_rows = exchanged((own_rows + arrived.astype(F32)).astype(BF16))
    proj_grad, shared_part, *sums_early, _, _, _ = mixer_backward(
        1, [memory, after, shared_after, proj_grad, shared_part], *shared_inputs
    )
    fsum, ssum, hsum = (a + b for a, b in zip(sums_late, sums_early))
    proj_grad, shared_part = unsequenced(proj_grad), unsequenced(shared_part)
    proj_grad, shared_part, out_rows = tie(proj_grad, shared_part, out_rows)
    out_one = line_step((out_rows, out_rows), 1)

    def back_part(grads, dx, dk):
        gate_part, proj_part = grads
        return contract_columns(rows_of(gate_part, dx, dk), gate_full) + contract_columns(
            rows_of(proj_part, dx, dk), in_full[:, : width + LANES]
        )

    shared_far, shared_side, shared_near, shared_own = group_parts(lambda dx, dk: rows_of(shared_part, dx, dk))
    own_shared = group_sum((shared_far, shared_side, shared_near, shared_own)).astype(BF16)
    far = swap(back_part((gate_in_grad, proj_grad), 1, 1).astype(BF16), "core")
    near = swap(back_part((gate_in_grad, proj_grad), 0, 1).astype(BF16), "core")
    far, gate_later, proj_later = tie(far, gate_in_grad, proj_grad)
    sent = (back_part((gate_later, proj_later), 1, 0) + far.astype(F32)).astype(BF16)
    own_back = back_part((gate_later, proj_later), 0, 0) + near.astype(F32)
    beside = swap(sent, "side")
    proj_later, out_one = tie(proj_later, out_one)
    in_grad = contract_rows(normed, jnp.concatenate([proj_later, gathered(own_shared)], axis=1)).astype(BF16)
    out_two = line_step(out_one, 2)
    in_grad, both_grad, own_back = tie(in_grad, both_grad, own_back)
    beside, out_two = tie(beside, out_two)
    both_grad = crossed(both_grad)
    normed_back = own_back + beside.astype(F32) + contract_columns(own_shared, in_full[:, width + LANES :])
    norm_gain_grad = jnp.sum(normed_back * hidden * scale, axis=0)
    gained = normed_back * norm_gain
    along = jnp.mean(gained * hidden, axis=1, keepdims=True)
    input_work = own_cot.astype(F32) + scale * gained - hidden * (scale**3 * along)
    line = lambda v: jnp.pad(v, (0, -v.shape[0] % width)).reshape(-1, width)
    skip_grad = fsum[5].reshape(heads, -1).sum(axis=1)
    small = jnp.concatenate(
        [
            fsum[:5],
            gate_gain_grad[None],
            jnp.pad(jnp.concatenate([hsum[0, :heads], hsum[1, :heads], skip_grad]), (0, width - 3 * heads))[None],
            jnp.zeros((1, width), F32),
            line(norm_gain_grad),
            line(ssum[:5].reshape(-1)),
        ],
        axis=0,
    )
    back_rows = exchanged(input_work.astype(BF16))
    small = summed(small, ("row",))
    small = jnp.concatenate([small[:8], summed(small[8:], ("core", "side"))], axis=0)
    back_rows, out_two, small, both_grad, in_grad = tie(back_rows, out_two, small, both_grad, in_grad)
    in_grad = lax.psum_scatter(row_scattered(in_grad), "tensor", scatter_dimension=0, tiled=True)
    back_one = line_step((back_rows, back_rows), 1)
    out_three = line_step(out_two, 3)
    back_two = line_step(back_one, 2)
    back_two, in_grad = tie(back_two, in_grad)
    back_three = line_step(back_two, 3)
    out_three, _ = tie(out_three, back_two)
    layer_out = settled([out_rows, slot_one(out_one)], (0, 1))
    layer_out = layer_out + settled([slot_two(out_one, out_two), slot_three(out_two, out_three)], (2, 3))
    input_grad = settled([back_rows, slot_one(back_one)], (0, 1))
    layer_out, input_grad, back_three, small = tie(layer_out, input_grad, back_three, small)
    input_grad = input_grad + settled([slot_two(back_one, back_two), slot_three(back_two, back_three)], (2, 3))
    small = small + swap(small, "tensor", 1)
    small = small + swap(small, "tensor", 2)
    mine, common = crossed(small[:8]), small[8:]
    in_grad = crossed(in_grad).astype(F32)
    inner_grad = jnp.stack([both_grad[:, :width].astype(F32), in_grad[:, :width]], axis=1)

    lines = line(norm_gain_grad).shape[0]
    norm_gain_grad = common[:lines].reshape(-1)[:model_width]
    shared_sums = common[lines:].reshape(-1)[: 5 * sf.shape[1]].reshape(5, -1)
    return (
        layer_out, input_grad, norm_gain_grad, inner_grad, in_grad[:, width + LANES :],
        in_grad[:, width : width + heads], mine[:4], mine[4], shared_sums[:4], shared_sums[4],
        mine[6, :heads], mine[6, heads : 2 * heads], mine[6, 2 * heads : 3 * heads], mine[5], both_grad[:, width:].astype(F32),
    )


def solution(mesh):
    count, planes = mesh.devices.shape
    assert planes == 4 and count % 4 == 0
    names = ("row", "side", "core", "tensor")
    inner = jax.sharding.Mesh(mesh.devices.reshape(count // 4, 2, 2, planes), names)
    dp = ("row", "side", "core")
    in_specs = (
        P(dp, None), P(dp, None), P(dp), P(dp, None), P(), P(dp, None, "tensor"), P(dp, None), P(dp, "tensor"),
        P(None, "tensor"), P("tensor"), P(), P(), P("tensor"), P("tensor"), P("tensor"), P("tensor"), P(dp, "tensor"),
    )
    out_specs = (
        P(dp, None), P(dp, None), P(), P(dp, None, "tensor"), P(dp, None), P(dp, "tensor"),
        P(None, "tensor"), P("tensor"), P(), P(), P("tensor"), P("tensor"), P("tensor"), P("tensor"), P(dp, "tensor"),
    )
    return jax.shard_map(on_device, mesh=inner, in_specs=in_specs, out_specs=out_specs, check_vma=False)
```

```python
import functools

import jax
import jax.numpy as jnp
from jax import lax
from jax.experimental import pallas as pl
from jax.experimental.pallas import tpu as pltpu
from jax.sharding import PartitionSpec as P

SPAN = 128
HALO = 8
LANES = 128
F32 = jnp.float32
BF16 = jnp.bfloat16
EPSILON = 1e-05


def mm(a, b):
    return jnp.dot(a, b, preferred_element_type=F32)


def mm_t(a, b):
    return lax.dot_general(a, b, (((1,), (1,)), ((), ())), preferred_element_type=F32)


def halves(v):
    high = v.astype(BF16)
    return high, (v - high.astype(F32)).astype(BF16)


def widen(v, spread):
    high, rest = halves(v)
    return mm(high, spread) + mm(rest, spread)


def head_sum(v, spread):
    high, rest = halves(v)
    return mm_t(high, spread) + mm_t(rest, spread)


def start_of(place, lens_ref):
    end, start = jnp.int32(0), jnp.zeros_like(place)
    for i in range(lens_ref.shape[0]):
        start = jnp.where(place >= end, end, start)
        end = end + lens_ref[i]
    return start


def taps(current, before, reach):
    whole = jnp.concatenate([before, current], axis=0)
    rows = current.shape[0]
    return [whole[HALO - k : HALO - k + rows] for k in range(reach)]


def filtered(shifted, allowed, kernel, bias):
    result = bias + kernel[0:1] * shifted[0]
    for k in range(1, len(shifted)):
        result = result + kernel[k : k + 1] * shifted[k] * allowed[k]
    return result


def permitted(place, start, reach, width):
    flags = [None]
    for k in range(1, reach):
        flags.append(jnp.where(place - k >= start, 1.0, 0.0)[:, :1])
    return flags


def softplus(v):
    return jnp.maximum(v, 0.0) + jnp.log1p(jnp.exp(-jnp.abs(v)))


def chunk_setup(base, lens_ref, span):
    place = base + lax.broadcasted_iota(jnp.int32, (span, LANES), 0)
    start = start_of(place, lens_ref)
    last_start = start_of(jnp.full((1, LANES), base + span - 1, jnp.int32), lens_ref)
    return place, start, last_start


def stacked(pair, low_lanes):
    zero = jnp.zeros_like(pair)
    return jnp.concatenate([jnp.where(low_lanes, pair, zero), jnp.where(low_lanes, zero, pair)], axis=0)


def forward_kernel(
    lens_ref, order_ref, proj_ref, fw_ref, fb_ref, sf_ref, sb_ref, head_ref, skip_ref, spread_ref,
    out_ref, kept_ref, memory, before, shared_before,
):
    step = pl.program_id(0)
    span = proj_ref.shape[0]
    width = out_ref.shape[1]
    reach = fw_ref.shape[0]
    pairs = width // LANES
    base = step * span

    @pl.when(step == 0)
    def _():
        memory[...] = jnp.zeros_like(memory)
        before[...] = jnp.zeros_like(before)
        shared_before[...] = jnp.zeros_like(shared_before)

    place, start, last_start = chunk_setup(base, lens_ref, span)
    allowed = permitted(place, start, reach, width)
    inputs = proj_ref[:, :width]
    shared = proj_ref[:, width + LANES :]
    conv = filtered(taps(inputs, before[...], reach), allowed, fw_ref, fb_ref[...])
    values = conv * jax.nn.sigmoid(conv)
    conv = filtered(taps(shared, shared_before[...], reach), allowed, sf_ref, sb_ref[...])
    factors = conv * jax.nn.sigmoid(conv)
    before[...] = inputs[span - HALO :]
    shared_before[...] = shared[span - HALO :]
    writes = factors[:, :LANES].astype(BF16)
    reads = factors[:, LANES:].astype(BF16)
    size = softplus(proj_ref[:, width : width + LANES] + head_ref[0:1])
    decay = -size * head_ref[1:2]
    row = lax.broadcasted_iota(jnp.int32, (span, span), 0)
    col = lax.broadcasted_iota(jnp.int32, (span, span), 1)
    lower = jnp.where(row >= col, 1.0, 0.0)
    total = jnp.dot(lower, decay, precision=lax.Precision.HIGHEST, preferred_element_type=F32)
    total_t = total.T
    inside = (col <= row) & (col + base >= start)
    scores = jnp.where(inside, mm_t(reads, writes), 0.0)
    spread = spread_ref[...]
    scaled = values * widen(size, spread)
    scaled_low = scaled.astype(BF16)
    entering = jnp.exp(total) * jnp.where(start < base, 1.0, 0.0)
    state = memory[...]
    state_low = state.astype(BF16)
    kept_ref[0] = state_low
    remote = mm(reads, state_low) * widen(entering, spread) + skip_ref[...] * values
    low_lanes = lax.broadcasted_iota(jnp.int32, (span, LANES), 1) < LANES // 2
    for pair in range(pairs):
        lanes = slice(pair * LANES, (pair + 1) * LANES)
        mixing = []
        for head in (2 * pair, 2 * pair + 1):
            fade = jnp.exp(jnp.minimum(total[:, head : head + 1] - total_t[head : head + 1, :], 0.0))
            mixing.append((scores * fade).astype(BF16))
        local = mm(jnp.concatenate(mixing, axis=1), stacked(scaled_low[:, lanes], low_lanes))
        out_ref[:, lanes] = (local + remote[:, lanes]).astype(out_ref.dtype)
    end = total[span - 1 : span]
    closing = jnp.exp(end - total) * jnp.where(place >= last_start, 1.0, 0.0)
    added = mm(writes.T, (scaled * widen(closing, spread)).astype(BF16))
    keeping = jnp.exp(end) * jnp.where(last_start < base, 1.0, 0.0)
    memory[...] = state * widen(jnp.broadcast_to(keeping, (8, LANES)), spread)[0:1] + added


def backward_kernel(
    first_chunk, lens_ref, order_ref, proj_ref, proj_before_ref, grad_ref, out_ref, kept_ref,
    fw_ref, fb_ref, sf_ref, sb_ref, head_ref, skip_ref, spread_ref,
    memory_from, after_from, shared_after_from, proj_grad_from, shared_grad_from,
    proj_grad_ref, shared_grad_ref, fsum_ref, ssum_ref, hsum_ref, memory_grad, after, shared_after,
):
    step = pl.program_id(0)
    span = proj_ref.shape[0]
    width = out_ref.shape[1]
    reach = fw_ref.shape[0]
    pairs = width // LANES
    chunk = first_chunk - step
    base = chunk * span

    @pl.when(step == 0)
    def _():
        memory_grad[...] = memory_from[...]
        after[...] = after_from[...]
        shared_after[...] = shared_after_from[...]
        fsum_ref[...] = jnp.zeros_like(fsum_ref)
        ssum_ref[...] = jnp.zeros_like(ssum_ref)
        hsum_ref[...] = jnp.zeros_like(hsum_ref)

    place, start, last_start = chunk_setup(base, lens_ref, span)
    allowed = permitted(place, start, reach, width)
    first = jnp.where(chunk > 0, 1.0, 0.0)
    inputs = proj_ref[:, :width]
    shifted = taps(inputs, proj_before_ref[:, :width] * first, reach)
    conv = filtered(shifted, allowed, fw_ref, fb_ref[...])
    gate = jax.nn.sigmoid(conv)
    values = conv * gate
    slope = gate * (1.0 + conv * (1.0 - gate))
    shared_shifted = taps(proj_ref[:, width + LANES :], proj_before_ref[:, width + LANES :] * first, reach)
    conv = filtered(shared_shifted, allowed, sf_ref, sb_ref[...])
    gate = jax.nn.sigmoid(conv)
    factors = conv * gate
    shared_slope = gate * (1.0 + conv * (1.0 - gate))
    writes = factors[:, :LANES].astype(BF16)
    reads = factors[:, LANES:].astype(BF16)
    raw = proj_ref[:, width : width + LANES] + head_ref[0:1]
    size = softplus(raw)
    decay = -size * head_ref[1:2]
    row = lax.broadcasted_iota(jnp.int32, (span, span), 0)
    col = lax.broadcasted_iota(jnp.int32, (span, span), 1)
    lower = jnp.where(row >= col, 1.0, 0.0)
    upper = jnp.where(row <= col, 1.0, 0.0)
    total = jnp.dot(lower, decay, precision=lax.Precision.HIGHEST, preferred_element_type=F32)
    total_t = total.T
    start_t = start_of(base + col[0:1], lens_ref)
    inside_t = (row <= col) & (row + base >= start_t)
    scores_t = jnp.where(inside_t, mm_t(writes, reads), 0.0)
    spread = spread_ref[...]
    size_wide = widen(size, spread)
    scaled = values * size_wide
    scaled_low = scaled.astype(BF16)
    grad = grad_ref[...].astype(F32)
    grad_low = grad.astype(BF16)
    state_low = kept_ref[0]
    later = memory_grad[...]
    later_low = later.astype(BF16)
    entering = jnp.exp(total) * jnp.where(start < base, 1.0, 0.0)
    entered = (grad * widen(entering, spread)).astype(BF16)
    end = total[span - 1 : span]
    closing = jnp.exp(end - total) * jnp.where(place >= last_start, 1.0, 0.0)
    closing_wide = widen(closing, spread)
    keeping = jnp.exp(end) * jnp.where(last_start < base, 1.0, 0.0)
    keeping_wide = widen(jnp.broadcast_to(keeping, (8, LANES)), spread)[0:1]
    closed = mm(writes, later_low) * closing_wide
    low_lanes = lax.broadcasted_iota(jnp.int32, (span, LANES), 1) < LANES // 2
    scores_grad_t = jnp.zeros((span, span), F32)
    local = []
    for pair in range(pairs):
        lanes = slice(pair * LANES, (pair + 1) * LANES)
        halved = stacked(grad_low[:, lanes], low_lanes)
        mixing_grad = mm_t(scaled_low[:, lanes], halved)
        mixing = []
        for which, head in enumerate((2 * pair, 2 * pair + 1)):
            fade = jnp.exp(jnp.minimum(total_t[head : head + 1, :] - total[:, head : head + 1], 0.0))
            mixing.append((scores_t * fade).astype(BF16))
            scores_grad_t = scores_grad_t + mixing_grad[:, which * span : (which + 1) * span] * fade
        local.append(mm(jnp.concatenate(mixing, axis=1), halved))
    scaled_grad = jnp.concatenate(local, axis=1) + closed
    scores_grad_t = jnp.where(inside_t, scores_grad_t, 0.0).astype(BF16)
    kept_closing = (scaled * closing_wide).astype(BF16)
    reads_grad = mm(scores_grad_t.T, writes) + mm_t(entered, state_low)
    writes_grad = mm(scores_grad_t, reads) + mm_t(kept_closing, later_low)
    memory_grad[...] = later * keeping_wide + mm(reads.T, entered)
    skip = skip_ref[...]
    size_grad = head_sum(values * scaled_grad, spread)
    paid = head_sum(
        grad_low.astype(F32) * (out_ref[...] - skip * values) - scaled_low.astype(F32) * scaled_grad, spread
    )
    tail = jnp.sum(scaled_low.astype(F32) * closed, axis=0, keepdims=True) + keeping_wide * jnp.sum(
        later * state_low.astype(F32), axis=0, keepdims=True
    )
    tail = head_sum(jnp.broadcast_to(tail, (8, width)), spread)[0:1]
    total_grad = paid + jnp.where(place == base + span - 1, tail, 0.0)
    decay_grad = jnp.dot(upper, total_grad, precision=lax.Precision.HIGHEST, preferred_element_type=F32)
    raw_grad = (size_grad - decay_grad * head_ref[1:2]) * jax.nn.sigmoid(raw)
    proj_grad_ref[:, width:] = raw_grad.astype(proj_grad_ref.dtype)
    hsum_ref[0:1] += jnp.sum(raw_grad, axis=0, keepdims=True)
    hsum_ref[1:2] += jnp.sum(decay_grad * decay, axis=0, keepdims=True)
    conv_grad = (size_wide * scaled_grad + skip * grad) * slope
    shared_conv_grad = jnp.concatenate([writes_grad, reads_grad], axis=1) * shared_slope
    fsum_ref[reach : reach + 1] += jnp.sum(conv_grad, axis=0, keepdims=True)
    fsum_ref[reach + 1 : reach + 2] += jnp.sum(grad * values, axis=0, keepdims=True)
    ssum_ref[reach : reach + 1] += jnp.sum(shared_conv_grad, axis=0, keepdims=True)
    late = base + lax.broadcasted_iota(jnp.int32, (span + HALO, LANES), 0)
    late_allowed = permitted(late, start_of(late, lens_ref), reach, width)
    whole = jnp.concatenate([conv_grad, after[...]], axis=0)
    shared_whole = jnp.concatenate([shared_conv_grad, shared_after[...]], axis=0)
    result = fw_ref[0:1] * conv_grad
    shared_result = sf_ref[0:1] * shared_conv_grad
    fsum_ref[0:1] += jnp.sum(conv_grad * shifted[0], axis=0, keepdims=True)
    ssum_ref[0:1] += jnp.sum(shared_conv_grad * shared_shifted[0], axis=0, keepdims=True)
    for k in range(1, reach):
        masked = whole * late_allowed[k]
        fsum_ref[k : k + 1] += jnp.sum(masked[:span] * shifted[k], axis=0, keepdims=True)
        result = result + fw_ref[k : k + 1] * masked[k : k + span]
        masked = shared_whole * late_allowed[k]
        ssum_ref[k : k + 1] += jnp.sum(masked[:span] * shared_shifted[k], axis=0, keepdims=True)
        shared_result = shared_result + sf_ref[k : k + 1] * masked[k : k + span]
    after[...] = conv_grad[:HALO]
    shared_after[...] = shared_conv_grad[:HALO]
    proj_grad_ref[:, :width] = result.astype(proj_grad_ref.dtype)
    shared_grad_ref[...] = shared_result.astype(shared_grad_ref.dtype)


def head_rows(step_bias, decay_log, skip_gain, width):
    heads = step_bias.shape[0]
    table = jnp.zeros((8, LANES), F32)
    table = table.at[0, :heads].set(step_bias).at[1, :heads].set(jnp.exp(decay_log))
    skip = jnp.repeat(skip_gain, width // heads)[None, :]
    spread = (jnp.arange(LANES)[:, None] == (jnp.arange(width) // (width // heads))[None, :]).astype(BF16)
    return table, skip, spread


def fixed(shape):
    return pl.BlockSpec(shape, lambda *_: (0,) * len(shape))


def mixer_forward(lens, order, proj, fw, fb, sf, sb, table, skip, spread):
    rows = proj.shape[0]
    width = fw.shape[1]
    steps = rows // SPAN
    block = lambda cols: pl.BlockSpec((SPAN, cols), lambda i, lens_ref, order_ref: (order_ref[i], 0))
    return pl.pallas_call(
        forward_kernel,
        grid_spec=pltpu.PrefetchScalarGridSpec(
            num_scalar_prefetch=2,
            grid=(steps,),
            in_specs=[
                block(proj.shape[1]), fixed(fw.shape), fixed(fb.shape), fixed(sf.shape),
                fixed(sb.shape), fixed(table.shape), fixed(skip.shape), fixed(spread.shape),
            ],
            out_specs=[block(width), pl.BlockSpec((1, LANES, width), lambda i, *_: (i, 0, 0))],
            scratch_shapes=[
                pltpu.VMEM((LANES, width), F32),
                pltpu.VMEM((HALO, width), F32),
                pltpu.VMEM((HALO, sf.shape[1]), F32),
            ],
        ),
        out_shape=[
            jax.ShapeDtypeStruct((rows, width), F32),
            jax.ShapeDtypeStruct((steps, LANES, width), BF16),
        ],
        cost_estimate=pl.CostEstimate(flops=20 * 10**9, bytes_accessed=30 * 10**6, transcendentals=0),
        name="mixer_forward",
    )(lens, order, proj, fw, fb, sf, sb, table, skip, spread)


def mixer_backward(half, carried, lens, order, proj, grad, out, kept, fw, fb, sf, sb, table, skip, spread):
    rows = proj.shape[0]
    width = fw.shape[1]
    steps = rows // SPAN // 2
    first_chunk = (2 - half) * steps - 1
    lead = SPAN // HALO
    block = lambda cols: pl.BlockSpec((SPAN, cols), lambda i, lens_ref, order_ref: (order_ref[first_chunk - i], 0))
    ahead = lambda cols: pl.BlockSpec(
        (HALO, cols),
        lambda i, lens_ref, order_ref: (order_ref[jnp.maximum(first_chunk - 1 - i, 0)] * lead + lead - 1, 0),
    )
    anywhere = pl.BlockSpec(memory_space=pl.ANY)
    out_shape = [
        jax.ShapeDtypeStruct((rows, width + LANES), BF16),
        jax.ShapeDtypeStruct((rows, sf.shape[1]), F32),
        jax.ShapeDtypeStruct((8, width), F32),
        jax.ShapeDtypeStruct((8, sf.shape[1]), F32),
        jax.ShapeDtypeStruct((8, LANES), F32),
        jax.ShapeDtypeStruct((LANES, width), F32),
        jax.ShapeDtypeStruct((HALO, width), F32),
        jax.ShapeDtypeStruct((HALO, sf.shape[1]), F32),
    ]
    if carried is None:
        carried = [jnp.zeros(v.shape, F32) for v in out_shape[5:]] + [jnp.zeros((8, LANES), F32)] * 2
        aliases = {}
    else:
        aliases = {17: 0, 18: 1}
    return pl.pallas_call(
        functools.partial(backward_kernel, first_chunk),
        grid_spec=pltpu.PrefetchScalarGridSpec(
            num_scalar_prefetch=2,
            grid=(steps,),
            in_specs=[
                block(proj.shape[1]), ahead(proj.shape[1]),
                block(width), block(width),
                pl.BlockSpec((1, LANES, width), lambda i, *_: (first_chunk - i, 0, 0)),
                fixed(fw.shape), fixed(fb.shape), fixed(sf.shape),
                fixed(sb.shape), fixed(table.shape), fixed(skip.shape), fixed(spread.shape),
                fixed((LANES, width)), fixed((HALO, width)), fixed((HALO, sf.shape[1])), anywhere, anywhere,
            ],
            out_specs=[
                block(width + LANES), block(sf.shape[1]),
                fixed((8, width)), fixed((8, sf.shape[1])), fixed((8, LANES)),
                fixed((LANES, width)), fixed((HALO, width)), fixed((HALO, sf.shape[1])),
            ],
        ),
        out_shape=out_shape,
        input_output_aliases=aliases,
        cost_estimate=pl.CostEstimate(flops=20 * 10**9, bytes_accessed=30 * 10**6, transcendentals=0),
        name="mixer_backward",
    )(lens, order, proj, proj, grad, out, kept, fw, fb, sf, sb, table, skip, spread, *carried)


def swap(v, axis, mask=1):
    count = lax.axis_size(axis)
    return lax.ppermute(v, axis, [(i, i ^ mask) for i in range(count)])


def crossed(v):
    pairs = [(a * 4 + b, b * 4 + a) for a in range(4) for b in range(4)]
    return lax.ppermute(v, ("side", "core", "tensor"), pairs)


def row_doubling(v):
    pieces = [v]
    while len(pieces) < lax.axis_size("row"):
        reach = len(pieces)
        pieces = pieces + [swap(p, "row", reach) for p in pieces]
    return pieces


SLOT_PLANES = ((0, 1, 2, 3), (1, 0, 2, 3), (2, 1, 3, 0), (3, 2, 1, 0))


def tie(*values):
    return lax.optimization_barrier(values)


def line_step(pair, j):
    left, right = pair
    return (
        lax.ppermute(left, "tensor", [(i, i + 1) for i in range(j - 1, 3)]),
        lax.ppermute(right, "tensor", [(i + 1, i) for i in range(0, 4 - j)]),
    )


def slot_one(one):
    return jnp.where(lax.axis_index("tensor") == 0, one[1], one[0])


def slot_two(one, two):
    plane = lax.axis_index("tensor")
    return jnp.where(plane == 0, two[1], jnp.where(plane == 3, two[0], one[1]))


def slot_three(two, three):
    plane = lax.axis_index("tensor")
    return jnp.where(
        plane == 0, three[1], jnp.where(plane == 1, two[1], jnp.where(plane == 2, two[0], three[0]))
    )


def summed(v, axes):
    for axis in axes:
        reach = 1
        while reach < lax.axis_size(axis):
            v = v + swap(v, axis, reach)
            reach = reach * 2
    return v


def row_scattered(v):
    row, reach = lax.axis_index("row"), lax.axis_size("row") // 2
    while reach:
        half = v.shape[0] // 2
        high = (row // reach) % 2
        kept = lax.dynamic_slice_in_dim(v, high * half, half, 0)
        given = lax.dynamic_slice_in_dim(v, (1 - high) * half, half, 0)
        v = (kept.astype(F32) + swap(given, "row", reach).astype(F32)).astype(BF16)
        reach = reach // 2
    return v


def contract_rows(a, b):
    return lax.dot_general(a, b, (((0,), (0,)), ((), ())), preferred_element_type=F32)


def contract_columns(a, b):
    return lax.dot_general(a, b, (((1,), (1,)), ((), ())), preferred_element_type=F32)


def on_device(
    tokens, cotangent, destination, lengths, norm_gain, inner_weight, shared_weight, step_weight, filter_weight,
    filter_bias, shared_filter, shared_filter_bias, step_bias, decay_log, skip_gain, gate_gain, out_weight,
):
    row_count, model_width = tokens.shape
    width = filter_weight.shape[1]
    heads = step_bias.shape[0]
    rows_n, planes = lax.axis_size("row"), lax.axis_size("tensor")
    row, side, core, plane = (lax.axis_index(a) for a in ("row", "side", "core", "tensor"))
    group_rows = row_count // (rows_n * 4)
    owned = rows_n * group_rows
    source = (row * 2 + side) * 2 + core

    wanted = jnp.concatenate(
        [
            ((row ^ d) * planes + plane) * row_count + source * group_rows + jnp.arange(group_rows, dtype=jnp.int32)
            for d in range(rows_n)
        ]
    )
    chosen = (wanted[:, None] == destination[None, :]).astype(BF16)

    def exchanged(sent):
        return jnp.concatenate([sent[:group_rows]] + [
            swap(sent[d * group_rows : (d + 1) * group_rows], "row", d) for d in range(1, rows_n)
        ])

    def gathered(own):
        beside = swap(own, "side")
        return jnp.concatenate([own, swap(own, "core"), beside, swap(beside, "core")])

    slot_planes = jnp.array(SLOT_PLANES, jnp.int32)[plane]

    def assembled(doubled):
        rows, columns = doubled[0][0].shape
        whole = jnp.zeros((planes * rows_n * rows, columns), BF16)
        for i, pieces in enumerate(doubled):
            for d, p in enumerate(pieces):
                whole = lax.dynamic_update_slice(whole, p, (((row ^ d) * planes + slot_planes[i]) * rows, 0))
        return whole

    picked = jnp.dot(chosen, tokens, preferred_element_type=F32).astype(BF16)
    step_low = jnp.pad(step_weight.astype(BF16), ((0, 0), (0, LANES - heads)))
    piece = jnp.concatenate([inner_weight[:, 1].astype(BF16), step_low, shared_weight.astype(BF16)], axis=1)
    gate_piece = jnp.concatenate([inner_weight[:, 0].astype(BF16), out_weight.astype(BF16)], axis=1)
    picked_cot = jnp.dot(chosen, cotangent, preferred_element_type=F32).astype(BF16)
    own_tokens, piece, picked_cot = tie(exchanged(picked), crossed(piece), picked_cot)
    own_cot = exchanged(picked_cot)
    one = line_step((piece, piece), 1)
    in_slots = [row_doubling(piece)]
    hidden = own_tokens.astype(F32)
    scale = lax.rsqrt(jnp.mean(hidden * hidden, axis=-1, keepdims=True) + EPSILON)
    own_normed = (hidden * scale * norm_gain).astype(BF16)
    beside, near = swap(own_normed, "side"), swap(own_normed, "core")
    one, near, gate_piece = tie(one, near, gate_piece)
    two = line_step(one, 2)
    gate_piece = crossed(gate_piece)
    in_slots = in_slots + [row_doubling(slot_one(one))]
    two, own_cot, in_slots = tie(two, own_cot, in_slots)
    three = line_step(two, 3)
    in_slots = in_slots + [row_doubling(slot_two(one, two))]
    three, beside, gate_piece, in_slots = tie(three, beside, gate_piece, in_slots)
    in_slots = in_slots + [row_doubling(slot_three(two, three))]
    far = swap(beside, "core")
    one = line_step((gate_piece, gate_piece), 1)
    in_slots, far, one = tie(in_slots, far, one)
    two = line_step(one, 2)
    gate_slots = [row_doubling(gate_piece), row_doubling(slot_one(one))]
    normed = jnp.concatenate([own_normed, near, beside, far])
    in_full = assembled(in_slots)

    params = jnp.concatenate(
        [
            filter_weight,
            filter_bias[None],
            gate_gain[None],
            jnp.pad(jnp.concatenate([step_bias, decay_log, skip_gain]), (0, width - 3 * heads))[None],
            jnp.pad(lengths.astype(F32), ((0, 0), (0, width - lengths.shape[1]))),
        ],
        axis=0,
    )
    params = crossed(params)
    fw, fb, gain = params[:4], params[4:5], params[5:6]
    bias_here, decay_here, skip_here = (params[6, i * heads : (i + 1) * heads] for i in range(3))
    lens = params[7, : lengths.shape[1]].astype(jnp.int32)
    sf, sb = shared_filter, shared_filter_bias[None]
    table, skip, spread = head_rows(bias_here, decay_here, skip_here, width)

    if group_rows % SPAN == 0:
        spans = jnp.arange(row_count // SPAN, dtype=jnp.int32)
        part = (spans * SPAN // group_rows) ^ source
        order = (((part // 2) % 2 * 2 + part % 2) * rows_n + part // 4) * (group_rows // SPAN)
        order = order + spans % (group_rows // SPAN)
        sequenced = unsequenced = lambda v: v
    else:
        order = jnp.arange(row_count // SPAN, dtype=jnp.int32)
        groups = jnp.arange(4 * rows_n, dtype=jnp.int32)
        part = groups ^ source
        to = ((part // 2) % 2 * 2 + part % 2) * rows_n + part // 4
        fro = (((groups % rows_n) * 4 + groups // rows_n) ^ source)
        sequenced = lambda v: v.reshape(4 * rows_n, group_rows, -1)[to].reshape(v.shape)
        unsequenced = lambda v: v.reshape(4 * rows_n, group_rows, -1)[fro].reshape(v.shape)

    def summed_over_group(v):
        v = v + swap(v, "core").reshape(2, 2, 2, owned)[:, :, ::-1].reshape(2, -1)
        return v + swap(v, "side").reshape(2, 2, 2 * owned)[:, ::-1].reshape(2, -1)

    def rows_of(v, dx, dk):
        return v[(dx * 2 + dk) * owned : (dx * 2 + dk + 1) * owned]

    def group_parts(part):
        return part(1, 1).astype(BF16), part(1, 0), part(0, 1).astype(BF16), part(0, 0)

    def group_sum(parts):
        far, side_part, near, own_part = parts
        beside = swap((side_part + swap(far, "core").astype(F32)).astype(BF16), "side")
        return own_part + swap(near, "core").astype(F32) + beside.astype(F32)

    block_of = destination // row_count
    row_of, plane_of = (block_of // planes) ^ row, block_of % planes
    slot = row_of * group_rows + destination - block_of * row_count - source * group_rows

    def settled(held, which):
        where = jnp.concatenate([jnp.where(plane_of == slot_planes[j], slot, -1)[:, None] == jnp.arange(owned)[None, :]
                                 for j in which], axis=1)
        return jnp.dot(where.astype(BF16), jnp.concatenate(held), preferred_element_type=F32).astype(BF16)

    proj = jnp.dot(normed, in_full, preferred_element_type=F32)
    proj, two, gate_slots, own_cot = tie(proj, two, gate_slots, own_cot)
    cot_beside, cot_near = swap(own_cot, "side"), swap(own_cot, "core")
    three = line_step(two, 3)
    gate_slots = gate_slots + [row_doubling(slot_two(one, two))]
    proj = sequenced(proj)
    mixed_seq, kept = mixer_forward(lens, order, proj, fw, fb, sf, sb, table, skip, spread)
    mixed_seq, three, gate_slots, cot_beside = tie(mixed_seq, three, gate_slots, cot_beside)
    both_full = assembled(gate_slots + [row_doubling(slot_three(two, three))])
    gate_full, out_full = both_full[:, :width], both_full[:, width:]
    cot = jnp.concatenate([own_cot, cot_near, cot_beside, swap(cot_beside, "core")])
    mixed = unsequenced(mixed_seq)
    gate_in = lax.optimization_barrier(jnp.dot(normed, gate_full, preferred_element_type=F32))
    normed_grad = lax.optimization_barrier(jnp.dot(cot, out_full, preferred_element_type=F32))
    gate_sig = jax.nn.sigmoid(gate_in)
    gate_act = gate_in * gate_sig
    gated = mixed * gate_act
    scaled_grad = normed_grad * gain
    sums = summed_over_group(jnp.stack([jnp.sum(gated * gated, axis=1), jnp.sum(scaled_grad * gated, axis=1)]))
    gate_scale = lax.rsqrt(sums[0] / (4 * width) + EPSILON)[:, None]
    gate_normed = (gated * gate_scale * gain).astype(BF16)
    far, side_part, near, own_part = group_parts(
        lambda dx, dk: contract_columns(rows_of(gate_normed, dx, dk), out_full)
    )
    sent = (side_part + swap(far, "core").astype(F32)).astype(BF16)
    own_rows = hidden + own_part + swap(near, "core").astype(F32)

    out_grad = contract_rows(cot, gate_normed).astype(BF16)
    gate_gain_grad = jnp.sum(normed_grad * gated * gate_scale, axis=0)
    gated_grad = gate_scale * scaled_grad - gated * gate_scale**3 * (sums[1] / (4 * width))[:, None]
    mixed_grad = gated_grad * gate_act
    gate_in_grad = (gated_grad * mixed * gate_sig * (1.0 + gate_in * (1.0 - gate_sig))).astype(BF16)
    gate_grad = contract_rows(normed, gate_in_grad).astype(BF16)
    both_grad = jnp.concatenate([gate_grad, out_grad], axis=1)
    mixed_grad, both_grad, sent, own_rows = lax.optimization_barrier((mixed_grad, both_grad, sent, own_rows))
    arrived = swap(sent, "side")
    both_grad = lax.psum_scatter(both_grad, ("row", "tensor"), scatter_dimension=0, tiled=True)
    shared_inputs = (lens, order, proj, sequenced(mixed_grad), mixed_seq, kept, fw, fb, sf, sb, table, skip, spread)
    proj_grad, shared_part, *sums_late, memory, after, shared_after = mixer_backward(0, None, *shared_inputs)
    memory, arrived = tie(memory, arrived)
    out_rows = exchanged((own_rows + arrived.astype(F32)).astype(BF16))
    proj_grad, shared_part, *sums_early, _, _, _ = mixer_backward(
        1, [memory, after, shared_after, proj_grad, shared_part], *shared_inputs
    )
    fsum, ssum, hsum = (a + b for a, b in zip(sums_late, sums_early))
    proj_grad, shared_part = unsequenced(proj_grad), unsequenced(shared_part)
    proj_grad, shared_part, out_rows = tie(proj_grad, shared_part, out_rows)
    out_one = line_step((out_rows, out_rows), 1)

    def back_part(grads, dx, dk):
        gate_part, proj_part = grads
        return contract_columns(rows_of(gate_part, dx, dk), gate_full) + contract_columns(
            rows_of(proj_part, dx, dk), in_full[:, : width + LANES]
        )

    shared_far, shared_side, shared_near, shared_own = group_parts(lambda dx, dk: rows_of(shared_part, dx, dk))
    own_shared = group_sum((shared_far, shared_side, shared_near, shared_own)).astype(BF16)
    far = swap(back_part((gate_in_grad, proj_grad), 1, 1).astype(BF16), "core")
    near = swap(back_part((gate_in_grad, proj_grad), 0, 1).astype(BF16), "core")
    far, gate_later, proj_later = tie(far, gate_in_grad, proj_grad)
    sent = (back_part((gate_later, proj_later), 1, 0) + far.astype(F32)).astype(BF16)
    own_back = back_part((gate_later, proj_later), 0, 0) + near.astype(F32)
    beside = swap(sent, "side")
    proj_later, out_one = tie(proj_later, out_one)
    in_grad = contract_rows(normed, jnp.concatenate([proj_later, gathered(own_shared)], axis=1)).astype(BF16)
    out_two = line_step(out_one, 2)
    in_grad, both_grad, own_back = tie(in_grad, both_grad, own_back)
    beside, out_two = tie(beside, out_two)
    out_three = line_step(out_two, 3)
    both_grad = crossed(both_grad)
    normed_back = own_back + beside.astype(F32) + contract_columns(own_shared, in_full[:, width + LANES :])
    norm_gain_grad = jnp.sum(normed_back * hidden * scale, axis=0)
    gained = normed_back * norm_gain
    along = jnp.mean(gained * hidden, axis=1, keepdims=True)
    input_work = own_cot.astype(F32) + scale * gained - hidden * (scale**3 * along)
    line = lambda v: jnp.pad(v, (0, -v.shape[0] % width)).reshape(-1, width)
    skip_grad = fsum[5].reshape(heads, -1).sum(axis=1)
    small = jnp.concatenate(
        [
            fsum[:5],
            gate_gain_grad[None],
            jnp.pad(jnp.concatenate([hsum[0, :heads], hsum[1, :heads], skip_grad]), (0, width - 3 * heads))[None],
            jnp.zeros((1, width), F32),
            line(norm_gain_grad),
            line(ssum[:5].reshape(-1)),
        ],
        axis=0,
    )
    back_rows = exchanged(input_work.astype(BF16))
    small = summed(small, ("row",))
    small = jnp.concatenate([small[:8], summed(small[8:], ("core", "side"))], axis=0)
    back_rows, out_three, small, both_grad, in_grad = tie(back_rows, out_three, small, both_grad, in_grad)
    in_grad = lax.psum_scatter(row_scattered(in_grad), "tensor", scatter_dimension=0, tiled=True)
    back_one = line_step((back_rows, back_rows), 1)
    back_two = line_step(back_one, 2)
    back_three = line_step(back_two, 3)
    layer_out = settled([out_rows, slot_one(out_one)], (0, 1))
    layer_out = layer_out + settled([slot_two(out_one, out_two), slot_three(out_two, out_three)], (2, 3))
    input_grad = settled([back_rows, slot_one(back_one)], (0, 1))
    layer_out, input_grad, back_three, small, in_grad = tie(layer_out, input_grad, back_three, small, in_grad)
    input_grad = input_grad + settled([slot_two(back_one, back_two), slot_three(back_two, back_three)], (2, 3))
    small = small + swap(small, "tensor", 1)
    small = small + swap(small, "tensor", 2)
    mine, common = crossed(small[:8]), small[8:]
    in_grad = crossed(in_grad).astype(F32)
    inner_grad = jnp.stack([both_grad[:, :width].astype(F32), in_grad[:, :width]], axis=1)

    lines = line(norm_gain_grad).shape[0]
    norm_gain_grad = common[:lines].reshape(-1)[:model_width]
    shared_sums = common[lines:].reshape(-1)[: 5 * sf.shape[1]].reshape(5, -1)
    return (
        layer_out, input_grad, norm_gain_grad, inner_grad, in_grad[:, width + LANES :],
        in_grad[:, width : width + heads], mine[:4], mine[4], shared_sums[:4], shared_sums[4],
        mine[6, :heads], mine[6, heads : 2 * heads], mine[6, 2 * heads : 3 * heads], mine[5], both_grad[:, width:].astype(F32),
    )


def solution(mesh):
    count, planes = mesh.devices.shape
    assert planes == 4 and count % 4 == 0
    names = ("row", "side", "core", "tensor")
    inner = jax.sharding.Mesh(mesh.devices.reshape(count // 4, 2, 2, planes), names)
    dp = ("row", "side", "core")
    in_specs = (
        P(dp, None), P(dp, None), P(dp), P(dp, None), P(), P(dp, None, "tensor"), P(dp, None), P(dp, "tensor"),
        P(None, "tensor"), P("tensor"), P(), P(), P("tensor"), P("tensor"), P("tensor"), P("tensor"), P(dp, "tensor"),
    )
    out_specs = (
        P(dp, None), P(dp, None), P(), P(dp, None, "tensor"), P(dp, None), P(dp, "tensor"),
        P(None, "tensor"), P("tensor"), P(), P(), P("tensor"), P("tensor"), P("tensor"), P("tensor"), P(dp, "tensor"),
    )
    return jax.shard_map(on_device, mesh=inner, in_specs=in_specs, out_specs=out_specs, check_vma=False)
```
